32 devices in a mesh: tp: 4 (over y, x), seq: 8 (over z, core).
Axes of the slice: x: 2, y: 2, z: 4, core: 2. Of those that a mesh axis runs over, the one named last changes fastest.
Arguments:
- query_rows: bfloat16 [2048, 8192], P('seq', 'tp'), may hold values from -24 to 24
- key_rows: bfloat16 [2048, 1024], P('seq', 'tp'), may hold values from -9 to 9
- value_rows: bfloat16 [2048, 1024], P('seq', 'tp'), may hold values from -9 to 9
- mixer_input: bfloat16 [2048, 8192], P('seq', 'tp'), may hold values from -6 to 6
- write_rows: bfloat16 [2048, 128], P('seq'), may hold values from -48 to 48
- read_rows: bfloat16 [2048, 128], P('seq'), may hold values from -48 to 48
- log_step: float32 [128, 2048], P('tp', 'seq'), may hold values from -20 to -4
- log_decay: float32 [128, 2048], P('tp', 'seq'), may hold values from -2 to 0
Outputs:
- grad_input: float32 [2048, 8192], P('seq', 'tp')
- grad_write: float32 [2048, 128], P('seq')
- grad_read: float32 [2048, 128], P('seq')
- grad_log_step: float32 [128, 2048], P('tp', 'seq')
The draws below stay inside these ranges and needn't reach their ends.
All inputs are finite; a program needn't handle non-finite values.
Results may differ from the reference program's by a relative error of at most 0.0015.
Values may be sent and summed in bfloat16 or wider, within the bound.
No kernel may reach another device: no remote copies, remote signals or barrier semaphores. Data moves between devices by JAX's collectives and lax.ppermute only.
A program may use at most 128 MiB of HBM per device.

```python
import math
import jax
import jax.numpy as jnp
from jax import lax

BLOCK = 128
HQ = 64
KV = 8
HD = 128
H = 128
P_SIZE = 64
N = 128
SEQ_LEN = 2048


def teacher_keys(key):
    length = SEQ_LEN
    columns = KV * HD
    normal_base = jax.random.normal(jax.random.fold_in(key, 11), (length, columns), jnp.float32)
    keys_drawn = jnp.clip(1.4 * normal_base, -8.4, 8.4)
    return keys_drawn


def draw_key_rows(key, part):
    return teacher_keys(key).astype(jnp.bfloat16)


def draw_query_rows(key, part):
    normal_base = jax.random.normal(jax.random.fold_in(key, 14), (SEQ_LEN, HQ * HD), jnp.float32)
    drawn = jnp.clip(1.4 * normal_base, -8.4, 8.4)
    return drawn.astype(jnp.bfloat16)


def head_rates(key):
    picked = jax.random.randint(jax.random.fold_in(key, 21), (H,), 0, 16)
    slow_heads = picked < 11
    slow_rate = jnp.exp(jax.random.uniform(jax.random.fold_in(key, 26), (H,), jnp.float32, math.log(0.05), math.log(0.6))) / SEQ_LEN
    fast_rate = jnp.exp(jax.random.uniform(jax.random.fold_in(key, 27), (H,), jnp.float32, math.log(0.02), math.log(0.033)))
    return jnp.where(slow_heads, slow_rate, fast_rate)


def draw_log_decay(key, part):
    rates = head_rates(key)
    rough = jnp.exp(jax.random.uniform(jax.random.fold_in(key, 22), (H, SEQ_LEN), jnp.float32, math.log(0.5), math.log(2.0)))
    drawn = -rates[:, None] * rough
    spots = jax.random.randint(jax.random.fold_in(key, 23), (3,), 0, SEQ_LEN)
    amount = jnp.exp(jax.random.uniform(jax.random.fold_in(key, 24), (H, 3), jnp.float32, math.log(0.2), math.log(0.5)))
    return drawn.at[:, spots].add(-amount)


def draw_log_step(key, part):
    rates = head_rates(key)
    rough = jnp.exp(jax.random.uniform(jax.random.fold_in(key, 25), (H, SEQ_LEN), jnp.float32, math.log(0.5), math.log(2.0)))
    factor = 1.0 / (64.0 * math.sqrt(N))
    return jnp.log(factor * jnp.sqrt(rates)[:, None] * rough)


def level_of(key, shape, shards, smallest, top_value):
    factor_of, own = 1.0, jax.random.fold_in(key, 6)
    for dim, shards_of in shards:
        steps = jnp.exp(jax.random.uniform(jax.random.fold_in(own, dim), (shards_of,), jnp.float32, smallest / len(shards), top_value / len(shards)))
        factor_of = factor_of * jnp.repeat(steps, shape[dim] // shards_of).reshape([-1 if axis == dim else 1 for axis in range(len(shape))])
    return factor_of


def bell_draw(key, extent, scale, limit, split=(), kind=jnp.bfloat16):
    level = level_of(key, extent, split, -0.22, 0.18) if split else 1.0
    values = jax.random.normal(key, extent, jnp.float32) * scale * level
    return jnp.minimum(jnp.maximum(values, -limit), limit).astype(kind)


def setup_inputs(seed: int = 0) -> dict:
    splits = jax.random.split(jax.random.key(seed), 9)
    return {
        "query_rows": draw_query_rows(jax.random.fold_in(splits[8], 71), 0),
        "key_rows": draw_key_rows(jax.random.fold_in(splits[8], 71), 0),
        "value_rows": bell_draw(splits[2], (SEQ_LEN, KV * HD), 1.5, 9.0, ((0, 8), (1, 4))),
        "mixer_input": bell_draw(splits[3], (SEQ_LEN, H * P_SIZE), 1.0, 6.0, ((0, 8), (1, 4))),
        "write_rows": bell_draw(splits[4], (SEQ_LEN, N), 8.0, 48.0, ((0, 8),)),
        "read_rows": bell_draw(splits[5], (SEQ_LEN, N), 8.0, 48.0, ((0, 8),)),
        "log_step": draw_log_step(jax.random.fold_in(splits[8], 71), 0),
        "log_decay": draw_log_decay(jax.random.fold_in(splits[8], 71), 0),
    }


precise = lax.Precision.HIGHEST

def teacher(query_rows, key_rows, value_rows):
    length = query_rows.shape[0]
    group = HQ // KV
    query_heads = jnp.transpose(query_rows.reshape(length, HQ, HD), (1, 0, 2))
    key_heads = jnp.transpose(key_rows.reshape(length, KV, HD), (1, 0, 2))
    value_heads = jnp.transpose(value_rows.reshape(length, KV, HD), (1, 0, 2))
    positions = jnp.arange(length, dtype=jnp.int32)
    allowed = positions[None, :] <= positions[:, None]
    scaling = 1.0 / math.sqrt(HD)

    def one_head(head):
        query_now = query_heads[head]
        key_now = key_heads[head // group]
        value_now = value_heads[head // group]
        scores = jnp.dot(query_now, key_now.T, preferred_element_type=jnp.float32) * scaling
        scores = jnp.where(allowed, scores, -1e+30)
        top_score = lax.optimization_barrier(jnp.max(scores, axis=-1, keepdims=True))
        weights = jnp.where(allowed, jnp.exp(scores - top_score), 0.0)
        totals = lax.optimization_barrier(jnp.sum(weights, axis=-1, keepdims=True))
        mixed = jnp.dot(weights.astype(jnp.bfloat16), value_now, preferred_element_type=jnp.float32)
        return mixed / totals
    output = lax.map(one_head, jnp.arange(HQ, dtype=jnp.int32))
    return jnp.transpose(output, (1, 0, 2)).reshape(length, HQ * HD).astype(jnp.bfloat16)

def student(signal, writes, reads, log_step, log_decay):
    head_count = log_step.shape[0]
    length = signal.shape[0]
    blocks = length // BLOCK
    head_width = signal.shape[1] // head_count
    states = writes.shape[1]
    signal_blocks = signal.reshape(blocks, BLOCK, head_count, head_width)
    write_blocks = writes.reshape(blocks, BLOCK, states)
    read_blocks = reads.reshape(blocks, BLOCK, states)
    step_blocks = jnp.transpose(jnp.exp(log_step).reshape(head_count, blocks, BLOCK), (1, 0, 2))
    decay_blocks = jnp.transpose(log_decay.reshape(head_count, blocks, BLOCK), (1, 0, 2))
    causal = jnp.arange(BLOCK, dtype=jnp.int32)[:, None] >= jnp.arange(BLOCK, dtype=jnp.int32)[None, :]

    def one_block(state, element):
        signal_now, write_now, read_now, step_now, decay_now = element
        cum_decay = jnp.cumsum(decay_now, axis=-1)
        log_gap = cum_decay[:, :, None] - cum_decay[:, None, :]
        within = jnp.where(causal, jnp.exp(jnp.where(causal, log_gap, 0.0)), 0.0)
        inner_rows = jnp.dot(read_now, write_now.T, preferred_element_type=jnp.float32, precision=precise)
        scaled = signal_now * step_now.T[:, :, None]
        y_local = jnp.einsum('hij,jhp->ihp', within * inner_rows[None], scaled, precision=precise)
        y_carried = jnp.einsum('hpn,in->ihp', state, read_now, precision=precise) * jnp.exp(cum_decay).T[:, :, None]
        to_end = jnp.exp(cum_decay[:, -1:] - cum_decay).T
        added = jnp.einsum('jhp,jn->hpn', scaled * to_end[:, :, None], write_now, precision=precise)
        new_state = jnp.exp(cum_decay[:, -1])[:, None, None] * state + added
        return (new_state, y_local + y_carried)
    initial = jnp.zeros((head_count, head_width, states), jnp.float32)
    final_state, outputs = lax.scan(one_block, initial, (signal_blocks, write_blocks, read_blocks, step_blocks, decay_blocks))
    return outputs.reshape(length, head_count * head_width)

def reference(query_rows, key_rows, value_rows, mixer_input, write_rows, read_rows, log_step, log_decay):
    target = teacher(query_rows, key_rows, value_rows)
    signal = mixer_input.astype(jnp.float32)
    writes = write_rows.astype(jnp.float32)
    reads = read_rows.astype(jnp.float32)

    def forward(signal_in, writes_in, reads_in, step_in):
        return student(signal_in, writes_in, reads_in, step_in, log_decay)
    student_out, pullback = jax.vjp(forward, signal, writes, reads, log_step)
    residual = student_out - target.astype(jnp.float32)
    grad_input, grad_write, grad_read, grad_log_step = pullback(residual)
    return (grad_input, grad_write, grad_read, grad_log_step)
```

```python
import functools
import math

import jax
import jax.numpy as jnp
from jax import lax
from jax.experimental import pallas as pl
from jax.experimental.pallas import tpu as pltpu
from jax.sharding import PartitionSpec as P

HD = 128
F32, BF16, F16 = jnp.float32, jnp.bfloat16, jnp.float16


def nn(a, b):
    return lax.dot_general(a, b, (((1,), (0,)), ((), ())), preferred_element_type=F32)


def nt(a, b):
    return lax.dot_general(a, b, (((1,), (1,)), ((), ())), preferred_element_type=F32)


def tn(a, b):
    return lax.dot_general(a, b, (((0,), (0,)), ((), ())), preferred_element_type=F32)


def split2(a):
    hi = a.astype(BF16)
    return hi, (a - hi.astype(F32)).astype(BF16)


def split3(a):
    hi = a.astype(BF16)
    rest = a - hi.astype(F32)
    mid = rest.astype(BF16)
    return hi, mid, (rest - mid.astype(F32)).astype(BF16)


def iota(shape, dim):
    return lax.broadcasted_iota(jnp.int32, shape, dim)


def lower(t):
    return (iota((t, t), 0) >= iota((t, t), 1)).astype(BF16)


def spread_matrix(heads, width):
    return (iota((heads, width), 1) // (width // heads) == iota((heads, width), 0)).astype(BF16)


def spread(col, width):
    mat = spread_matrix(col.shape[1], width)
    a, b, c = split3(col)
    return nn(a, mat) + nn(b, mat) + nn(c, mat)


def spread_row(row, width):
    return spread(jnp.broadcast_to(row, (8, row.shape[1])), width)[0:1]


def cum_col(ld):
    tri = lower(ld.shape[1])
    a, b, c = split3(ld)
    return nt(tri, a) + nt(tri, b) + nt(tri, c)


def cum_row(ld):
    tri = lower(ld.shape[1])
    a, b, c = split3(ld)
    return nt(a, tri) + nt(b, tri) + nt(c, tri)


def turn(rows):
    t = rows.shape[1]
    eye = (iota((t, t), 0) == iota((t, t), 1)).astype(BF16)
    a, b, c = split3(rows)
    return nt(eye, a) + nt(eye, b) + nt(eye, c)


def state_kernel(x_ref, w_ref, ls_ref, ld_ref, st0_ref, st_ref):
    t = x_ref.shape[0] // 2
    width = x_ref.shape[1]
    parts, tots = [], []
    for b in (0, 1):
        rows = slice(b * t, (b + 1) * t)
        ccol = cum_col(ld_ref[:, rows])
        tot = ccol[t - 1 : t, :]
        wexp = spread(jnp.exp(tot - ccol + turn(ls_ref[:, rows])), width)
        hi, lo = split2(x_ref[rows, :].astype(F32) * wexp)
        parts.append(tn(w_ref[rows, :], hi) + tn(w_ref[rows, :], lo))
        tots.append(tot)
    st0_ref[...] = parts[0]
    st_ref[...] = spread_row(jnp.exp(tots[1]), width) * parts[0] + parts[1]


def local_kernel(x_ref, w_ref, r_ref, ls_ref, ld_ref, st0_ref, y_ref, cexp, clsrow, a_ref):
    t = x_ref.shape[0] // 2
    th = t // 2
    width = x_ref.shape[1]
    heads = ls_ref.shape[0]
    hw = width // heads
    per = 128 // hw
    for b in (0, 1):
        rows = slice(b * t, (b + 1) * t)
        ccol = cum_col(ld_ref[:, rows])
        cexp[...] = spread(ccol, width)
        clsrow[...] = cum_row(ld_ref[:, rows]) - ls_ref[:, rows]
        keep = iota((t, t), 0) >= iota((t, t), 1)
        a_ref[...] = jnp.where(keep, nt(r_ref[rows, :], w_ref[rows, :]), 0.0)
        if b == 1:
            fs = spread(jnp.exp(ccol), width)
            hi, lo = split2(st0_ref[...])
            y_ref[rows, :] = fs * (nn(r_ref[rows, :], hi) + nn(r_ref[rows, :], lo))

        def one(i, _, rows=rows, b=b):
            cols = pl.ds(pl.multiple_of(i * 128, 128), 128)
            xp = x_ref[rows, cols]
            cc = cexp[:, cols]
            lane = iota((t, 128), 1)
            out = None
            for a in range(per):
                ci = cc[:, a * hw : a * hw + 1]
                cj = clsrow[pl.ds(i * per + a, 1), :]
                top = jnp.exp(jnp.minimum(ci[:th] - cj[:, :th], 0.0)) * a_ref[:th, :th]
                bot = jnp.exp(jnp.minimum(ci[th:] - cj, 0.0)) * a_ref[th:, :]
                t1, t2 = split2(top)
                b1, b2 = split2(bot)
                yt = nn(t1, xp[:th]) + nn(t2, xp[:th])
                yb = nn(b1, xp) + nn(b2, xp)
                mine = jnp.concatenate([yt, yb], axis=0)
                out = mine if out is None else jnp.where(lane >= a * hw, mine, out)
            if b == 1:
                out = out + y_ref[rows, cols]
            y_ref[rows, cols] = out
            return 0

        lax.fori_loop(0, width // 128, one, 0)


def attention_kernel(c_ref, q_ref, kv_ref, *rest):
    others, (o_ref, far, sem) = rest[:-3], rest[-3:]
    t2 = q_ref.shape[0]
    t = t2 // 2
    kw = kv_ref.shape[1] // 2
    heads = q_ref.shape[1] // HD
    kvh = kw // HD
    group = heads // kvh
    chip = c_ref[0]
    scale = math.log2(math.e) / math.sqrt(HD)
    copies = [
        pltpu.make_async_copy(ref.at[pl.ds(0, t2)], far.at[k], sem.at[k])
        for k, ref in enumerate(others)
    ]
    for copy in copies:
        copy.start()
    for copy in copies:
        copy.wait()
    for g in range(kvh):
        kc = slice(g * HD, (g + 1) * HD)
        vc = slice(kw + g * HD, kw + (g + 1) * HD)

        def head(h, _, kc=kc, vc=vc, g=g):
            cols = pl.ds(pl.multiple_of((g * group + h) * HD, HD), HD)
            for b in (0, 1):
                rows = slice(b * t, (b + 1) * t)
                q = q_ref[rows, cols]
                span = (b + 1) * t
                s = nt(q, kv_ref[0:span, kc]) * scale
                keep = iota((t, span), 1) <= iota((t, span), 0) + b * t
                s = jnp.where(keep, s, -1e30)
                top = jnp.max(s, axis=1, keepdims=True)
                e = jnp.exp2(s - top)
                total = jnp.sum(e, axis=1, keepdims=True)
                acc = nn(e.astype(BF16), kv_ref[0:span, vc])

                def far_chunk(p, carry, q=q):
                    top, total, acc = carry
                    k = jnp.bitwise_xor(p, chip) - 1
                    s = nt(q, far[k, :, kc]) * scale
                    new = jnp.maximum(top, jnp.max(s, axis=1, keepdims=True))
                    e = jnp.exp2(s - new)
                    fade = jnp.exp2(top - new)
                    total = total * fade + jnp.sum(e, axis=1, keepdims=True)
                    acc = acc * fade + nn(e.astype(BF16), far[k, :, vc])
                    return new, total, acc

                top, total, acc = lax.fori_loop(0, chip, far_chunk, (top, total, acc))
                o_ref[rows, cols] = (acc / total).astype(BF16)
            return 0

        lax.fori_loop(0, group, head, 0)


def residual_kernel(y_ref, teach_ref, r_ref, ld_ref, sin_ref, res_ref, d1_ref, d_ref):
    t = y_ref.shape[0] // 2
    width = y_ref.shape[1]
    state = sin_ref[...]
    parts = []
    first = None
    for b in (0, 1):
        rows = slice(b * t, (b + 1) * t)
        ccol = cum_col(ld_ref[:, rows])
        fs = spread(jnp.exp(ccol), width)
        if b == 0:
            first = fs[t - 1 : t, :]
        else:
            state = state * first
        hi, lo = split2(state)
        r = r_ref[rows, :]
        res = y_ref[rows, :] + fs * (nn(r, hi) + nn(r, lo)) - teach_ref[rows, :].astype(F32)
        res_ref[rows, :] = res
        hi, lo = split2(res * fs)
        parts.append(tn(r, hi) + tn(r, lo))
    d1_ref[...] = parts[1]
    d_ref[...] = parts[0] + first * parts[1]


def back_kernel(
    res_ref, x_ref, w_ref, r_ref, ls_ref, ld_ref, sin_ref, st0_ref, d1_ref,
    back_ref, gw_ref, gr_ref, cexp, crow, a_ref, pair,
):
    t = x_ref.shape[0] // 2
    th = t // 2
    width = x_ref.shape[1]
    heads = ls_ref.shape[0]
    hw = width // heads
    per = 128 // hw
    first = None
    for b in (0, 1):
        rows = slice(b * t, (b + 1) * t)
        ccol = cum_col(ld_ref[:, rows])
        clscol = ccol - turn(ls_ref[:, rows])
        cexp[...] = spread(clscol, width)
        crow[...] = cum_row(ld_ref[:, rows])
        keep = iota((t, t), 1) >= iota((t, t), 0)
        w = w_ref[rows, :]
        r = r_ref[rows, :]
        a_ref[...] = jnp.where(keep, nt(w, r), 0.0)
        pair[...] = jnp.zeros_like(pair)
        fs = spread(jnp.exp(ccol), width)
        if b == 0:
            first = fs[t - 1 : t, :]
            wexp = spread(jnp.exp(ccol[t - 1 : t, :] - clscol), width)
            dh, dl = split2(d1_ref[...])
            back_ref[rows, :] = wexp * (nn(w, dh) + nn(w, dl))
            xh, xl = split2(x_ref[rows, :].astype(F32) * wexp)
            gw = nt(xh, dh) + nt(xh, dl) + nt(xl, dh)
            state = sin_ref[...]
        else:
            gw = None
            state = first * sin_ref[...] + st0_ref[...]
        sh, sl = split2(state)
        rh, rl = split2(res_ref[rows, :] * fs)
        gr = nt(rh, sh) + nt(rh, sl) + nt(rl, sh)

        def one(i, _, rows=rows, b=b):
            cols = pl.ds(pl.multiple_of(i * 128, 128), 128)
            xp = x_ref[rows, cols]
            rp = res_ref[rows, cols]
            rh, rl = split2(rp)
            both = jnp.concatenate([rh, rl], axis=1)
            cc = cexp[:, cols]
            lane = iota((t, 128), 1)
            out = None
            for a in range(per):
                cj = cc[:, a * hw : a * hw + 1]
                ci = crow[pl.ds(i * per + a, 1), :]
                mine = (lane // hw) == a
                xa = jnp.where(mine, xp, jnp.zeros_like(xp))
                xx = jnp.concatenate([xa, xa], axis=1)
                e1 = jnp.exp(jnp.minimum(ci - cj[:th], 0.0))
                e2 = jnp.exp(jnp.minimum(ci[:, th:] - cj[th:], 0.0))
                h1, l1 = split2(e1 * a_ref[:th, :])
                h2, l2 = split2(e2 * a_ref[th:, th:])
                p1 = nn(h1, both)
                p2 = nn(h2, both[th:])
                u1 = p1[:, :128] + p1[:, 128:] + nn(l1, rh)
                u2 = p2[:, :128] + p2[:, 128:] + nn(l2, rh[th:])
                u = jnp.concatenate([u1, u2], axis=0)
                out = u if out is None else jnp.where(lane >= a * hw, u, out)
                pair[:th, :] += e1 * nt(xx[:th], both)
                pair[th:, th:] += e2 * nt(xx[th:], both[th:])
            if b == 0:
                out = out + back_ref[rows, cols]
            back_ref[rows, cols] = out
            return 0

        lax.fori_loop(0, width // 128, one, 0)
        ph, plo = split2(jnp.where(keep, pair[...], 0.0))
        gr_ref[rows, :] = gr + tn(ph, w) + tn(plo, w)
        mixed = nn(ph, r) + nn(plo, r)
        gw_ref[rows, :] = mixed if gw is None else mixed + gw


def final_kernel(
    back_ref, x_ref, w_ref, ls_ref, ld_ref, extra_ref, g_ref, gw0_ref, gi_ref, gls_ref, gw_ref
):
    t = x_ref.shape[0]
    width = x_ref.shape[1]
    heads = ls_ref.shape[0]
    ccol = cum_col(ld_ref[...])
    wexp = spread(
        jnp.exp(ccol[t - 1 : t, :] + extra_ref[...] - ccol + turn(ls_ref[...])), width
    )
    gh, gl = split2(g_ref[...])
    w = w_ref[...]
    x = x_ref[...].astype(F32)
    out = back_ref[...] + wexp * (nn(w, gh) + nn(w, gl))
    gi_ref[...] = out
    mat = spread_matrix(heads, width)
    ph, plo = split2(x * out)
    gls_ref[...] = nt(mat, ph) + nt(mat, plo)
    xh, xl = split2(x * wexp)
    gw_ref[...] = gw0_ref[...] + nt(xh, gh) + nt(xh, gl) + nt(xl, gh)


VM = pl.BlockSpec(memory_space=pltpu.VMEM)


def call(kernel, outs, args, scratch=(), flops=0, name=None, in_specs=None):
    shapes = [jax.ShapeDtypeStruct(s, d) for s, d in outs]
    moved = sum(a.size * a.dtype.itemsize for a in args)
    return pl.pallas_call(
        kernel,
        out_shape=shapes,
        in_specs=in_specs or [VM] * len(args),
        out_specs=[VM] * len(shapes),
        scratch_shapes=list(scratch),
        name=name,
        cost_estimate=pl.CostEstimate(flops=flops, bytes_accessed=moved, transcendentals=0),
        compiler_params=pltpu.CompilerParams(vmem_limit_bytes=60 * 2**20),
    )(*args)


def encode(state):
    top = jnp.max(jnp.abs(state), axis=0, keepdims=True)
    power = jnp.ceil(jnp.log2(jnp.maximum(top, 1e-30)))
    body = (state * jnp.exp2(12.0 - power)).astype(F16)
    tail = jnp.broadcast_to(power, (16, state.shape[1])).astype(F16)
    return jnp.concatenate([body, tail], axis=0)


def decode(coded, rows, weight):
    power = coded[rows : rows + 1].astype(F32)
    return coded[:rows].astype(F32) * (jnp.exp2(power - 12.0) * weight)


def on_device(q, k, v, x, wr, rd, ls, ld):
    t = q.shape[0]
    count = lax.axis_size("seq")
    tp = lax.axis_size("tp")
    chips = count // 2
    index = lax.axis_index("seq")
    core, chip = index % 2, index // 2
    heads = ls.shape[0]
    hh = heads // 2
    n = wr.shape[1]
    hc = x.shape[1] // 2
    hw = x.shape[1] // heads
    qc = q.shape[1] // 2
    kvh = k.shape[1] // HD
    kw = k.shape[1] // 2 if kvh % 2 == 0 else k.shape[1]

    def swap(a, bits):
        return lax.ppermute(a, "seq", [(i, i ^ bits) for i in range(count)])

    def half(a, which, width, axis=1):
        return lax.dynamic_slice_in_dim(a, which * width, width, axis=axis)

    def joined(own, other, axis=0):
        a = jnp.where(core == 0, own, other)
        b = jnp.where(core == 0, other, own)
        return jnp.concatenate([a, b], axis=axis)

    def kv_half(which):
        if kvh % 2 == 0:
            return jnp.concatenate([half(k, which, kw), half(v, which, kw)], axis=1)
        return jnp.concatenate([k, v], axis=1)

    sent = swap(jnp.concatenate([kv_half(1 - core), wr, rd], axis=1), 1)
    rates = swap(jnp.concatenate([ls, ld], axis=0), 1)
    kv = joined(kv_half(core), sent[:, : 2 * kw])
    wc = joined(wr, sent[:, 2 * kw : 2 * kw + n])
    rc = joined(rd, sent[:, 2 * kw + n :])
    lsc = joined(half(ls, core, hh, 0), half(rates, core, hh, 0), 1)
    ldc = joined(half(ld, core, hh, 0), half(rates[heads:], core, hh, 0), 1)
    xc = joined(half(x, core, hc), swap(half(x, 1 - core, hc), 1))
    qg = joined(half(q, core, qc), swap(half(q, 1 - core, qc), 1))

    total = jnp.sum(ldc, axis=1)
    p1 = lax.reduce_precision(total, 8, 7)
    p2 = lax.reduce_precision(total - p1, 8, 7)
    p3 = lax.reduce_precision(total - p1 - p2, 8, 7)
    tail = jnp.zeros((16, 2 * kw), BF16).at[:3, :hh].set(jnp.stack([p1, p2, p3]).astype(BF16))
    payload = jnp.concatenate([kv, tail], axis=0)
    far = [swap(payload, 2 * d) for d in range(1, chips)]
    decays = [jnp.sum(f[2 * t : 2 * t + 3, :hh].astype(F32), axis=0) for f in far]

    def weight(d, later):
        p = chip ^ d
        low, high = (chip, p) if later else (p, chip)
        between = jnp.zeros((hh,), F32)
        for m in range(1, chips):
            at = chip ^ m
            between += jnp.where((at > low) & (at < high), decays[m - 1], 0.0)
        use = jnp.where((p > chip) if later else (p < chip), jnp.exp(between), 0.0)
        return jnp.repeat(use, hw)[None, :]

    def exchange(state, later):
        coded = encode(state)
        got = [swap(coded, 2 * d) for d in range(1, chips)]
        return sum(decode(g, n, weight(d, later)) for d, g in enumerate(got, 1))

    mm = 2 * 2 * t * hc * n
    st0, st = call(
        state_kernel, [((n, hc), F32)] * 2, (xc, wc, lsc, ldc), flops=4 * mm, name="chip_state"
    )
    incoming = exchange(st, False)
    (ybase,) = call(
        local_kernel, [((2 * t, hc), F32)], (xc, wc, rc, lsc, ldc, st0),
        scratch=[pltpu.VMEM((t, hc), F32), pltpu.VMEM((hh, t), F32), pltpu.VMEM((t, t), F32)],
        flops=8 * mm, name="local_scan",
    )
    chip_at = jnp.reshape(chip, (1,)).astype(jnp.int32)
    (teacher,) = call(
        attention_kernel, [((2 * t, qc), BF16)], (chip_at, qg, payload, *far),
        scratch=[pltpu.VMEM((chips - 1, 2 * t, 2 * kw), BF16), pltpu.SemaphoreType.DMA((chips - 1,))],
        flops=4 * t * t * qc * count, name="teacher",
        in_specs=[pl.BlockSpec(memory_space=pltpu.SMEM), VM, VM] + [pl.BlockSpec(memory_space=pl.ANY)] * (chips - 1),
    )
    res, d1, dt = call(
        residual_kernel, [((2 * t, hc), F32), ((n, hc), F32), ((n, hc), F32)],
        (ybase, teacher, rc, ldc, incoming), flops=8 * mm, name="residual",
    )
    arriving = exchange(dt, True)
    back, gw, gr = call(
        back_kernel, [((2 * t, hc), F32), ((2 * t, n), F32), ((2 * t, n), F32)],
        (res, xc, wc, rc, lsc, ldc, incoming, st0, d1),
        scratch=[pltpu.VMEM((t, hc), F32), pltpu.VMEM((hh, t), F32), pltpu.VMEM((t, t), F32), pltpu.VMEM((t, t), F32)],
        flops=16 * mm, name="local_back",
    )

    def home(a):
        return half(a, core, t, 0), swap(half(a, 1 - core, t, 0), 1)

    back_all = joined(*home(back), 1)
    own, other = home(jnp.concatenate([gw, gr], axis=1))
    grads = own + other
    gw0, gr0 = grads[:, :n], grads[:, n:]

    def tp_sum(a):
        bit = 1
        while bit < tp:
            a = a + lax.ppermute(a, "tp", [(i, i ^ bit) for i in range(tp)])
            bit *= 2
        return a

    grad_read = tp_sum(gr0)
    arrived = joined(arriving, swap(arriving, 1), 1)
    other_total = jnp.sum(rates[heads:], axis=1)[None, :]
    extra = jnp.where(core == 0, other_total, 0.0)
    gi, gls, gwp = call(
        final_kernel, [((t, 2 * hc), F32), ((heads, t), F32), ((t, n), F32)],
        (back_all, x, wr, ls, ld, extra, arrived, gw0), flops=8 * mm, name="finish",
    )
    return (gi, tp_sum(gwp), grad_read, gls)


def solution(mesh):
    in_specs = (
        P("seq", "tp"), P("seq", "tp"), P("seq", "tp"), P("seq", "tp"),
        P("seq", None), P("seq", None), P("tp", "seq"), P("tp", "seq"),
    )
    out_specs = (P("seq", "tp"), P("seq", None), P("seq", None), P("tp", "seq"))
    return jax.shard_map(
        on_device, mesh=mesh, in_specs=in_specs, out_specs=out_specs, check_vma=False
    )
```

```python
import functools
import math

import jax
import jax.numpy as jnp
from jax import lax
from jax.experimental import pallas as pl
from jax.experimental.pallas import tpu as pltpu
from jax.sharding import PartitionSpec as P

HD = 128
F32, BF16, F16 = jnp.float32, jnp.bfloat16, jnp.float16


def nn(a, b):
    return lax.dot_general(a, b, (((1,), (0,)), ((), ())), preferred_element_type=F32)


def nt(a, b):
    return lax.dot_general(a, b, (((1,), (1,)), ((), ())), preferred_element_type=F32)


def tn(a, b):
    return lax.dot_general(a, b, (((0,), (0,)), ((), ())), preferred_element_type=F32)


def split2(a):
    hi = a.astype(BF16)
    return hi, (a - hi.astype(F32)).astype(BF16)


def split3(a):
    hi = a.astype(BF16)
    rest = a - hi.astype(F32)
    mid = rest.astype(BF16)
    return hi, mid, (rest - mid.astype(F32)).astype(BF16)


def iota(shape, dim):
    return lax.broadcasted_iota(jnp.int32, shape, dim)


def lower(t):
    return (iota((t, t), 0) >= iota((t, t), 1)).astype(BF16)


def spread_matrix(heads, width):
    return (iota((heads, width), 1) // (width // heads) == iota((heads, width), 0)).astype(BF16)


def spread(col, width, exact=False):
    mat = spread_matrix(col.shape[1], width)
    a, b, c = split3(col)
    out = nn(a, mat) + nn(b, mat)
    return out + nn(c, mat) if exact else out


def spread_row(row, width):
    return spread(jnp.broadcast_to(row, (8, row.shape[1])), width)[0:1]


def cum_col(ld):
    tri = lower(ld.shape[1])
    a, b, c = split3(ld)
    return nt(tri, a) + nt(tri, b) + nt(tri, c)


def cum_row(ld):
    tri = lower(ld.shape[1])
    a, b, c = split3(ld)
    return nt(a, tri) + nt(b, tri) + nt(c, tri)


def turn(rows):
    t = rows.shape[1]
    eye = (iota((t, t), 0) == iota((t, t), 1)).astype(BF16)
    a, b, c = split3(rows)
    return nt(eye, a) + nt(eye, b) + nt(eye, c)


def state_kernel(x_ref, w_ref, ls_ref, ld_ref, st0_ref, st_ref):
    t = x_ref.shape[0] // 2
    width = x_ref.shape[1]
    parts, tots = [], []
    for b in (0, 1):
        rows = slice(b * t, (b + 1) * t)
        ccol = cum_col(ld_ref[:, rows])
        tot = ccol[t - 1 : t, :]
        wexp = spread(jnp.exp(tot - ccol + turn(ls_ref[:, rows])), width)
        hi, lo = split2(x_ref[rows, :].astype(F32) * wexp)
        parts.append(tn(w_ref[rows, :], hi) + tn(w_ref[rows, :], lo))
        tots.append(tot)
    st0_ref[...] = parts[0]
    st_ref[...] = spread_row(jnp.exp(tots[1]), width) * parts[0] + parts[1]


def local_kernel(x_ref, w_ref, r_ref, ls_ref, ld_ref, st0_ref, y_ref, cexp, clsrow, a_ref):
    t = x_ref.shape[0] // 2
    th = t // 2
    width = x_ref.shape[1]
    heads = ls_ref.shape[0]
    hw = width // heads
    per = 128 // hw
    for b in (0, 1):
        rows = slice(b * t, (b + 1) * t)
        ccol = cum_col(ld_ref[:, rows])
        cexp[...] = spread(ccol, width, True)
        clsrow[...] = cum_row(ld_ref[:, rows]) - ls_ref[:, rows]
        keep = iota((t, t), 0) >= iota((t, t), 1)
        a_ref[...] = jnp.where(keep, nt(r_ref[rows, :], w_ref[rows, :]), 0.0)
        if b == 1:
            fs = spread(jnp.exp(ccol), width)
            hi, lo = split2(st0_ref[...])
            y_ref[rows, :] = fs * (nn(r_ref[rows, :], hi) + nn(r_ref[rows, :], lo))

        def one(i, _, rows=rows, b=b):
            cols = pl.ds(pl.multiple_of(i * 128, 128), 128)
            xp = x_ref[rows, cols]
            cc = cexp[:, cols]
            lane = iota((t, 128), 1)
            out = None
            for a in range(per):
                ci = cc[:, a * hw : a * hw + 1]
                cj = clsrow[pl.ds(i * per + a, 1), :]
                top = jnp.exp(jnp.minimum(ci[:th] - cj[:, :th], 0.0)) * a_ref[:th, :th]
                bot = jnp.exp(jnp.minimum(ci[th:] - cj, 0.0)) * a_ref[th:, :]
                t1, t2 = split2(top)
                b1, b2 = split2(bot)
                yt = nn(t1, xp[:th]) + nn(t2, xp[:th])
                yb = nn(b1, xp) + nn(b2, xp)
                mine = jnp.concatenate([yt, yb], axis=0)
                out = mine if out is None else jnp.where(lane >= a * hw, mine, out)
            if b == 1:
                out = out + y_ref[rows, cols]
            y_ref[rows, cols] = out
            return 0

        lax.fori_loop(0, width // 128, one, 0)


def keys_twice(kv_ref, g, kw):
    k = kv_ref[:, g * HD : (g + 1) * HD]
    return jnp.concatenate([k, k], axis=1), kv_ref[:, kw + g * HD : kw + (g + 1) * HD].T


def own_kernel(q_ref, kv_ref, qs_ref, acc_ref, m_ref, l_ref, k2, vt, bias, s0a, s1a, s0b, s1b):
    t = q_ref.shape[0] // 2
    kw = kv_ref.shape[1] // 2
    kvh = kw // HD
    group = q_ref.shape[1] // HD // kvh
    scale = 1.0 / math.sqrt(HD)
    bias[...] = jnp.where(iota((t, t), 0) <= iota((t, t), 1), 0.0, -1e30)
    for g in range(kvh):
        k2[...], vt[...] = keys_twice(kv_ref, g, kw)

        def scores(h, s0, s1, g=g):
            at = g * group + h
            q = q_ref[:, pl.ds(pl.multiple_of(at * HD, HD), HD)].astype(F32) * scale
            both = jnp.concatenate(split2(q), axis=1)
            qs_ref[:, pl.ds(pl.multiple_of(at * 2 * HD, 2 * HD), 2 * HD)] = both
            s0[...] = nt(k2[:t, :], both[:t]) + bias[...]
            s1[:t, :] = nt(k2[:t, :], both[t:])
            s1[t:, :] = nt(k2[t:, :], both[t:]) + bias[...]

        def soft(h, s0, s1, g=g):
            at = g * group + h
            cols = pl.ds(pl.multiple_of(at * HD, HD), HD)
            for b, s_ref in ((0, s0), (1, s1)):
                rows = slice(b * t, (b + 1) * t)
                s = s_ref[...]
                top = jnp.max(s, axis=0, keepdims=True)
                e = jnp.exp(s - top)
                m_ref[pl.ds(at, 1), rows] = top
                l_ref[pl.ds(at, 1), rows] = jnp.sum(e, axis=0, keepdims=True)
                acc_ref[cols, rows] = nn(vt[:, : (b + 1) * t], e.astype(BF16))

        scores(0, s0a, s1a)

        def pair(i, _):
            scores(2 * i + 1, s0b, s1b)
            soft(2 * i, s0a, s1a)
            scores(jnp.minimum(2 * i + 2, group - 1), s0a, s1a)
            soft(2 * i + 1, s0b, s1b)
            return 0

        lax.fori_loop(0, group // 2, pair, 0)


def far_kernel(flag, qs_ref, kv_ref, acc_in, m_in, l_in, acc_ref, m_ref, l_ref, k2, vt, sa, sb):
    t = qs_ref.shape[0] // 2
    kw = kv_ref.shape[1] // 2
    kvh = kw // HD
    group = qs_ref.shape[1] // (2 * HD) // kvh

    @pl.when(flag[0] == 0)
    def _():
        acc_ref[...] = acc_in[...]
        m_ref[...] = m_in[...]
        l_ref[...] = l_in[...]

    @pl.when(flag[0] == 1)
    def _():
        for g in range(kvh):
            k2[...], vt[...] = keys_twice(kv_ref, g, kw)

            def scores(h, s_ref, g=g):
                at = g * group + h
                s_ref[...] = nt(k2[...], qs_ref[:, pl.ds(pl.multiple_of(at * 2 * HD, 2 * HD), 2 * HD)])

            def soft(h, s_ref, g=g):
                at = g * group + h
                cols = pl.ds(pl.multiple_of(at * HD, HD), HD)
                row = pl.ds(at, 1)
                for b in (0, 1):
                    rows = slice(b * t, (b + 1) * t)
                    s = s_ref[:, rows]
                    old = m_in[row, rows]
                    new = jnp.maximum(old, jnp.max(s, axis=0, keepdims=True))
                    e = jnp.exp(s - new)
                    fade = jnp.exp(old - new)
                    m_ref[row, rows] = new
                    l_ref[row, rows] = l_in[row, rows] * fade + jnp.sum(e, axis=0, keepdims=True)
                    acc_ref[cols, rows] = acc_in[cols, rows] * fade + nn(vt[...], e.astype(BF16))

            scores(0, sa)

            def pair(i, _):
                scores(2 * i + 1, sb)
                soft(2 * i, sa)
                scores(jnp.minimum(2 * i + 2, group - 1), sa)
                soft(2 * i + 1, sb)
                return 0

            lax.fori_loop(0, group // 2, pair, 0)


def residual_kernel(y_ref, acc_ref, l_ref, r_ref, ld_ref, sin_ref, res_ref, d1_ref, d_ref):
    t = y_ref.shape[0] // 2
    width = y_ref.shape[1]
    state = sin_ref[...]
    parts = []
    first = None
    for b in (0, 1):
        rows = slice(b * t, (b + 1) * t)
        ccol = cum_col(ld_ref[:, rows])
        fs = spread(jnp.exp(ccol), width)
        if b == 0:
            first = fs[t - 1 : t, :]
        else:
            state = state * first
        hi, lo = split2(state)
        r = r_ref[rows, :]
        heads = [
            (acc_ref[h * HD : (h + 1) * HD, rows] / l_ref[h : h + 1, rows]).astype(BF16).T
            for h in range(width // HD)
        ]
        teach = jnp.concatenate(heads, axis=1).astype(F32)
        res = y_ref[rows, :] + fs * (nn(r, hi) + nn(r, lo)) - teach
        res_ref[rows, :] = res
        hi, lo = split2(res * fs)
        parts.append(tn(r, hi) + tn(r, lo))
    d1_ref[...] = parts[1]
    d_ref[...] = parts[0] + first * parts[1]


def back_kernel(
    res_ref, x_ref, w_ref, r_ref, ls_ref, ld_ref, sin_ref, st0_ref, d1_ref,
    back_ref, gw_ref, gr_ref, cexp, crow, a_ref, pair,
):
    t = x_ref.shape[0] // 2
    th = t // 2
    width = x_ref.shape[1]
    heads = ls_ref.shape[0]
    hw = width // heads
    per = 128 // hw
    first = None
    for b in (0, 1):
        rows = slice(b * t, (b + 1) * t)
        ccol = cum_col(ld_ref[:, rows])
        clscol = ccol - turn(ls_ref[:, rows])
        cexp[...] = spread(clscol, width, True)
        crow[...] = cum_row(ld_ref[:, rows])
        keep = iota((t, t), 1) >= iota((t, t), 0)
        w = w_ref[rows, :]
        r = r_ref[rows, :]
        a_ref[...] = jnp.where(keep, nt(w, r), 0.0)
        pair[...] = jnp.zeros_like(pair)
        fs = spread(jnp.exp(ccol), width)
        if b == 0:
            first = fs[t - 1 : t, :]
            wexp = spread(jnp.exp(ccol[t - 1 : t, :] - clscol), width)
            dh, dl = split2(d1_ref[...])
            back_ref[rows, :] = wexp * (nn(w, dh) + nn(w, dl))
            xh, xl = split2(x_ref[rows, :].astype(F32) * wexp)
            gw = nt(xh, dh) + nt(xh, dl) + nt(xl, dh)
            state = sin_ref[...]
        else:
            gw = None
            state = first * sin_ref[...] + st0_ref[...]
        sh, sl = split2(state)
        rh, rl = split2(res_ref[rows, :] * fs)
        gr = nt(rh, sh) + nt(rh, sl) + nt(rl, sh)

        def one(i, _, rows=rows, b=b):
            cols = pl.ds(pl.multiple_of(i * 128, 128), 128)
            xp = x_ref[rows, cols]
            rp = res_ref[rows, cols]
            rh, rl = split2(rp)
            both = jnp.concatenate([rh, rl], axis=1)
            cc = cexp[:, cols]
            lane = iota((t, 128), 1)
            out = None
            for a in range(per):
                cj = cc[:, a * hw : a * hw + 1]
                ci = crow[pl.ds(i * per + a, 1), :]
                mine = (lane // hw) == a
                xa = jnp.where(mine, xp, jnp.zeros_like(xp))
                xx = jnp.concatenate([xa, xa], axis=1)
                e1 = jnp.exp(jnp.minimum(ci - cj[:th], 0.0))
                e2 = jnp.exp(jnp.minimum(ci[:, th:] - cj[th:], 0.0))
                h1, l1 = split2(e1 * a_ref[:th, :])
                h2, l2 = split2(e2 * a_ref[th:, th:])
                p1 = nn(h1, both)
                p2 = nn(h2, both[th:])
                u1 = p1[:, :128] + p1[:, 128:] + nn(l1, rh)
                u2 = p2[:, :128] + p2[:, 128:] + nn(l2, rh[th:])
                u = jnp.concatenate([u1, u2], axis=0)
                out = u if out is None else jnp.where(lane >= a * hw, u, out)
                pair[:th, :] += e1 * nt(xx[:th], both)
                pair[th:, th:] += e2 * nt(xx[th:], both[th:])
            if b == 0:
                out = out + back_ref[rows, cols]
            back_ref[rows, cols] = out
            return 0

        lax.fori_loop(0, width // 128, one, 0)
        ph, plo = split2(jnp.where(keep, pair[...], 0.0))
        gr_ref[rows, :] = gr + tn(ph, w) + tn(plo, w)
        mixed = nn(ph, r) + nn(plo, r)
        gw_ref[rows, :] = mixed if gw is None else mixed + gw


def ready_kernel(x_ref, ls_ref, ld_ref, extra_ref, wexp_ref, xh_ref, xl_ref):
    t = x_ref.shape[0]
    ccol = cum_col(ld_ref[...])
    wexp = spread(
        jnp.exp(ccol[t - 1 : t, :] + extra_ref[...] - ccol + turn(ls_ref[...])), x_ref.shape[1]
    )
    wexp_ref[...] = wexp
    xh_ref[...], xl_ref[...] = split2(x_ref[...].astype(F32) * wexp)


def write_kernel(xh_ref, xl_ref, g_ref, gw0_ref, gw_ref):
    gh, gl = split2(g_ref[...])
    xh = xh_ref[...]
    gw_ref[...] = gw0_ref[...] + nt(xh, gh) + nt(xh, gl) + nt(xl_ref[...], gh)


def final_kernel(back_ref, wexp_ref, x_ref, w_ref, g_ref, gi_ref, gls_ref):
    width = x_ref.shape[1]
    heads = gls_ref.shape[0]
    gh, gl = split2(g_ref[...])
    w = w_ref[...]
    out = back_ref[...] + wexp_ref[...] * (nn(w, gh) + nn(w, gl))
    gi_ref[...] = out
    ph, plo = split2(x_ref[...].astype(F32) * out)
    mat = spread_matrix(heads, width)
    gls_ref[...] = nt(mat, ph) + nt(mat, plo)


VM = pl.BlockSpec(memory_space=pltpu.VMEM)


def call(kernel, outs, args, scratch=(), flops=0, name=None, in_specs=None, alias=None):
    shapes = [jax.ShapeDtypeStruct(s, d) for s, d in outs]
    moved = sum(a.size * a.dtype.itemsize for a in args)
    return pl.pallas_call(
        kernel,
        out_shape=shapes,
        in_specs=in_specs or [VM] * len(args),
        out_specs=[VM] * len(shapes),
        scratch_shapes=list(scratch),
        name=name,
        input_output_aliases=alias or {},
        cost_estimate=pl.CostEstimate(flops=flops, bytes_accessed=moved, transcendentals=0),
        compiler_params=pltpu.CompilerParams(vmem_limit_bytes=60 * 2**20),
    )(*args)


def half_float(a):
    return lax.reduce_precision(a, 5, 10)


def encode(state, extra):
    top = jnp.max(jnp.abs(state), axis=0, keepdims=True)
    power = jnp.ceil(jnp.log2(jnp.maximum(top, 1e-30)))
    body = state * jnp.exp2(12.0 - power)
    rest = jnp.zeros((15 - extra.shape[0], state.shape[1]), F32)
    return jnp.concatenate([body, power, extra, rest], axis=0).astype(F16)


def decode(coded, rows, weight):
    power = coded[rows : rows + 1].astype(F32)
    return coded[:rows].astype(F32) * (jnp.exp2(power - 12.0) * weight)


def on_device(q, k, v, x, wr, rd, ls, ld):
    t = q.shape[0]
    count = lax.axis_size("seq")
    tp = lax.axis_size("tp")
    chips = count // 2
    index = lax.axis_index("seq")
    core, chip = index % 2, index // 2
    heads = ls.shape[0]
    hh = heads // 2
    n = wr.shape[1]
    hc = x.shape[1] // 2
    hw = x.shape[1] // heads
    qc = q.shape[1] // 2
    kvh = k.shape[1] // HD
    kw = k.shape[1] // 2 if kvh % 2 == 0 else k.shape[1]

    def swap(a, bits):
        return lax.ppermute(a, "seq", [(i, i ^ bits) for i in range(count)])

    def half(a, which, width, axis=1):
        return lax.dynamic_slice_in_dim(a, which * width, width, axis=axis)

    def joined(own, other, axis=0):
        a = jnp.where(core == 0, own, other)
        b = jnp.where(core == 0, other, own)
        return jnp.concatenate([a, b], axis=axis)

    def gather(a):
        got = {}
        for d in range(1, chips):
            low = d & -d
            got[d] = swap(a if d == low else got[d - low], 2 * low)
        return [got[d] for d in range(1, chips)]

    def kv_half(which):
        if kvh % 2 == 0:
            return jnp.concatenate([half(k, which, kw), half(v, which, kw)], axis=1)
        return jnp.concatenate([k, v], axis=1)

    kv = joined(kv_half(core), swap(kv_half(1 - core), 1))
    far = gather(kv)
    rates = swap(jnp.concatenate([ls, ld], axis=0), 1)
    lsc = joined(half(ls, core, hh, 0), half(rates, core, hh, 0), 1)
    ldc = joined(half(ld, core, hh, 0), half(rates[heads:], core, hh, 0), 1)
    mates = swap(jnp.concatenate([half(x, 1 - core, hc), wr, rd], axis=1), 1)
    xc = joined(half(x, core, hc), mates[:, :hc])
    wc = joined(wr, mates[:, hc : hc + n])
    rc = joined(rd, mates[:, hc + n :])
    qg = joined(half(q, core, qc), swap(half(q, 1 - core, qc), 1))

    mm = 2 * 2 * t * hc * n
    st0, st = call(
        state_kernel, [((n, hc), F32)] * 2, (xc, wc, lsc, ldc), flops=4 * mm, name="chip_state"
    )
    total = jnp.repeat(jnp.sum(ldc, axis=1), hw)[None, :]
    p1 = half_float(total)
    p2 = half_float(total - p1)
    mine = encode(st, jnp.concatenate([p1, p2, total - p1 - p2], axis=0))
    states = gather(mine)
    decays = [jnp.sum(f[n + 1 : n + 4].astype(F32), axis=0, keepdims=True) for f in states]

    def weight(d, later):
        p = chip ^ d
        low, high = (chip, p) if later else (p, chip)
        between = jnp.zeros((1, hc), F32)
        for m in range(1, chips):
            at = chip ^ m
            between += jnp.where((at > low) & (at < high), decays[m - 1], 0.0)
        return jnp.where((p > chip) if later else (p < chip), jnp.exp(between), 0.0)

    def combine(got, later):
        return sum(decode(g, n, weight(d, later)) for d, g in enumerate(got, 1))

    (ybase,) = call(
        local_kernel, [((2 * t, hc), F32)], (xc, wc, rc, lsc, ldc, st0),
        scratch=[pltpu.VMEM((t, hc), F32), pltpu.VMEM((hh, t), F32), pltpu.VMEM((t, t), F32)],
        flops=8 * mm, name="local_scan",
    )
    qh = qc // HD
    carry = [((qc, 2 * t), F32), ((qh, 2 * t), F32), ((qh, 2 * t), F32)]
    qs, *soft = call(
        own_kernel, [((2 * t, 2 * qc), BF16), *carry], (qg, kv),
        scratch=[pltpu.VMEM((2 * t, 2 * HD), BF16), pltpu.VMEM((HD, 2 * t), BF16), pltpu.VMEM((t, t), F32)]
        + [pltpu.VMEM((t, t), F32), pltpu.VMEM((2 * t, t), F32)] * 2,
        flops=4 * (2 * t) ** 2 * qc, name="teacher_own",
    )
    for d, keys in enumerate(far, 1):
        flag = jnp.reshape((chip ^ d) < chip, (1,)).astype(jnp.int32)
        soft = call(
            far_kernel, carry, (flag, qs, keys, *soft),
            scratch=[pltpu.VMEM((2 * t, 2 * HD), BF16), pltpu.VMEM((HD, 2 * t), BF16)] + [pltpu.VMEM((2 * t, 2 * t), F32)] * 2,
            flops=4 * (2 * t) ** 2 * qc, name="teacher_far", alias={3: 0, 4: 1, 5: 2},
            in_specs=[pl.BlockSpec(memory_space=pltpu.SMEM)] + [VM] * 5,
        )
    incoming = combine(states, False)
    res, d1, dt = call(
        residual_kernel, [((2 * t, hc), F32), ((n, hc), F32), ((n, hc), F32)],
        (ybase, soft[0], soft[2], rc, ldc, incoming), flops=8 * mm, name="residual",
    )
    coded = encode(dt, jnp.zeros((0, hc), F32))
    coming = [swap(coded, 2 * d) for d in range(1, chips)]
    back, gw, gr = call(
        back_kernel, [((2 * t, hc), F32), ((2 * t, n), F32), ((2 * t, n), F32)],
        (res, xc, wc, rc, lsc, ldc, incoming, st0, d1),
        scratch=[pltpu.VMEM((t, hc), F32), pltpu.VMEM((hh, t), F32), pltpu.VMEM((t, t), F32), pltpu.VMEM((t, t), F32)],
        flops=16 * mm, name="local_back",
    )
    other_total = jnp.sum(rates[heads:], axis=1)[None, :]
    extra = jnp.where(core == 0, other_total, 0.0)
    wexp, xh, xl = call(
        ready_kernel, [((t, 2 * hc), F32), ((t, 2 * hc), BF16), ((t, 2 * hc), BF16)],
        (x, ls, ld, extra), flops=2 * mm, name="ready",
    )

    def home(a):
        return half(a, core, t, 0), swap(half(a, 1 - core, t, 0), 1)

    def tp_sum(a):
        bit = 1
        while bit < tp:
            a = a + lax.ppermute(a, "tp", [(i, i ^ bit) for i in range(tp)])
            bit *= 2
        return a

    back_all = joined(*home(back), 1)
    own, other = home(jnp.concatenate([gw, gr], axis=1))
    grads = own + other
    gw0, gr0 = grads[:, :n], grads[:, n:]
    grad_read = tp_sum(gr0)
    arriving = combine(coming, True)
    arrived = joined(arriving, swap(arriving, 1), 1)
    (gwp,) = call(
        write_kernel, [((t, n), F32)], (xh, xl, arrived, gw0), flops=4 * mm, name="write_grad"
    )
    grad_write = tp_sum(gwp)
    gi, gls = call(
        final_kernel, [((t, 2 * hc), F32), ((heads, t), F32)], (back_all, wexp, x, wr, arrived),
        flops=8 * mm, name="finish",
    )
    return (gi, grad_write, grad_read, gls)


def solution(mesh):
    in_specs = (
        P("seq", "tp"), P("seq", "tp"), P("seq", "tp"), P("seq", "tp"),
        P("seq", None), P("seq", None), P("tp", "seq"), P("tp", "seq"),
    )
    out_specs = (P("seq", "tp"), P("seq", None), P("seq", None), P("tp", "seq"))
    return jax.shard_map(
        on_device, mesh=mesh, in_specs=in_specs, out_specs=out_specs, check_vma=False
    )
```

```python
import functools
import math

import jax
import jax.numpy as jnp
from jax import lax
from jax.experimental import pallas as pl
from jax.experimental.pallas import tpu as pltpu
from jax.sharding import PartitionSpec as P

HD = 128
F32, BF16, F16 = jnp.float32, jnp.bfloat16, jnp.float16


def nn(a, b):
    return lax.dot_general(a, b, (((1,), (0,)), ((), ())), preferred_element_type=F32)


def nt(a, b):
    return lax.dot_general(a, b, (((1,), (1,)), ((), ())), preferred_element_type=F32)


def tn(a, b):
    return lax.dot_general(a, b, (((0,), (0,)), ((), ())), preferred_element_type=F32)


def split2(a):
    hi = a.astype(BF16)
    return hi, (a - hi.astype(F32)).astype(BF16)


def split3(a):
    hi = a.astype(BF16)
    rest = a - hi.astype(F32)
    mid = rest.astype(BF16)
    return hi, mid, (rest - mid.astype(F32)).astype(BF16)


def iota(shape, dim):
    return lax.broadcasted_iota(jnp.int32, shape, dim)


def lower(t):
    return (iota((t, t), 0) >= iota((t, t), 1)).astype(BF16)


def spread_matrix(heads, width):
    return (iota((heads, width), 1) // (width // heads) == iota((heads, width), 0)).astype(BF16)


def spread(col, width, exact=False):
    mat = spread_matrix(col.shape[1], width)
    a, b, c = split3(col)
    out = nn(a, mat) + nn(b, mat)
    return out + nn(c, mat) if exact else out


def spread_row(row, width):
    return spread(jnp.broadcast_to(row, (8, row.shape[1])), width)[0:1]


def cum_col(ld):
    tri = lower(ld.shape[1])
    a, b, c = split3(ld)
    return nt(tri, a) + nt(tri, b) + nt(tri, c)


def cum_row(ld):
    tri = lower(ld.shape[1])
    a, b, c = split3(ld)
    return nt(a, tri) + nt(b, tri) + nt(c, tri)


def turn(rows):
    t = rows.shape[1]
    eye = (iota((t, t), 0) == iota((t, t), 1)).astype(BF16)
    a, b, c = split3(rows)
    return nt(eye, a) + nt(eye, b) + nt(eye, c)


def state_kernel(x_ref, w_ref, ls_ref, ld_ref, st0_ref, st_ref):
    t = x_ref.shape[0] // 2
    width = x_ref.shape[1]
    parts, tots = [], []
    for b in (0, 1):
        rows = slice(b * t, (b + 1) * t)
        ccol = cum_col(ld_ref[:, rows])
        tot = ccol[t - 1 : t, :]
        wexp = spread(jnp.exp(tot - ccol + turn(ls_ref[:, rows])), width)
        hi, lo = split2(x_ref[rows, :].astype(F32) * wexp)
        parts.append(tn(w_ref[rows, :], hi) + tn(w_ref[rows, :], lo))
        tots.append(tot)
    st0_ref[...] = parts[0]
    st_ref[...] = spread_row(jnp.exp(tots[1]), width) * parts[0] + parts[1]


def local_kernel(x_ref, w_ref, r_ref, ls_ref, ld_ref, st0_ref, y_ref, cexp, clsrow, a_ref):
    t = x_ref.shape[0] // 2
    th = t // 2
    width = x_ref.shape[1]
    heads = ls_ref.shape[0]
    hw = width // heads
    per = 128 // hw
    for b in (0, 1):
        rows = slice(b * t, (b + 1) * t)
        ccol = cum_col(ld_ref[:, rows])
        cexp[...] = spread(ccol, width, True)
        clsrow[...] = cum_row(ld_ref[:, rows]) - ls_ref[:, rows]
        keep = iota((t, t), 0) >= iota((t, t), 1)
        a_ref[...] = jnp.where(keep, nt(r_ref[rows, :], w_ref[rows, :]), 0.0)
        if b == 1:
            fs = spread(jnp.exp(ccol), width)
            hi, lo = split2(st0_ref[...])
            y_ref[rows, :] = fs * (nn(r_ref[rows, :], hi) + nn(r_ref[rows, :], lo))

        def one(i, _, rows=rows, b=b):
            cols = pl.ds(pl.multiple_of(i * 128, 128), 128)
            xp = x_ref[rows, cols]
            cc = cexp[:, cols]
            lane = iota((t, 128), 1)
            out = None
            for a in range(per):
                ci = cc[:, a * hw : a * hw + 1]
                cj = clsrow[pl.ds(i * per + a, 1), :]
                top = jnp.exp(jnp.minimum(ci[:th] - cj[:, :th], 0.0)) * a_ref[:th, :th]
                bot = jnp.exp(jnp.minimum(ci[th:] - cj, 0.0)) * a_ref[th:, :]
                t1, t2 = split2(top)
                b1, b2 = split2(bot)
                yt = nn(t1, xp[:th]) + nn(t2, xp[:th])
                yb = nn(b1, xp) + nn(b2, xp)
                mine = jnp.concatenate([yt, yb], axis=0)
                out = mine if out is None else jnp.where(lane >= a * hw, mine, out)
            if b == 1:
                out = out + y_ref[rows, cols]
            y_ref[rows, cols] = out
            return 0

        lax.fori_loop(0, width // 128, one, 0)


def keys_twice(kv_ref, g, kw):
    k = kv_ref[:, g * HD : (g + 1) * HD]
    return jnp.concatenate([k, k], axis=1), kv_ref[:, kw + g * HD : kw + (g + 1) * HD].T


def own_kernel(q_ref, kv_ref, qs_ref, acc_ref, m_ref, l_ref, k2, vt, bias, s0a, s1a, s0b, s1b):
    t = q_ref.shape[0] // 2
    kw = kv_ref.shape[1] // 2
    kvh = kw // HD
    group = q_ref.shape[1] // HD // kvh
    scale = 1.0 / math.sqrt(HD)
    bias[...] = jnp.where(iota((t, t), 0) <= iota((t, t), 1), 0.0, -1e30)
    for g in range(kvh):
        k2[...], vt[...] = keys_twice(kv_ref, g, kw)

        def scores(h, s0, s1, g=g):
            at = g * group + h
            q = q_ref[:, pl.ds(pl.multiple_of(at * HD, HD), HD)].astype(F32) * scale
            both = jnp.concatenate(split2(q), axis=1)
            qs_ref[:, pl.ds(pl.multiple_of(at * 2 * HD, 2 * HD), 2 * HD)] = both
            s0[...] = nt(k2[:t, :], both[:t]) + bias[...]
            s1[:t, :] = nt(k2[:t, :], both[t:])
            s1[t:, :] = nt(k2[t:, :], both[t:]) + bias[...]

        def soft(h, s0, s1, g=g):
            at = g * group + h
            cols = pl.ds(pl.multiple_of(at * HD, HD), HD)
            for b, s_ref in ((0, s0), (1, s1)):
                rows = slice(b * t, (b + 1) * t)
                s = s_ref[...]
                top = jnp.max(s, axis=0, keepdims=True)
                e = jnp.exp(s - top)
                m_ref[pl.ds(at, 1), rows] = top
                l_ref[pl.ds(at, 1), rows] = jnp.sum(e, axis=0, keepdims=True)
                acc_ref[cols, rows] = nn(vt[:, : (b + 1) * t], e.astype(BF16))

        scores(0, s0a, s1a)

        def pair(i, _):
            scores(2 * i + 1, s0b, s1b)
            soft(2 * i, s0a, s1a)
            scores(jnp.minimum(2 * i + 2, group - 1), s0a, s1a)
            soft(2 * i + 1, s0b, s1b)
            return 0

        lax.fori_loop(0, group // 2, pair, 0)


def far_kernel(flag, qs_ref, kv_ref, acc_in, m_in, l_in, acc_ref, m_ref, l_ref, k2, vt, sa, sb):
    t = qs_ref.shape[0] // 2
    kw = kv_ref.shape[1] // 2
    kvh = kw // HD
    group = qs_ref.shape[1] // (2 * HD) // kvh

    @pl.when(flag[0] == 0)
    def _():
        acc_ref[...] = acc_in[...]
        m_ref[...] = m_in[...]
        l_ref[...] = l_in[...]

    @pl.when(flag[0] == 1)
    def _():
        for g in range(kvh):
            k2[...], vt[...] = keys_twice(kv_ref, g, kw)

            def scores(h, s_ref, g=g):
                at = g * group + h
                s_ref[...] = nt(k2[...], qs_ref[:, pl.ds(pl.multiple_of(at * 2 * HD, 2 * HD), 2 * HD)])

            def soft(h, s_ref, g=g):
                at = g * group + h
                cols = pl.ds(pl.multiple_of(at * HD, HD), HD)
                row = pl.ds(at, 1)
                for b in (0, 1):
                    rows = slice(b * t, (b + 1) * t)
                    s = s_ref[:, rows]
                    old = m_in[row, rows]
                    new = jnp.maximum(old, jnp.max(s, axis=0, keepdims=True))
                    e = jnp.exp(s - new)
                    fade = jnp.exp(old - new)
                    m_ref[row, rows] = new
                    l_ref[row, rows] = l_in[row, rows] * fade + jnp.sum(e, axis=0, keepdims=True)
                    acc_ref[cols, rows] = acc_in[cols, rows] * fade + nn(vt[...], e.astype(BF16))

            scores(0, sa)

            def pair(i, _):
                scores(2 * i + 1, sb)
                soft(2 * i, sa)
                scores(jnp.minimum(2 * i + 2, group - 1), sa)
                soft(2 * i + 1, sb)
                return 0

            lax.fori_loop(0, group // 2, pair, 0)


def residual_kernel(y_ref, acc_ref, l_ref, r_ref, ld_ref, sin_ref, res_ref, d1_ref, d_ref):
    t = y_ref.shape[0] // 2
    width = y_ref.shape[1]
    state = sin_ref[...]
    parts = []
    first = None
    for b in (0, 1):
        rows = slice(b * t, (b + 1) * t)
        ccol = cum_col(ld_ref[:, rows])
        fs = spread(jnp.exp(ccol), width)
        if b == 0:
            first = fs[t - 1 : t, :]
        else:
            state = state * first
        hi, lo = split2(state)
        r = r_ref[rows, :]
        heads = [
            (acc_ref[h * HD : (h + 1) * HD, rows] / l_ref[h : h + 1, rows]).astype(BF16).T
            for h in range(width // HD)
        ]
        teach = jnp.concatenate(heads, axis=1).astype(F32)
        res = y_ref[rows, :] + fs * (nn(r, hi) + nn(r, lo)) - teach
        res_ref[rows, :] = res
        hi, lo = split2(res * fs)
        parts.append(tn(r, hi) + tn(r, lo))
    d1_ref[...] = parts[1]
    d_ref[...] = parts[0] + first * parts[1]


def back_kernel(
    res_ref, x_ref, w_ref, r_ref, ls_ref, ld_ref, sin_ref, st0_ref, d1_ref,
    back_ref, gw_ref, gr_ref, cexp, crow, a_ref, pair,
):
    t = x_ref.shape[0] // 2
    th = t // 2
    width = x_ref.shape[1]
    heads = ls_ref.shape[0]
    hw = width // heads
    per = 128 // hw
    first = None
    for b in (0, 1):
        rows = slice(b * t, (b + 1) * t)
        ccol = cum_col(ld_ref[:, rows])
        clscol = ccol - turn(ls_ref[:, rows])
        cexp[...] = spread(clscol, width, True)
        crow[...] = cum_row(ld_ref[:, rows])
        keep = iota((t, t), 1) >= iota((t, t), 0)
        w = w_ref[rows, :]
        r = r_ref[rows, :]
        a_ref[...] = jnp.where(keep, nt(w, r), 0.0)
        pair[...] = jnp.zeros_like(pair)
        fs = spread(jnp.exp(ccol), width)
        if b == 0:
            first = fs[t - 1 : t, :]
            wexp = spread(jnp.exp(ccol[t - 1 : t, :] - clscol), width)
            dh, dl = split2(d1_ref[...])
            back_ref[rows, :] = wexp * (nn(w, dh) + nn(w, dl))
            xh, xl = split2(x_ref[rows, :].astype(F32) * wexp)
            gw = nt(xh, dh) + nt(xh, dl) + nt(xl, dh)
            state = sin_ref[...]
        else:
            gw = None
            state = first * sin_ref[...] + st0_ref[...]
        sh, sl = split2(state)
        rh, rl = split2(res_ref[rows, :] * fs)
        gr = nt(rh, sh) + nt(rh, sl) + nt(rl, sh)

        def one(i, _, rows=rows, b=b):
            cols = pl.ds(pl.multiple_of(i * 128, 128), 128)
            xp = x_ref[rows, cols]
            rp = res_ref[rows, cols]
            rh, rl = split2(rp)
            both = jnp.concatenate([rh, rl], axis=1)
            cc = cexp[:, cols]
            lane = iota((t, 128), 1)
            out = None
            for a in range(per):
                cj = cc[:, a * hw : a * hw + 1]
                ci = crow[pl.ds(i * per + a, 1), :]
                mine = (lane // hw) == a
                xa = jnp.where(mine, xp, jnp.zeros_like(xp))
                xx = jnp.concatenate([xa, xa], axis=1)
                e1 = jnp.exp(jnp.minimum(ci - cj[:th], 0.0))
                e2 = jnp.exp(jnp.minimum(ci[:, th:] - cj[th:], 0.0))
                h1, l1 = split2(e1 * a_ref[:th, :])
                h2, l2 = split2(e2 * a_ref[th:, th:])
                p1 = nn(h1, both)
                p2 = nn(h2, both[th:])
                u1 = p1[:, :128] + p1[:, 128:] + nn(l1, rh)
                u2 = p2[:, :128] + p2[:, 128:] + nn(l2, rh[th:])
                u = jnp.concatenate([u1, u2], axis=0)
                out = u if out is None else jnp.where(lane >= a * hw, u, out)
                pair[:th, :] += e1 * nt(xx[:th], both)
                pair[th:, th:] += e2 * nt(xx[th:], both[th:])
            if b == 0:
                out = out + back_ref[rows, cols]
            back_ref[rows, cols] = out
            return 0

        lax.fori_loop(0, width // 128, one, 0)
        ph, plo = split2(jnp.where(keep, pair[...], 0.0))
        gr_ref[rows, :] = gr + tn(ph, w) + tn(plo, w)
        mixed = nn(ph, r) + nn(plo, r)
        gw_ref[rows, :] = mixed if gw is None else mixed + gw


def ready_kernel(x_ref, ls_ref, ld_ref, extra_ref, wexp_ref, xh_ref, xl_ref):
    t = x_ref.shape[0]
    ccol = cum_col(ld_ref[...])
    wexp = spread(
        jnp.exp(ccol[t - 1 : t, :] + extra_ref[...] - ccol + turn(ls_ref[...])), x_ref.shape[1]
    )
    wexp_ref[...] = wexp
    xh_ref[...], xl_ref[...] = split2(x_ref[...].astype(F32) * wexp)


def write_kernel(xh_ref, xl_ref, g_ref, gw0_ref, gw_ref):
    gh, gl = split2(g_ref[...])
    xh = xh_ref[...]
    gw_ref[...] = gw0_ref[...] + nt(xh, gh) + nt(xh, gl) + nt(xl_ref[...], gh)


def final_kernel(back_ref, wexp_ref, x_ref, w_ref, g_ref, gi_ref, gls_ref):
    width = x_ref.shape[1]
    heads = gls_ref.shape[0]
    gh, gl = split2(g_ref[...])
    w = w_ref[...]
    out = back_ref[...] + wexp_ref[...] * (nn(w, gh) + nn(w, gl))
    gi_ref[...] = out
    ph, plo = split2(x_ref[...].astype(F32) * out)
    mat = spread_matrix(heads, width)
    gls_ref[...] = nt(mat, ph) + nt(mat, plo)


VM = pl.BlockSpec(memory_space=pltpu.VMEM)


def call(kernel, outs, args, scratch=(), flops=0, name=None, in_specs=None, alias=None):
    shapes = [jax.ShapeDtypeStruct(s, d) for s, d in outs]
    moved = sum(a.size * a.dtype.itemsize for a in args)
    return pl.pallas_call(
        kernel,
        out_shape=shapes,
        in_specs=in_specs or [VM] * len(args),
        out_specs=[VM] * len(shapes),
        scratch_shapes=list(scratch),
        name=name,
        input_output_aliases=alias or {},
        cost_estimate=pl.CostEstimate(flops=flops, bytes_accessed=moved, transcendentals=0),
        compiler_params=pltpu.CompilerParams(vmem_limit_bytes=16 * 2**20),
    )(*args)


def half_float(a):
    return lax.reduce_precision(a, 5, 10)


def encode(state, extra):
    top = jnp.max(jnp.abs(state), axis=0, keepdims=True)
    power = jnp.ceil(jnp.log2(jnp.maximum(top, 1e-30)))
    body = state * jnp.exp2(12.0 - power)
    rest = jnp.zeros((15 - extra.shape[0], state.shape[1]), F32)
    return jnp.concatenate([body, power, extra, rest], axis=0).astype(F16)


def decode(coded, rows, weight):
    power = coded[rows : rows + 1].astype(F32)
    return coded[:rows].astype(F32) * (jnp.exp2(power - 12.0) * weight)


def on_device(q, k, v, x, wr, rd, ls, ld):
    t = q.shape[0]
    count = lax.axis_size("seq")
    tp = lax.axis_size("tp")
    chips = count // 2
    index = lax.axis_index("seq")
    core, chip = index % 2, index // 2
    heads = ls.shape[0]
    hh = heads // 2
    n = wr.shape[1]
    hc = x.shape[1] // 2
    hw = x.shape[1] // heads
    qc = q.shape[1] // 2
    kvh = k.shape[1] // HD
    kw = k.shape[1] // 2 if kvh % 2 == 0 else k.shape[1]

    def swap(a, bits):
        return lax.ppermute(a, "seq", [(i, i ^ bits) for i in range(count)])

    def half(a, which, width, axis=1):
        return lax.dynamic_slice_in_dim(a, which * width, width, axis=axis)

    def joined(own, other, axis=0):
        a = jnp.where(core == 0, own, other)
        b = jnp.where(core == 0, other, own)
        return jnp.concatenate([a, b], axis=axis)

    def near(a):
        return {1 << b: swap(a, 2 << b) for b in range(chips.bit_length() - 1)}

    def relay(got, token):
        got = dict(got)
        for d in range(1, chips):
            if d not in got:
                low = d & -d
                held, _ = lax.optimization_barrier((got[d - low], token))
                got[d] = swap(held, 2 * low)
        return [got[d] for d in range(1, chips)]

    def kv_half(which):
        if kvh % 2 == 0:
            return jnp.concatenate([half(k, which, kw), half(v, which, kw)], axis=1)
        return jnp.concatenate([k, v], axis=1)

    kv = joined(kv_half(core), swap(kv_half(1 - core), 1))
    keys_near = near(kv)
    rates = swap(jnp.concatenate([ls, ld], axis=0), 1)
    lsc = joined(half(ls, core, hh, 0), half(rates, core, hh, 0), 1)
    ldc = joined(half(ld, core, hh, 0), half(rates[heads:], core, hh, 0), 1)
    mates = swap(jnp.concatenate([half(x, 1 - core, hc), wr, rd], axis=1), 1)
    xc = joined(half(x, core, hc), mates[:, :hc])
    wc = joined(wr, mates[:, hc : hc + n])
    rc = joined(rd, mates[:, hc + n :])
    qg = joined(half(q, core, qc), swap(half(q, 1 - core, qc), 1))

    mm = 2 * 2 * t * hc * n
    st0, st = call(
        state_kernel, [((n, hc), F32)] * 2, (xc, wc, lsc, ldc), flops=4 * mm, name="chip_state"
    )
    total = jnp.repeat(jnp.sum(ldc, axis=1), hw)[None, :]
    p1 = half_float(total)
    p2 = half_float(total - p1)
    mine = encode(st, jnp.concatenate([p1, p2, total - p1 - p2], axis=0))
    states_near = near(mine)
    qh = qc // HD
    carry = [((qc, 2 * t), F32), ((qh, 2 * t), F32), ((qh, 2 * t), F32)]
    qs, *soft = call(
        own_kernel, [((2 * t, 2 * qc), BF16), *carry], (qg, kv),
        scratch=[pltpu.VMEM((2 * t, 2 * HD), BF16), pltpu.VMEM((HD, 2 * t), BF16), pltpu.VMEM((t, t), F32)]
        + [pltpu.VMEM((t, t), F32), pltpu.VMEM((2 * t, t), F32)] * 2,
        flops=4 * (2 * t) ** 2 * qc, name="teacher_own",
    )
    (ybase,) = call(
        local_kernel, [((2 * t, hc), F32)], (xc, wc, rc, lsc, ldc, st0),
        scratch=[pltpu.VMEM((t, hc), F32), pltpu.VMEM((hh, t), F32), pltpu.VMEM((t, t), F32)],
        flops=8 * mm, name="local_scan",
    )
    far = relay(keys_near, soft[1])
    states = relay(states_near, soft[1])
    decays = [jnp.sum(f[n + 1 : n + 4].astype(F32), axis=0, keepdims=True) for f in states]

    def weight(d, later):
        p = chip ^ d
        low, high = (chip, p) if later else (p, chip)
        between = jnp.zeros((1, hc), F32)
        for m in range(1, chips):
            at = chip ^ m
            between += jnp.where((at > low) & (at < high), decays[m - 1], 0.0)
        return jnp.where((p > chip) if later else (p < chip), jnp.exp(between), 0.0)

    def combine(got, later):
        return sum(decode(g, n, weight(d, later)) for d, g in enumerate(got, 1))

    for d, keys in enumerate(far, 1):
        flag = jnp.reshape((chip ^ d) < chip, (1,)).astype(jnp.int32)
        soft = call(
            far_kernel, carry, (flag, qs, keys, *soft),
            scratch=[pltpu.VMEM((2 * t, 2 * HD), BF16), pltpu.VMEM((HD, 2 * t), BF16)] + [pltpu.VMEM((2 * t, 2 * t), F32)] * 2,
            flops=4 * (2 * t) ** 2 * qc, name="teacher_far", alias={3: 0, 4: 1, 5: 2},
            in_specs=[pl.BlockSpec(memory_space=pltpu.SMEM)] + [VM] * 5,
        )
    incoming = combine(states, False)
    res, d1, dt = call(
        residual_kernel, [((2 * t, hc), F32), ((n, hc), F32), ((n, hc), F32)],
        (ybase, soft[0], soft[2], rc, ldc, incoming), flops=8 * mm, name="residual",
    )
    coded = encode(dt, jnp.zeros((0, hc), F32))
    coming = [swap(coded, 2 * d) for d in range(1, chips)]
    back, gw, gr = call(
        back_kernel, [((2 * t, hc), F32), ((2 * t, n), F32), ((2 * t, n), F32)],
        (res, xc, wc, rc, lsc, ldc, incoming, st0, d1),
        scratch=[pltpu.VMEM((t, hc), F32), pltpu.VMEM((hh, t), F32), pltpu.VMEM((t, t), F32), pltpu.VMEM((t, t), F32)],
        flops=16 * mm, name="local_back",
    )
    other_total = jnp.sum(rates[heads:], axis=1)[None, :]
    extra = jnp.where(core == 0, other_total, 0.0)
    wexp, xh, xl = call(
        ready_kernel, [((t, 2 * hc), F32), ((t, 2 * hc), BF16), ((t, 2 * hc), BF16)],
        (x, ls, ld, extra), flops=2 * mm, name="ready",
    )

    def home(a):
        return half(a, core, t, 0), swap(half(a, 1 - core, t, 0), 1)

    def tp_sum(a):
        bit = 1
        while bit < tp:
            a = a + lax.ppermute(a, "tp", [(i, i ^ bit) for i in range(tp)])
            bit *= 2
        return a

    back_all = joined(*home(back), 1)
    own, other = home(jnp.concatenate([gw, gr], axis=1))
    grads = own + other
    gw0, gr0 = grads[:, :n], grads[:, n:]
    grad_read = tp_sum(gr0)
    arriving = combine(coming, True)
    arrived = joined(arriving, swap(arriving, 1), 1)
    (gwp,) = call(
        write_kernel, [((t, n), F32)], (xh, xl, arrived, gw0), flops=4 * mm, name="write_grad"
    )
    grad_write = tp_sum(gwp)
    gi, gls = call(
        final_kernel, [((t, 2 * hc), F32), ((heads, t), F32)], (back_all, wexp, x, wr, arrived),
        flops=8 * mm, name="finish",
    )
    return (gi, grad_write, grad_read, gls)


def solution(mesh):
    in_specs = (
        P("seq", "tp"), P("seq", "tp"), P("seq", "tp"), P("seq", "tp"),
        P("seq", None), P("seq", None), P("tp", "seq"), P("tp", "seq"),
    )
    out_specs = (P("seq", "tp"), P("seq", None), P("seq", None), P("tp", "seq"))
    return jax.shard_map(
        on_device, mesh=mesh, in_specs=in_specs, out_specs=out_specs, check_vma=False
    )
```

```python
import math

import jax
import jax.numpy as jnp
from jax import lax
from jax.experimental import pallas as pl
from jax.experimental.pallas import tpu as pltpu
from jax.sharding import PartitionSpec as P


HD = 128
F32, BF16, F16 = jnp.float32, jnp.bfloat16, jnp.float16


def nn(a, b):
    return lax.dot_general(a, b, (((1,), (0,)), ((), ())), preferred_element_type=F32)


def nt(a, b):
    return lax.dot_general(a, b, (((1,), (1,)), ((), ())), preferred_element_type=F32)


def tn(a, b):
    return lax.dot_general(a, b, (((0,), (0,)), ((), ())), preferred_element_type=F32)


def split2(a):
    hi = a.astype(BF16)
    return hi, (a - hi.astype(F32)).astype(BF16)


def split3(a):
    hi = a.astype(BF16)
    rest = a - hi.astype(F32)
    mid = rest.astype(BF16)
    return hi, mid, (rest - mid.astype(F32)).astype(BF16)


def iota(shape, dim):
    return lax.broadcasted_iota(jnp.int32, shape, dim)


def lower(t):
    return (iota((t, t), 0) >= iota((t, t), 1)).astype(BF16)


def spread_matrix(heads, width, times=1):
    row = iota((times * heads, width), 0) % heads
    return (iota((times * heads, width), 1) // (width // heads) == row).astype(BF16)


def spread(col, width):
    pieces = [p.astype(F32) for p in split3(col)]
    stacked = jnp.concatenate(pieces, axis=1).astype(BF16)
    return nn(stacked, spread_matrix(col.shape[1], width, 3))


def stack2(a):
    return jnp.concatenate(split2(a), axis=0)


def twice(a):
    return jnp.concatenate([a, a], axis=1)


def nt3(a, b):
    ah, al = split2(a)
    bh, bl = split2(b)
    both = nt(ah, jnp.concatenate([bh, bl], axis=0))
    half = both.shape[1] // 2
    return both[:, :half] + both[:, half:] + nt(al, bh)


def code_rows(state, extra):
    top = jnp.max(jnp.abs(state), axis=0, keepdims=True)
    power = jnp.ceil(jnp.log2(jnp.maximum(top, 1e-30)))
    rest = jnp.zeros((15 - len(extra), state.shape[1]), F32)
    return state * jnp.exp2(12.0 - power), jnp.concatenate([power, *extra, rest], axis=0)


def spread_row(row, width):
    return spread(jnp.broadcast_to(row, (8, row.shape[1])), width)[0:1]


def cum_col(ld):
    tri = lower(ld.shape[1])
    a, b, c = split3(ld)
    return nt(tri, a) + nt(tri, b) + nt(tri, c)


def cum_row(ld):
    tri = lower(ld.shape[1])
    a, b, c = split3(ld)
    return nt(a, tri) + nt(b, tri) + nt(c, tri)


def turn(rows):
    t = rows.shape[1]
    eye = (iota((t, t), 0) == iota((t, t), 1)).astype(BF16)
    a, b, c = split3(rows)
    return nt(eye, a) + nt(eye, b) + nt(eye, c)


def state_kernel(x_ref, w_ref, ls_ref, ld_ref, st0_ref, coded_ref, wexp_ref):
    t = x_ref.shape[0] // 2
    width = x_ref.shape[1]
    n = w_ref.shape[1]
    parts, tots = [], []
    for b in (0, 1):
        rows = slice(b * t, (b + 1) * t)
        ccol = cum_col(ld_ref[:, rows])
        tot = ccol[t - 1 : t, :]
        wexp = spread(jnp.exp(tot - ccol + turn(ls_ref[:, rows])), width)
        wexp_ref[rows, :] = wexp
        hi, lo = split2(x_ref[rows, :].astype(F32) * wexp)
        parts.append(tn(w_ref[rows, :], hi) + tn(w_ref[rows, :], lo))
        tots.append(tot)
    st0_ref[...] = parts[0]
    state = spread_row(jnp.exp(tots[1]), width) * parts[0] + parts[1]
    pieces = [p.astype(F32) for p in split3(spread_row(tots[0] + tots[1], width))]
    coded_ref[:n, :], coded_ref[n:, :] = code_rows(state, pieces)


def local_kernel(
    x_ref, w_ref, r_ref, ls_ref, ld_ref, st0_ref,
    y_ref, fs_ref, clsx_ref, crow_ref, cexp, clsrow, a_ref,
):
    t = x_ref.shape[0] // 2
    th = t // 2
    width = x_ref.shape[1]
    heads = ls_ref.shape[0]
    hw = width // heads
    per = 128 // hw
    for b in (0, 1):
        rows = slice(b * t, (b + 1) * t)
        ccol = cum_col(ld_ref[:, rows])
        cexp[...] = spread(ccol, width)
        fs = spread(jnp.exp(ccol), width)
        fs_ref[rows, :] = fs
        clsx_ref[rows, :] = spread(ccol - turn(ls_ref[:, rows]), width)
        crow = cum_row(ld_ref[:, rows])
        crow_ref[:, rows] = crow
        clsrow[...] = crow - ls_ref[:, rows]
        keep = iota((t, t), 0) >= iota((t, t), 1)
        a_ref[...] = jnp.where(keep, nt(r_ref[rows, :], w_ref[rows, :]), 0.0)
        if b == 1:
            y_ref[rows, :] = fs * nn(twice(r_ref[rows, :]), stack2(st0_ref[...]))

        def one(i, rows=rows, b=b):
            cols = pl.ds(pl.multiple_of(i * 128, 128), 128)
            xp = x_ref[rows, cols]
            xtop = jnp.concatenate([xp[:th], xp[:th]], axis=0)
            cc = cexp[:, cols]
            lane = iota((t, 128), 1)
            out = None
            for a in range(per):
                ci = cc[:, a * hw : a * hw + 1]
                cj = clsrow[pl.ds(i * per + a, 1), :]
                top = jnp.exp(jnp.minimum(ci[:th] - cj[:, :th], 0.0)) * a_ref[:th, :th]
                bot = jnp.exp(jnp.minimum(ci[th:] - cj, 0.0)) * a_ref[th:, :]
                yt = nn(jnp.concatenate(split2(top), axis=1), xtop)
                b1, b2 = split2(bot)
                yb = nn(b1, xp) + nn(b2, xp)
                mine = jnp.concatenate([yt, yb], axis=0)
                out = mine if out is None else jnp.where(lane >= a * hw, mine, out)
            if b == 1:
                out = out + y_ref[rows, cols]
            return cols, out

        def two(i, _, rows=rows, one=one):
            done = [one(2 * i), one(2 * i + 1)]
            for cols, out in done:
                y_ref[rows, cols] = out
            return 0

        lax.fori_loop(0, width // 256, two, 0)


def keys_twice(kv_ref, g, kw):
    k = kv_ref[:, g * HD : (g + 1) * HD]
    return jnp.concatenate([k, k], axis=1), kv_ref[:, kw + g * HD : kw + (g + 1) * HD].T


def own_kernel(q_ref, kv_ref, qs_ref, acc_ref, m_ref, l_ref, k2, vt, bias, s0a, s1a, s0b, s1b):
    t = q_ref.shape[0] // 2
    kw = kv_ref.shape[1] // 2
    kvh = kw // HD
    group = q_ref.shape[1] // HD // kvh
    scale = 1.0 / math.sqrt(HD)
    bias[...] = jnp.where(iota((t, t), 0) <= iota((t, t), 1), 0.0, -1e30)
    for g in range(kvh):
        k2[...], vt[...] = keys_twice(kv_ref, g, kw)

        def scores(h, s0, s1, g=g):
            at = g * group + h
            q = q_ref[:, pl.ds(pl.multiple_of(at * HD, HD), HD)].astype(F32) * scale
            both = jnp.concatenate(split2(q), axis=1)
            qs_ref[:, pl.ds(pl.multiple_of(at * 2 * HD, 2 * HD), 2 * HD)] = both
            s0[...] = nt(k2[:t, :], both[:t]) + bias[...]
            s1[:t, :] = nt(k2[:t, :], both[t:])
            s1[t:, :] = nt(k2[t:, :], both[t:]) + bias[...]

        def soft(h, s0, s1, g=g):
            at = g * group + h
            cols = pl.ds(pl.multiple_of(at * HD, HD), HD)
            for b, s_ref in ((0, s0), (1, s1)):
                rows = slice(b * t, (b + 1) * t)
                s = s_ref[...]
                top = jnp.max(s, axis=0, keepdims=True)
                e = jnp.exp(s - top)
                m_ref[pl.ds(at, 1), rows] = top
                l_ref[pl.ds(at, 1), rows] = jnp.sum(e, axis=0, keepdims=True)
                acc_ref[cols, rows] = nn(vt[:, : (b + 1) * t], e.astype(BF16))

        scores(0, s0a, s1a)

        def pair(i, _):
            scores(2 * i + 1, s0b, s1b)
            soft(2 * i, s0a, s1a)
            scores(jnp.minimum(2 * i + 2, group - 1), s0a, s1a)
            soft(2 * i + 1, s0b, s1b)
            return 0

        lax.fori_loop(0, group // 2, pair, 0)


def far_kernel(flag, qs_ref, kv_ref, acc_in, m_in, l_in, acc_ref, m_ref, l_ref, k2, vt, sa, sb):
    t = qs_ref.shape[0] // 2
    kw = kv_ref.shape[1] // 2
    kvh = kw // HD
    group = qs_ref.shape[1] // (2 * HD) // kvh

    @pl.when(flag[0] == 0)
    def _():
        acc_ref[...] = acc_in[...]
        m_ref[...] = m_in[...]
        l_ref[...] = l_in[...]

    @pl.when(flag[0] == 1)
    def _():
        for g in range(kvh):
            k2[...], vt[...] = keys_twice(kv_ref, g, kw)

            def scores(h, s_ref, g=g):
                at = g * group + h
                s_ref[...] = nt(k2[...], qs_ref[:, pl.ds(pl.multiple_of(at * 2 * HD, 2 * HD), 2 * HD)])

            def soft(h, s_ref, g=g):
                at = g * group + h
                cols = pl.ds(pl.multiple_of(at * HD, HD), HD)
                row = pl.ds(at, 1)
                for b in (0, 1):
                    rows = slice(b * t, (b + 1) * t)
                    s = s_ref[:, rows]
                    old = m_in[row, rows]
                    new = jnp.maximum(old, jnp.max(s, axis=0, keepdims=True))
                    e = jnp.exp(s - new)
                    fade = jnp.exp(old - new)
                    m_ref[row, rows] = new
                    l_ref[row, rows] = l_in[row, rows] * fade + jnp.sum(e, axis=0, keepdims=True)
                    acc_ref[cols, rows] = acc_in[cols, rows] * fade + nn(vt[...], e.astype(BF16))

            scores(0, sa)

            def pair(i, _):
                scores(2 * i + 1, sb)
                soft(2 * i, sa)
                scores(jnp.minimum(2 * i + 2, group - 1), sa)
                soft(2 * i + 1, sb)
                return 0

            lax.fori_loop(0, group // 2, pair, 0)


def residual_kernel(y_ref, acc_ref, l_ref, r_ref, fs_ref, sin_ref, res_ref, d1_ref, coded_ref):
    t = y_ref.shape[0] // 2
    width = y_ref.shape[1]
    n = r_ref.shape[1]
    state = sin_ref[...]
    first = fs_ref[t - 1 : t, :]
    parts = []
    for b in (0, 1):
        rows = slice(b * t, (b + 1) * t)
        fs = fs_ref[rows, :]
        r = r_ref[rows, :]
        heads = [
            (acc_ref[h * HD : (h + 1) * HD, rows] / l_ref[h : h + 1, rows]).astype(BF16).T
            for h in range(width // HD)
        ]
        teach = jnp.concatenate(heads, axis=1).astype(F32)
        res = y_ref[rows, :] + fs * nn(twice(r), stack2(state * first if b else state)) - teach
        res_ref[rows, :] = res
        hi, lo = split2(res * fs)
        parts.append(tn(r, hi) + tn(r, lo))
    d1_ref[...] = parts[1]
    coded_ref[:n, :], coded_ref[n:, :] = code_rows(parts[0] + first * parts[1], [])


def back_kernel(
    res_ref, x_ref, w_ref, r_ref, clsx_ref, crow_ref, fs_ref, wexp_ref, sin_ref, st0_ref, d1_ref,
    back_ref, gw_ref, gr_ref, a_ref, pair,
):
    t = x_ref.shape[0] // 2
    th = t // 2
    width = x_ref.shape[1]
    heads = crow_ref.shape[0]
    hw = width // heads
    per = 128 // hw
    first = fs_ref[t - 1 : t, :]
    for b in (0, 1):
        rows = slice(b * t, (b + 1) * t)
        keep = iota((t, t), 1) >= iota((t, t), 0)
        w = w_ref[rows, :]
        r = r_ref[rows, :]
        a_ref[...] = jnp.where(keep, nt(w, r), 0.0)
        pair[...] = jnp.zeros_like(pair)
        if b == 0:
            d1 = d1_ref[...]
            wexp = wexp_ref[rows, :]
            back_ref[rows, :] = wexp * nn(twice(w), stack2(d1))
            gw = nt3(x_ref[rows, :].astype(F32) * wexp, d1)
            state = sin_ref[...]
        else:
            gw = None
            state = first * sin_ref[...] + st0_ref[...]
        gr = nt3(res_ref[rows, :] * fs_ref[rows, :], state)

        def one(i, rows=rows, b=b):
            cols = pl.ds(pl.multiple_of(i * 128, 128), 128)
            xp = x_ref[rows, cols]
            rh, rl = split2(res_ref[rows, cols])
            both = jnp.concatenate([rh, rl], axis=1)
            cc = clsx_ref[rows, cols]
            lane = iota((t, 128), 1)
            out, above, below = None, 0.0, 0.0
            for a in range(per):
                cj = cc[:, a * hw : a * hw + 1]
                ci = crow_ref[pl.ds(i * per + a, 1), rows]
                xx = twice(jnp.where((lane // hw) == a, xp, jnp.zeros_like(xp)))
                e1 = jnp.exp(jnp.minimum(ci - cj[:th], 0.0))
                e2 = jnp.exp(jnp.minimum(ci[:, th:] - cj[th:], 0.0))
                h1, l1 = split2(e1 * a_ref[:th, :])
                h2, l2 = split2(e2 * a_ref[th:, th:])
                p1 = nn(h1, both)
                p2 = nn(h2, both[th:])
                u1 = p1[:, :128] + p1[:, 128:] + nn(l1, rh)
                u2 = p2[:, :128] + p2[:, 128:] + nn(l2, rh[th:])
                u = jnp.concatenate([u1, u2], axis=0)
                out = u if out is None else jnp.where(lane >= a * hw, u, out)
                above += e1 * nt(xx[:th], both)
                below += e2 * nt(xx[th:], both[th:])
            if b == 0:
                out = out + back_ref[rows, cols]
            return cols, out, above, below

        def two(i, _, rows=rows, one=one):
            done = [one(2 * i), one(2 * i + 1)]
            for cols, out, _, _ in done:
                back_ref[rows, cols] = out
            pair[:th, :] += done[0][2] + done[1][2]
            pair[th:, th:] += done[0][3] + done[1][3]
            return 0

        lax.fori_loop(0, width // 256, two, 0)
        ph, plo = split2(jnp.where(keep, pair[...], 0.0))
        gr_ref[rows, :] = gr + tn(ph, w) + tn(plo, w)
        mixed = nn(ph, r) + nn(plo, r)
        gw_ref[rows, :] = mixed if gw is None else mixed + gw


def ready_kernel(x_ref, ls_ref, ld_ref, extra_ref, wexp_ref, xh_ref, xl_ref):
    t = x_ref.shape[0]
    ccol = cum_col(ld_ref[...])
    wexp = spread(
        jnp.exp(ccol[t - 1 : t, :] + extra_ref[...] - ccol + turn(ls_ref[...])), x_ref.shape[1]
    )
    wexp_ref[...] = wexp
    xh_ref[...], xl_ref[...] = split2(x_ref[...].astype(F32) * wexp)


def write_kernel(xh_ref, xl_ref, g_ref, gw0_ref, gw_ref):
    gh, gl = split2(g_ref[...])
    n = gh.shape[0]
    both = nt(xh_ref[...], jnp.concatenate([gh, gl], axis=0))
    gw_ref[...] = gw0_ref[...] + both[:, :n] + both[:, n:] + nt(xl_ref[...], gh)


def final_kernel(back_ref, wexp_ref, x_ref, w_ref, g_ref, gi_ref, gls_ref):
    width = x_ref.shape[1]
    heads = gls_ref.shape[0]
    out = back_ref[...] + wexp_ref[...] * nn(twice(w_ref[...]), stack2(g_ref[...]))
    gi_ref[...] = out
    ph, plo = split2(x_ref[...].astype(F32) * out)
    mat = spread_matrix(heads, width)
    gls_ref[...] = nt(mat, ph) + nt(mat, plo)


VM = pl.BlockSpec(memory_space=pltpu.VMEM)


def call(kernel, outs, args, scratch=(), flops=0, in_specs=None, alias=None):
    shapes = [jax.ShapeDtypeStruct(s, d) for s, d in outs]
    moved = sum(a.size * a.dtype.itemsize for a in args)
    return pl.pallas_call(
        kernel,
        out_shape=shapes,
        in_specs=in_specs or [VM] * len(args),
        out_specs=[VM] * len(shapes),
        scratch_shapes=list(scratch),
        input_output_aliases=alias or {},
        cost_estimate=pl.CostEstimate(flops=flops, bytes_accessed=moved, transcendentals=0),
        compiler_params=pltpu.CompilerParams(vmem_limit_bytes=16 * 2**20),
    )(*args)


def decode(coded, rows, weight):
    power = coded[rows : rows + 1].astype(F32)
    return coded[:rows].astype(F32) * (jnp.exp2(power - 12.0) * weight)


def on_device(q, k, v, x, wr, rd, ls, ld):
    t = q.shape[0]
    count = lax.axis_size("seq")
    tp = lax.axis_size("tp")
    chips = count // 2
    index = lax.axis_index("seq")
    core, chip = index % 2, index // 2
    heads = ls.shape[0]
    hh = heads // 2
    n = wr.shape[1]
    hc = x.shape[1] // 2
    qc = q.shape[1] // 2
    kvh = k.shape[1] // HD
    kw = k.shape[1] // 2 if kvh % 2 == 0 else k.shape[1]

    def swap(a, bits):
        return lax.ppermute(a, "seq", [(i, i ^ bits) for i in range(count)])

    def half(a, which, width, axis=1):
        return lax.dynamic_slice_in_dim(a, which * width, width, axis=axis)

    def joined(own, other, axis=0):
        a = jnp.where(core == 0, own, other)
        b = jnp.where(core == 0, other, own)
        return jnp.concatenate([a, b], axis=axis)

    def near(a):
        return {1 << b: swap(a, 2 << b) for b in range(chips.bit_length() - 1)}

    def relay(got, token):
        got = dict(got)
        for d in range(1, chips):
            if d not in got:
                low = d & -d
                held, _ = lax.optimization_barrier((got[d - low], token))
                got[d] = swap(held, 2 * low)
        return [got[d] for d in range(1, chips)]

    def kv_half(which):
        if kvh % 2 == 0:
            return jnp.concatenate([half(k, which, kw), half(v, which, kw)], axis=1)
        return jnp.concatenate([k, v], axis=1)

    kv = joined(kv_half(core), swap(kv_half(1 - core), 1))
    keys_near = near(kv)
    x1, q1, wr1, rd1, _ = lax.optimization_barrier((x, q, wr, rd, kv))
    rates = swap(jnp.concatenate([ls, ld], axis=0), 1)
    lsc = joined(half(ls, core, hh, 0), half(rates, core, hh, 0), 1)
    ldc = joined(half(ld, core, hh, 0), half(rates[heads:], core, hh, 0), 1)
    mates = swap(jnp.concatenate([half(x1, 1 - core, hc), wr1, rd1], axis=1), 1)
    xc = joined(half(x1, core, hc), mates[:, :hc])
    wc = joined(wr1, mates[:, hc : hc + n])
    rc = joined(rd1, mates[:, hc + n :])
    qg = joined(half(q1, core, qc), swap(half(q1, 1 - core, qc), 1))

    mm = 2 * 2 * t * hc * n
    code = ((n + 16, hc), F32)
    st0, coded, wexpc = call(
        state_kernel, [((n, hc), F32), code, ((2 * t, hc), F32)], (xc, wc, lsc, ldc),
        flops=4 * mm,
    )
    mine = coded.astype(F16)
    states_near = near(mine)
    qh = qc // HD
    carry = [((qc, 2 * t), F32), ((qh, 2 * t), F32), ((qh, 2 * t), F32)]
    qs, *soft = call(
        own_kernel, [((2 * t, 2 * qc), BF16), *carry], (qg, kv),
        scratch=[pltpu.VMEM((2 * t, 2 * HD), BF16), pltpu.VMEM((HD, 2 * t), BF16), pltpu.VMEM((t, t), F32)]
        + [pltpu.VMEM((t, t), F32), pltpu.VMEM((2 * t, t), F32)] * 2,
        flops=4 * (2 * t) ** 2 * qc,
    )
    ybase, fs, clsx, crow = call(
        local_kernel,
        [((2 * t, hc), F32), ((2 * t, hc), F32), ((2 * t, hc), F32), ((hh, 2 * t), F32)],
        (xc, wc, rc, lsc, ldc, st0),
        scratch=[pltpu.VMEM((t, hc), F32), pltpu.VMEM((hh, t), F32), pltpu.VMEM((t, t), F32)],
        flops=8 * mm,
    )
    far = relay(keys_near, soft[1])
    states = relay(states_near, soft[1])
    decays = [jnp.sum(f[n + 1 : n + 4].astype(F32), axis=0, keepdims=True) for f in states]

    def weight(d, later):
        p = chip ^ d
        low, high = (chip, p) if later else (p, chip)
        between = jnp.zeros((1, hc), F32)
        for m in range(1, chips):
            at = chip ^ m
            between += jnp.where((at > low) & (at < high), decays[m - 1], 0.0)
        return jnp.where((p > chip) if later else (p < chip), jnp.exp(between), 0.0)

    def combine(got, later):
        return sum(decode(g, n, weight(d, later)) for d, g in enumerate(got, 1))

    for d, keys in enumerate(far, 1):
        flag = jnp.reshape((chip ^ d) < chip, (1,)).astype(jnp.int32)
        soft = call(
            far_kernel, carry, (flag, qs, keys, *soft),
            scratch=[pltpu.VMEM((2 * t, 2 * HD), BF16), pltpu.VMEM((HD, 2 * t), BF16)] + [pltpu.VMEM((2 * t, 2 * t), F32)] * 2,
            flops=4 * (2 * t) ** 2 * qc, alias={3: 0, 4: 1, 5: 2},
            in_specs=[pl.BlockSpec(memory_space=pltpu.SMEM)] + [VM] * 5,
        )
    incoming = combine(states, False)
    res, d1, dcode = call(
        residual_kernel, [((2 * t, hc), F32), ((n, hc), F32), code],
        (ybase, soft[0], soft[2], rc, fs, incoming), flops=8 * mm,
    )
    sent = dcode.astype(F16)
    coming = [swap(sent, 2 * d) for d in range(1, chips)]
    back, gw, gr = call(
        back_kernel, [((2 * t, hc), F32), ((2 * t, n), F32), ((2 * t, n), F32)],
        (res, xc, wc, rc, clsx, crow, fs, wexpc, incoming, st0, d1),
        scratch=[pltpu.VMEM((t, t), F32), pltpu.VMEM((t, t), F32)],
        flops=16 * mm,
    )
    other_total = jnp.sum(rates[heads:], axis=1)[None, :]
    extra = jnp.where(core == 0, other_total, 0.0)
    wexp, xh, xl = call(
        ready_kernel, [((t, 2 * hc), F32), ((t, 2 * hc), BF16), ((t, 2 * hc), BF16)],
        (x, ls, ld, extra), flops=2 * mm,
    )

    def home(a):
        return half(a, core, t, 0), swap(half(a, 1 - core, t, 0), 1)

    def tp_sum(a):
        bit = 1
        while bit < tp:
            a = a + lax.ppermute(a, "tp", [(i, i ^ bit) for i in range(tp)])
            bit *= 2
        return a

    back_all = joined(*home(back), 1)
    own, other = home(jnp.concatenate([gw, gr], axis=1))
    grads = own + other
    gw0, gr0 = grads[:, :n], grads[:, n:]
    grad_read = tp_sum(gr0)
    *coming, grad_read, wexp, back_all = lax.optimization_barrier((*coming, grad_read, wexp, back_all))
    arriving = combine(coming, True)
    arrived = joined(arriving, swap(arriving, 1), 1)
    (gwp,) = call(write_kernel, [((t, n), F32)], (xh, xl, arrived, gw0), flops=4 * mm)
    grad_write = tp_sum(gwp)
    gi, gls = call(
        final_kernel, [((t, 2 * hc), F32), ((heads, t), F32)], (back_all, wexp, x, wr, arrived),
        flops=8 * mm,
    )
    return (gi, grad_write, grad_read, gls)


def solution(mesh):
    in_specs = (
        P("seq", "tp"), P("seq", "tp"), P("seq", "tp"), P("seq", "tp"),
        P("seq", None), P("seq", None), P("tp", "seq"), P("tp", "seq"),
    )
    out_specs = (P("seq", "tp"), P("seq", None), P("seq", None), P("tp", "seq"))
    return jax.shard_map(
        on_device, mesh=mesh, in_specs=in_specs, out_specs=out_specs, check_vma=False
    )
```

```python
import functools
import math

import jax
import jax.numpy as jnp
from jax import lax
from jax.experimental import pallas as pl
from jax.experimental.pallas import tpu as pltpu
from jax.sharding import PartitionSpec as P


HD = 128
F32, BF16, F16 = jnp.float32, jnp.bfloat16, jnp.float16


def nn(a, b):
    return lax.dot_general(a, b, (((1,), (0,)), ((), ())), preferred_element_type=F32)


def nt(a, b):
    return lax.dot_general(a, b, (((1,), (1,)), ((), ())), preferred_element_type=F32)


def tn(a, b):
    return lax.dot_general(a, b, (((0,), (0,)), ((), ())), preferred_element_type=F32)


def split2(a):
    hi = a.astype(BF16)
    return hi, (a - hi.astype(F32)).astype(BF16)


def split3(a):
    hi = a.astype(BF16)
    rest = a - hi.astype(F32)
    mid = rest.astype(BF16)
    return hi, mid, (rest - mid.astype(F32)).astype(BF16)


def iota(shape, dim):
    return lax.broadcasted_iota(jnp.int32, shape, dim)


def lower(t):
    return (iota((t, t), 0) >= iota((t, t), 1)).astype(BF16)


def spread_matrix(heads, width, times=1):
    row = iota((times * heads, width), 0) % heads
    return (iota((times * heads, width), 1) // (width // heads) == row).astype(BF16)


def spread(col, width):
    pieces = [p.astype(F32) for p in split3(col)]
    stacked = jnp.concatenate(pieces, axis=1).astype(BF16)
    return nn(stacked, spread_matrix(col.shape[1], width, 3))


def stack2(a):
    return jnp.concatenate(split2(a), axis=0)


def twice(a):
    return jnp.concatenate([a, a], axis=1)


def nt3(a, b):
    ah, al = split2(a)
    bh, bl = split2(b)
    both = nt(ah, jnp.concatenate([bh, bl], axis=0))
    half = both.shape[1] // 2
    return both[:, :half] + both[:, half:] + nt(al, bh)


def code_rows(state, extra):
    top = jnp.max(jnp.abs(state), axis=0, keepdims=True)
    power = jnp.ceil(jnp.log2(jnp.maximum(top, 1e-30)))
    used = sum(e.shape[0] for e in extra)
    rest = jnp.zeros((15 - used, state.shape[1]), F32)
    return state * jnp.exp2(12.0 - power), jnp.concatenate([power, *extra, rest], axis=0)


def spread_row(row, width):
    return spread(jnp.broadcast_to(row, (8, row.shape[1])), width)[0:1]


def cum_col(ld):
    tri = lower(ld.shape[1])
    a, b, c = split3(ld)
    return nt(tri, a) + nt(tri, b) + nt(tri, c)


def cum_row(ld):
    tri = lower(ld.shape[1])
    a, b, c = split3(ld)
    return nt(a, tri) + nt(b, tri) + nt(c, tri)


def turn(rows):
    t = rows.shape[1]
    eye = (iota((t, t), 0) == iota((t, t), 1)).astype(BF16)
    a, b, c = split3(rows)
    return nt(eye, a) + nt(eye, b) + nt(eye, c)


def state_kernel(x_ref, w_ref, ls_ref, ld_ref, st0_ref, coded_ref, wexp_ref):
    t = x_ref.shape[0] // 2
    width = x_ref.shape[1]
    n = w_ref.shape[1]
    parts, tots = [], []
    for b in (0, 1):
        rows = slice(b * t, (b + 1) * t)
        ccol = cum_col(ld_ref[:, rows])
        tot = ccol[t - 1 : t, :]
        wexp = spread(jnp.exp(tot - ccol + turn(ls_ref[:, rows])), width)
        wexp_ref[rows, :] = wexp
        hi, lo = split2(x_ref[rows, :].astype(F32) * wexp)
        parts.append(tn(w_ref[rows, :], hi) + tn(w_ref[rows, :], lo))
        tots.append(tot)
    st0_ref[...] = parts[0]
    state = spread_row(jnp.exp(tots[1]), width) * parts[0] + parts[1]
    pieces = [p.astype(F32) for p in split3(spread_row(tots[0] + tots[1], width))]
    coded_ref[:n, :], coded_ref[n:, :] = code_rows(state, pieces)


def merge_kernel(flag, own_ref, got_ref, out_ref, *, group):
    n = own_ref.shape[0] - 16
    used = 3 * group
    own_rows = own_ref[n + 1 : n + 1 + used, :]
    got_rows = got_ref[n + 1 : n + 1 + used, :]
    own = own_ref[:n, :] * jnp.exp2(own_ref[n : n + 1, :] - 12.0)
    got = got_ref[:n, :] * jnp.exp2(got_ref[n : n + 1, :] - 12.0)
    own_fade = jnp.exp(jnp.sum(own_rows, axis=0, keepdims=True))
    got_fade = jnp.exp(jnp.sum(got_rows, axis=0, keepdims=True))
    earlier = flag[0] == 1
    merged = own * jnp.where(earlier, 1.0, got_fade) + got * jnp.where(earlier, own_fade, 1.0)
    out_ref[:n, :], out_ref[n:, :] = code_rows(merged, [own_rows, got_rows])


def local_kernel(
    x_ref, w_ref, r_ref, ls_ref, ld_ref, st0_ref,
    y_ref, fs_ref, clsx_ref, crow_ref, cexp, clsrow, a_ref,
):
    t = x_ref.shape[0] // 2
    th = t // 2
    width = x_ref.shape[1]
    heads = ls_ref.shape[0]
    hw = width // heads
    per = 128 // hw
    for b in (0, 1):
        rows = slice(b * t, (b + 1) * t)
        ccol = cum_col(ld_ref[:, rows])
        cexp[...] = spread(ccol, width)
        fs = spread(jnp.exp(ccol), width)
        fs_ref[rows, :] = fs
        clsx_ref[rows, :] = spread(ccol - turn(ls_ref[:, rows]), width)
        crow = cum_row(ld_ref[:, rows])
        crow_ref[:, rows] = crow
        clsrow[...] = crow - ls_ref[:, rows]
        keep = iota((t, t), 0) >= iota((t, t), 1)
        a_ref[...] = jnp.where(keep, nt(r_ref[rows, :], w_ref[rows, :]), 0.0)
        if b == 1:
            y_ref[rows, :] = fs * nn(twice(r_ref[rows, :]), stack2(st0_ref[...]))

        def one(i, rows=rows, b=b):
            cols = pl.ds(pl.multiple_of(i * 128, 128), 128)
            xp = x_ref[rows, cols]
            xtop = jnp.concatenate([xp[:th], xp[:th]], axis=0)
            cc = cexp[:, cols]
            lane = iota((t, 128), 1)
            out = None
            for a in range(per):
                ci = cc[:, a * hw : a * hw + 1]
                cj = clsrow[pl.ds(i * per + a, 1), :]
                top = jnp.exp(jnp.minimum(ci[:th] - cj[:, :th], 0.0)) * a_ref[:th, :th]
                bot = jnp.exp(jnp.minimum(ci[th:] - cj, 0.0)) * a_ref[th:, :]
                yt = nn(jnp.concatenate(split2(top), axis=1), xtop)
                b1, b2 = split2(bot)
                yb = nn(b1, xp) + nn(b2, xp)
                mine = jnp.concatenate([yt, yb], axis=0)
                out = mine if out is None else jnp.where(lane >= a * hw, mine, out)
            if b == 1:
                out = out + y_ref[rows, cols]
            return cols, out

        def two(i, _, rows=rows, one=one):
            done = [one(2 * i), one(2 * i + 1)]
            for cols, out in done:
                y_ref[rows, cols] = out
            return 0

        lax.fori_loop(0, width // 256, two, 0)


def keys_twice(kv_ref, g, kw):
    k = kv_ref[:, g * HD : (g + 1) * HD]
    return jnp.concatenate([k, k], axis=1), kv_ref[:, kw + g * HD : kw + (g + 1) * HD].T


def own_kernel(q_ref, kv_ref, qs_ref, acc_ref, m_ref, l_ref, k2, vt, bias, s0a, s1a, s0b, s1b):
    t = q_ref.shape[0] // 2
    kw = kv_ref.shape[1] // 2
    kvh = kw // HD
    group = q_ref.shape[1] // HD // kvh
    scale = 1.0 / math.sqrt(HD)
    bias[...] = jnp.where(iota((t, t), 0) <= iota((t, t), 1), 0.0, -1e30)
    for g in range(kvh):
        k2[...], vt[...] = keys_twice(kv_ref, g, kw)

        def scores(h, s0, s1, g=g):
            at = g * group + h
            q = q_ref[:, pl.ds(pl.multiple_of(at * HD, HD), HD)].astype(F32) * scale
            both = jnp.concatenate(split2(q), axis=1)
            qs_ref[:, pl.ds(pl.multiple_of(at * 2 * HD, 2 * HD), 2 * HD)] = both
            s0[...] = nt(k2[:t, :], both[:t]) + bias[...]
            s1[:t, :] = nt(k2[:t, :], both[t:])
            s1[t:, :] = nt(k2[t:, :], both[t:]) + bias[...]

        def soft(h, s0, s1, g=g):
            at = g * group + h
            cols = pl.ds(pl.multiple_of(at * HD, HD), HD)
            for b, s_ref in ((0, s0), (1, s1)):
                rows = slice(b * t, (b + 1) * t)
                s = s_ref[...]
                top = jnp.max(s, axis=0, keepdims=True)
                e = jnp.exp(s - top)
                m_ref[pl.ds(at, 1), rows] = top
                l_ref[pl.ds(at, 1), rows] = jnp.sum(e, axis=0, keepdims=True)
                acc_ref[cols, rows] = nn(vt[:, : (b + 1) * t], e.astype(BF16))

        scores(0, s0a, s1a)

        def pair(i, _):
            scores(2 * i + 1, s0b, s1b)
            soft(2 * i, s0a, s1a)
            scores(jnp.minimum(2 * i + 2, group - 1), s0a, s1a)
            soft(2 * i + 1, s0b, s1b)
            return 0

        lax.fori_loop(0, group // 2, pair, 0)


def far_kernel(flag, qs_ref, kv_ref, acc_in, m_in, l_in, acc_ref, m_ref, l_ref, k2, vt, sa, sb):
    t = qs_ref.shape[0] // 2
    kw = kv_ref.shape[1] // 2
    kvh = kw // HD
    group = qs_ref.shape[1] // (2 * HD) // kvh

    @pl.when(flag[0] == 0)
    def _():
        acc_ref[...] = acc_in[...]
        m_ref[...] = m_in[...]
        l_ref[...] = l_in[...]

    @pl.when(flag[0] == 1)
    def _():
        for g in range(kvh):
            k2[...], vt[...] = keys_twice(kv_ref, g, kw)

            def scores(h, s_ref, g=g):
                at = g * group + h
                s_ref[...] = nt(k2[...], qs_ref[:, pl.ds(pl.multiple_of(at * 2 * HD, 2 * HD), 2 * HD)])

            def soft(h, s_ref, g=g):
                at = g * group + h
                cols = pl.ds(pl.multiple_of(at * HD, HD), HD)
                row = pl.ds(at, 1)
                for b in (0, 1):
                    rows = slice(b * t, (b + 1) * t)
                    s = s_ref[:, rows]
                    old = m_in[row, rows]
                    new = jnp.maximum(old, jnp.max(s, axis=0, keepdims=True))
                    e = jnp.exp(s - new)
                    fade = jnp.exp(old - new)
                    m_ref[row, rows] = new
                    l_ref[row, rows] = l_in[row, rows] * fade + jnp.sum(e, axis=0, keepdims=True)
                    acc_ref[cols, rows] = acc_in[cols, rows] * fade + nn(vt[...], e.astype(BF16))

            scores(0, sa)

            def pair(i, _):
                scores(2 * i + 1, sb)
                soft(2 * i, sa)
                scores(jnp.minimum(2 * i + 2, group - 1), sa)
                soft(2 * i + 1, sb)
                return 0

            lax.fori_loop(0, group // 2, pair, 0)


def residual_kernel(y_ref, acc_ref, l_ref, r_ref, fs_ref, sin_ref, res_ref, d1_ref, coded_ref):
    t = y_ref.shape[0] // 2
    width = y_ref.shape[1]
    n = r_ref.shape[1]
    state = sin_ref[...]
    first = fs_ref[t - 1 : t, :]
    parts = []
    for b in (0, 1):
        rows = slice(b * t, (b + 1) * t)
        fs = fs_ref[rows, :]
        r = r_ref[rows, :]
        heads = [
            (acc_ref[h * HD : (h + 1) * HD, rows] / l_ref[h : h + 1, rows]).astype(BF16).T
            for h in range(width // HD)
        ]
        teach = jnp.concatenate(heads, axis=1).astype(F32)
        res = y_ref[rows, :] + fs * nn(twice(r), stack2(state * first if b else state)) - teach
        res_ref[rows, :] = res
        hi, lo = split2(res * fs)
        parts.append(tn(r, hi) + tn(r, lo))
    d1_ref[...] = parts[1]
    coded_ref[:n, :], coded_ref[n:, :] = code_rows(parts[0] + first * parts[1], [])


def back_kernel(
    res_ref, x_ref, w_ref, r_ref, clsx_ref, crow_ref, fs_ref, wexp_ref, sin_ref, st0_ref, d1_ref,
    back_ref, gw_ref, gr_ref, a_ref, pair,
):
    t = x_ref.shape[0] // 2
    th = t // 2
    width = x_ref.shape[1]
    heads = crow_ref.shape[0]
    hw = width // heads
    per = 128 // hw
    first = fs_ref[t - 1 : t, :]
    for b in (0, 1):
        rows = slice(b * t, (b + 1) * t)
        keep = iota((t, t), 1) >= iota((t, t), 0)
        w = w_ref[rows, :]
        r = r_ref[rows, :]
        a_ref[...] = jnp.where(keep, nt(w, r), 0.0)
        pair[...] = jnp.zeros_like(pair)
        if b == 0:
            d1 = d1_ref[...]
            wexp = wexp_ref[rows, :]
            back_ref[rows, :] = wexp * nn(twice(w), stack2(d1))
            gw = nt3(x_ref[rows, :].astype(F32) * wexp, d1)
            state = sin_ref[...]
        else:
            gw = None
            state = first * sin_ref[...] + st0_ref[...]
        gr = nt3(res_ref[rows, :] * fs_ref[rows, :], state)

        def one(i, rows=rows, b=b):
            cols = pl.ds(pl.multiple_of(i * 128, 128), 128)
            xp = x_ref[rows, cols]
            rh, rl = split2(res_ref[rows, cols])
            both = jnp.concatenate([rh, rl], axis=1)
            cc = clsx_ref[rows, cols]
            lane = iota((t, 128), 1)
            out, above, below = None, 0.0, 0.0
            for a in range(per):
                cj = cc[:, a * hw : a * hw + 1]
                ci = crow_ref[pl.ds(i * per + a, 1), rows]
                xx = twice(jnp.where((lane // hw) == a, xp, jnp.zeros_like(xp)))
                e1 = jnp.exp(jnp.minimum(ci - cj[:th], 0.0))
                e2 = jnp.exp(jnp.minimum(ci[:, th:] - cj[th:], 0.0))
                h1, l1 = split2(e1 * a_ref[:th, :])
                h2, l2 = split2(e2 * a_ref[th:, th:])
                p1 = nn(h1, both)
                p2 = nn(h2, both[th:])
                u1 = p1[:, :128] + p1[:, 128:] + nn(l1, rh)
                u2 = p2[:, :128] + p2[:, 128:] + nn(l2, rh[th:])
                u = jnp.concatenate([u1, u2], axis=0)
                out = u if out is None else jnp.where(lane >= a * hw, u, out)
                above += e1 * nt(xx[:th], both)
                below += e2 * nt(xx[th:], both[th:])
            if b == 0:
                out = out + back_ref[rows, cols]
            return cols, out, above, below

        def two(i, _, rows=rows, one=one):
            done = [one(2 * i), one(2 * i + 1)]
            for cols, out, _, _ in done:
                back_ref[rows, cols] = out
            pair[:th, :] += done[0][2] + done[1][2]
            pair[th:, th:] += done[0][3] + done[1][3]
            return 0

        lax.fori_loop(0, width // 256, two, 0)
        ph, plo = split2(jnp.where(keep, pair[...], 0.0))
        gr_ref[rows, :] = gr + tn(ph, w) + tn(plo, w)
        mixed = nn(ph, r) + nn(plo, r)
        gw_ref[rows, :] = mixed if gw is None else mixed + gw


def ready_kernel(x_ref, ls_ref, ld_ref, extra_ref, wexp_ref, xh_ref, xl_ref):
    t = x_ref.shape[0]
    ccol = cum_col(ld_ref[...])
    wexp = spread(
        jnp.exp(ccol[t - 1 : t, :] + extra_ref[...] - ccol + turn(ls_ref[...])), x_ref.shape[1]
    )
    wexp_ref[...] = wexp
    xh_ref[...], xl_ref[...] = split2(x_ref[...].astype(F32) * wexp)


def write_kernel(xh_ref, xl_ref, g_ref, gw0_ref, gw_ref):
    gh, gl = split2(g_ref[...])
    n = gh.shape[0]
    both = nt(xh_ref[...], jnp.concatenate([gh, gl], axis=0))
    gw_ref[...] = gw0_ref[...] + both[:, :n] + both[:, n:] + nt(xl_ref[...], gh)


def final_kernel(back_ref, wexp_ref, x_ref, w_ref, g_ref, gi_ref, gls_ref):
    width = x_ref.shape[1]
    heads = gls_ref.shape[0]
    out = back_ref[...] + wexp_ref[...] * nn(twice(w_ref[...]), stack2(g_ref[...]))
    gi_ref[...] = out
    ph, plo = split2(x_ref[...].astype(F32) * out)
    mat = spread_matrix(heads, width)
    gls_ref[...] = nt(mat, ph) + nt(mat, plo)


VM = pl.BlockSpec(memory_space=pltpu.VMEM)


def call(kernel, outs, args, scratch=(), flops=0, in_specs=None, alias=None):
    shapes = [jax.ShapeDtypeStruct(s, d) for s, d in outs]
    moved = sum(a.size * a.dtype.itemsize for a in args)
    return pl.pallas_call(
        kernel,
        out_shape=shapes,
        in_specs=in_specs or [VM] * len(args),
        out_specs=[VM] * len(shapes),
        scratch_shapes=list(scratch),
        input_output_aliases=alias or {},
        cost_estimate=pl.CostEstimate(flops=flops, bytes_accessed=moved, transcendentals=0),
        compiler_params=pltpu.CompilerParams(vmem_limit_bytes=16 * 2**20),
    )(*args)


def decode(coded, rows, weight):
    power = coded[rows : rows + 1].astype(F32)
    return coded[:rows].astype(F32) * (jnp.exp2(power - 12.0) * weight)


def on_device(q, k, v, x, wr, rd, ls, ld):
    t = q.shape[0]
    count = lax.axis_size("seq")
    tp = lax.axis_size("tp")
    chips = count // 2
    index = lax.axis_index("seq")
    core, chip = index % 2, index // 2
    heads = ls.shape[0]
    hh = heads // 2
    n = wr.shape[1]
    hc = x.shape[1] // 2
    qc = q.shape[1] // 2
    kvh = k.shape[1] // HD
    kw = k.shape[1] // 2 if kvh % 2 == 0 else k.shape[1]

    def swap(a, bits):
        return lax.ppermute(a, "seq", [(i, i ^ bits) for i in range(count)])

    def half(a, which, width, axis=1):
        return lax.dynamic_slice_in_dim(a, which * width, width, axis=axis)

    def joined(own, other, axis=0):
        a = jnp.where(core == 0, own, other)
        b = jnp.where(core == 0, other, own)
        return jnp.concatenate([a, b], axis=axis)

    def near(a):
        return {1 << b: swap(a, 2 << b) for b in range(chips.bit_length() - 1)}

    def relay(got, token):
        got = dict(got)
        for d in range(1, chips):
            if d not in got:
                low = d & -d
                held, _ = lax.optimization_barrier((got[d - low], token))
                need = [c for c in range(chips) if c ^ d < c or c ^ low ^ d < c ^ low]
                pairs = [(2 * c + k, 2 * (c ^ low) + k) for c in need for k in (0, 1)]
                got[d] = lax.ppermute(held, "seq", pairs)
        return [got[d] for d in range(1, chips)]

    def kv_half(which):
        if kvh % 2 == 0:
            return jnp.concatenate([half(k, which, kw), half(v, which, kw)], axis=1)
        return jnp.concatenate([k, v], axis=1)

    kv = joined(kv_half(core), swap(kv_half(1 - core), 1))
    keys_near = near(kv)
    x1, q1, wr1, rd1, _ = lax.optimization_barrier((x, q, wr, rd, kv))
    rates = swap(jnp.concatenate([ls, ld], axis=0), 1)
    lsc = joined(half(ls, core, hh, 0), half(rates, core, hh, 0), 1)
    ldc = joined(half(ld, core, hh, 0), half(rates[heads:], core, hh, 0), 1)
    mates = swap(jnp.concatenate([half(x1, 1 - core, hc), wr1, rd1], axis=1), 1)
    xc = joined(half(x1, core, hc), mates[:, :hc])
    wc = joined(wr1, mates[:, hc : hc + n])
    rc = joined(rd1, mates[:, hc + n :])
    qg = joined(half(q1, core, qc), swap(half(q1, 1 - core, qc), 1))

    mm = 2 * 2 * t * hc * n
    code = ((n + 16, hc), F32)
    st0, coded, wexpc = call(
        state_kernel, [((n, hc), F32), code, ((2 * t, hc), F32)], (xc, wc, lsc, ldc),
        flops=4 * mm,
    )

    def state_stage(coded, bit):
        return swap(coded.astype(F16), 2 << bit).astype(F32)

    stages = [state_stage(coded, 0)] if chips > 1 else []
    qh = qc // HD
    carry = [((qc, 2 * t), F32), ((qh, 2 * t), F32), ((qh, 2 * t), F32)]
    qs, *soft = call(
        own_kernel, [((2 * t, 2 * qc), BF16), *carry], (qg, kv),
        scratch=[pltpu.VMEM((2 * t, 2 * HD), BF16), pltpu.VMEM((HD, 2 * t), BF16), pltpu.VMEM((t, t), F32)]
        + [pltpu.VMEM((t, t), F32), pltpu.VMEM((2 * t, t), F32)] * 2,
        flops=4 * (2 * t) ** 2 * qc,
    )
    ybase, fs, clsx, crow = call(
        local_kernel,
        [((2 * t, hc), F32), ((2 * t, hc), F32), ((2 * t, hc), F32), ((hh, 2 * t), F32)],
        (xc, wc, rc, lsc, ldc, st0),
        scratch=[pltpu.VMEM((t, hc), F32), pltpu.VMEM((hh, t), F32), pltpu.VMEM((t, t), F32)],
        flops=8 * mm,
    )
    for bit in range(1, chips.bit_length() - 1):
        flag = jnp.reshape((chip >> (bit - 1)) % 2, (1,)).astype(jnp.int32)
        (coded,) = call(
            functools.partial(merge_kernel, group=1 << (bit - 1)), [code], (flag, coded, stages[-1]),
            in_specs=[pl.BlockSpec(memory_space=pltpu.SMEM), VM, VM],
        )
        stages.append(state_stage(coded, bit))
    decays = {}
    for bit, got in enumerate(stages):
        for m in range(1 << bit):
            at = n + 1 + 3 * m
            decays[(1 << bit) + m] = jnp.sum(got[at : at + 3], axis=0, keepdims=True)

    def between(low, high, most):
        out = jnp.zeros((1, hc), F32)
        for m in range(1, most):
            at = chip ^ m
            out += jnp.where((at > low) & (at < high), decays[m], 0.0)
        return out

    incoming = jnp.zeros((n, hc), F32)
    for bit, got in enumerate(stages):
        fade = jnp.exp(between(-1, chip, 1 << bit))
        incoming += decode(got, n, jnp.where((chip >> bit) % 2 == 1, fade, 0.0))
    far = relay(keys_near, soft[1])

    def combine(got):
        out = 0.0
        for d, g in enumerate(got, 1):
            fade = jnp.exp(between(chip, chip ^ d, chips))
            out += decode(g, n, jnp.where((chip ^ d) > chip, fade, 0.0))
        return out

    for d, keys in enumerate(far, 1):
        flag = jnp.reshape((chip ^ d) < chip, (1,)).astype(jnp.int32)
        soft = call(
            far_kernel, carry, (flag, qs, keys, *soft),
            scratch=[pltpu.VMEM((2 * t, 2 * HD), BF16), pltpu.VMEM((HD, 2 * t), BF16)] + [pltpu.VMEM((2 * t, 2 * t), F32)] * 2,
            flops=4 * (2 * t) ** 2 * qc, alias={3: 0, 4: 1, 5: 2},
            in_specs=[pl.BlockSpec(memory_space=pltpu.SMEM)] + [VM] * 5,
        )
    res, d1, dcode = call(
        residual_kernel, [((2 * t, hc), F32), ((n, hc), F32), code],
        (ybase, soft[0], soft[2], rc, fs, incoming), flops=8 * mm,
    )
    sent = dcode.astype(F16)
    coming = [swap(sent, 2 * d) for d in range(1, chips)]
    back, gw, gr = call(
        back_kernel, [((2 * t, hc), F32), ((2 * t, n), F32), ((2 * t, n), F32)],
        (res, xc, wc, rc, clsx, crow, fs, wexpc, incoming, st0, d1),
        scratch=[pltpu.VMEM((t, t), F32), pltpu.VMEM((t, t), F32)],
        flops=16 * mm,
    )
    other_total = jnp.sum(rates[heads:], axis=1)[None, :]
    extra = jnp.where(core == 0, other_total, 0.0)
    wexp, xh, xl = call(
        ready_kernel, [((t, 2 * hc), F32), ((t, 2 * hc), BF16), ((t, 2 * hc), BF16)],
        (x, ls, ld, extra), flops=2 * mm,
    )

    def home(a):
        return half(a, core, t, 0), swap(half(a, 1 - core, t, 0), 1)

    def tp_sum(a):
        bit = 1
        while bit < tp:
            a = a + lax.ppermute(a, "tp", [(i, i ^ bit) for i in range(tp)])
            bit *= 2
        return a

    back_all = joined(*home(back), 1)
    own, other = home(jnp.concatenate([gw, gr], axis=1))
    grads = own + other
    gw0, gr0 = grads[:, :n], grads[:, n:]
    grad_read = tp_sum(gr0)
    arriving = combine(coming)
    arrived = joined(arriving, swap(arriving, 1), 1)
    (gwp,) = call(write_kernel, [((t, n), F32)], (xh, xl, arrived, gw0), flops=4 * mm)
    grad_write = tp_sum(gwp)
    gi, gls = call(
        final_kernel, [((t, 2 * hc), F32), ((heads, t), F32)], (back_all, wexp, x, wr, arrived),
        flops=8 * mm,
    )
    return (gi, grad_write, grad_read, gls)


def solution(mesh):
    in_specs = (
        P("seq", "tp"), P("seq", "tp"), P("seq", "tp"), P("seq", "tp"),
        P("seq", None), P("seq", None), P("tp", "seq"), P("tp", "seq"),
    )
    out_specs = (P("seq", "tp"), P("seq", None), P("seq", None), P("tp", "seq"))
    return jax.shard_map(
        on_device, mesh=mesh, in_specs=in_specs, out_specs=out_specs, check_vma=False
    )
```

```python
import functools
import math

import jax
import jax.numpy as jnp
from jax import lax
from jax.experimental import pallas as pl
from jax.experimental.pallas import tpu as pltpu
from jax.sharding import PartitionSpec as P


HD = 128
F32, BF16, F16 = jnp.float32, jnp.bfloat16, jnp.float16


def nn(a, b):
    return lax.dot_general(a, b, (((1,), (0,)), ((), ())), preferred_element_type=F32)


def nt(a, b):
    return lax.dot_general(a, b, (((1,), (1,)), ((), ())), preferred_element_type=F32)


def tn(a, b):
    return lax.dot_general(a, b, (((0,), (0,)), ((), ())), preferred_element_type=F32)


def split2(a):
    hi = a.astype(BF16)
    return hi, (a - hi.astype(F32)).astype(BF16)


def split3(a):
    hi = a.astype(BF16)
    rest = a - hi.astype(F32)
    mid = rest.astype(BF16)
    return hi, mid, (rest - mid.astype(F32)).astype(BF16)


def iota(shape, dim):
    return lax.broadcasted_iota(jnp.int32, shape, dim)


def lower(t):
    return (iota((t, t), 0) >= iota((t, t), 1)).astype(BF16)


def spread_matrix(heads, width, times=1):
    row = iota((times * heads, width), 0) % heads
    return (iota((times * heads, width), 1) // (width // heads) == row).astype(BF16)


def spread(col, width):
    pieces = [p.astype(F32) for p in split3(col)]
    stacked = jnp.concatenate(pieces, axis=1).astype(BF16)
    return nn(stacked, spread_matrix(col.shape[1], width, 3))


def stack2(a):
    return jnp.concatenate(split2(a), axis=0)


def twice(a):
    return jnp.concatenate([a, a], axis=1)


def nt3(a, b):
    ah, al = split2(a)
    bh, bl = split2(b)
    both = nt(ah, jnp.concatenate([bh, bl], axis=0))
    half = both.shape[1] // 2
    return both[:, :half] + both[:, half:] + nt(al, bh)


def code_rows(state, extra):
    top = jnp.max(jnp.abs(state), axis=0, keepdims=True)
    power = jnp.ceil(jnp.log2(jnp.maximum(top, 1e-30)))
    used = sum(e.shape[0] for e in extra)
    rest = jnp.zeros((15 - used, state.shape[1]), F32)
    return state * jnp.exp2(12.0 - power), jnp.concatenate([power, *extra, rest], axis=0)


def spread_row(row, width):
    return spread(jnp.broadcast_to(row, (8, row.shape[1])), width)[0:1]


def cum_col(ld):
    tri = lower(ld.shape[1])
    a, b, c = split3(ld)
    return nt(tri, a) + nt(tri, b) + nt(tri, c)


def cum_row(ld):
    tri = lower(ld.shape[1])
    a, b, c = split3(ld)
    return nt(a, tri) + nt(b, tri) + nt(c, tri)


def turn(rows):
    t = rows.shape[1]
    eye = (iota((t, t), 0) == iota((t, t), 1)).astype(BF16)
    a, b, c = split3(rows)
    return nt(eye, a) + nt(eye, b) + nt(eye, c)


def state_kernel(x_ref, w_ref, ls_ref, ld_ref, st0_ref, coded_ref, wexp_ref):
    t = x_ref.shape[0] // 2
    width = x_ref.shape[1]
    n = w_ref.shape[1]
    parts, tots = [], []
    for b in (0, 1):
        rows = slice(b * t, (b + 1) * t)
        ccol = cum_col(ld_ref[:, rows])
        tot = ccol[t - 1 : t, :]
        wexp = spread(jnp.exp(tot - ccol + turn(ls_ref[:, rows])), width)
        wexp_ref[rows, :] = wexp
        hi, lo = split2(x_ref[rows, :].astype(F32) * wexp)
        parts.append(tn(w_ref[rows, :], hi) + tn(w_ref[rows, :], lo))
        tots.append(tot)
    st0_ref[...] = parts[0]
    state = spread_row(jnp.exp(tots[1]), width) * parts[0] + parts[1]
    pieces = [p.astype(F32) for p in split3(spread_row(tots[0] + tots[1], width))]
    coded_ref[:n, :], coded_ref[n:, :] = code_rows(state, pieces)


def merge_kernel(flag, own_ref, got_ref, out_ref, *, group):
    n = own_ref.shape[0] - 16
    used = 3 * group
    own_rows = own_ref[n + 1 : n + 1 + used, :]
    got_rows = got_ref[n + 1 : n + 1 + used, :]
    own = own_ref[:n, :] * jnp.exp2(own_ref[n : n + 1, :] - 12.0)
    got = got_ref[:n, :] * jnp.exp2(got_ref[n : n + 1, :] - 12.0)
    own_fade = jnp.exp(jnp.sum(own_rows, axis=0, keepdims=True))
    got_fade = jnp.exp(jnp.sum(got_rows, axis=0, keepdims=True))
    earlier = flag[0] == 1
    merged = own * jnp.where(earlier, 1.0, got_fade) + got * jnp.where(earlier, own_fade, 1.0)
    out_ref[:n, :], out_ref[n:, :] = code_rows(merged, [own_rows, got_rows])


def local_kernel(
    x_ref, w_ref, r_ref, ls_ref, ld_ref, st0_ref,
    y_ref, fs_ref, clsx_ref, crow_ref, cexp, clsrow, a_ref,
):
    t = x_ref.shape[0] // 2
    th = t // 2
    width = x_ref.shape[1]
    heads = ls_ref.shape[0]
    hw = width // heads
    per = 128 // hw
    for b in (0, 1):
        rows = slice(b * t, (b + 1) * t)
        ccol = cum_col(ld_ref[:, rows])
        cexp[...] = spread(ccol, width)
        fs = spread(jnp.exp(ccol), width)
        fs_ref[rows, :] = fs
        clsx_ref[rows, :] = spread(ccol - turn(ls_ref[:, rows]), width)
        crow = cum_row(ld_ref[:, rows])
        crow_ref[:, rows] = crow
        clsrow[...] = crow - ls_ref[:, rows]
        keep = iota((t, t), 0) >= iota((t, t), 1)
        a_ref[...] = jnp.where(keep, nt(r_ref[rows, :], w_ref[rows, :]), 0.0)
        if b == 1:
            y_ref[rows, :] = fs * nn(twice(r_ref[rows, :]), stack2(st0_ref[...]))

        def one(i, rows=rows, b=b):
            cols = pl.ds(pl.multiple_of(i * 128, 128), 128)
            xp = x_ref[rows, cols]
            xtop = jnp.concatenate([xp[:th], xp[:th]], axis=0)
            cc = cexp[:, cols]
            lane = iota((t, 128), 1)
            out = None
            for a in range(per):
                ci = cc[:, a * hw : a * hw + 1]
                cj = clsrow[pl.ds(i * per + a, 1), :]
                top = jnp.exp(jnp.minimum(ci[:th] - cj[:, :th], 0.0)) * a_ref[:th, :th]
                bot = jnp.exp(jnp.minimum(ci[th:] - cj, 0.0)) * a_ref[th:, :]
                yt = nn(jnp.concatenate(split2(top), axis=1), xtop)
                b1, b2 = split2(bot)
                yb = nn(b1, xp) + nn(b2, xp)
                mine = jnp.concatenate([yt, yb], axis=0)
                out = mine if out is None else jnp.where(lane >= a * hw, mine, out)
            if b == 1:
                out = out + y_ref[rows, cols]
            return cols, out

        def two(i, _, rows=rows, one=one):
            done = [one(2 * i), one(2 * i + 1)]
            for cols, out in done:
                y_ref[rows, cols] = out
            return 0

        lax.fori_loop(0, width // 256, two, 0)


def keys_twice(kv_ref, g, kw):
    k = kv_ref[:, g * HD : (g + 1) * HD]
    return jnp.concatenate([k, k], axis=1), kv_ref[:, kw + g * HD : kw + (g + 1) * HD].T


def own_kernel(q_ref, kv_ref, qs_ref, acc_ref, m_ref, l_ref, k2, vt, bias, s0a, s1a, s0b, s1b):
    t = q_ref.shape[0] // 2
    kw = kv_ref.shape[1] // 2
    kvh = kw // HD
    group = q_ref.shape[1] // HD // kvh
    scale = 1.0 / math.sqrt(HD)
    bias[...] = jnp.where(iota((t, t), 0) <= iota((t, t), 1), 0.0, -1e30)
    for g in range(kvh):
        k2[...], vt[...] = keys_twice(kv_ref, g, kw)

        def scores(h, s0, s1, g=g):
            at = g * group + h
            q = q_ref[:, pl.ds(pl.multiple_of(at * HD, HD), HD)].astype(F32) * scale
            both = jnp.concatenate(split2(q), axis=1)
            qs_ref[:, pl.ds(pl.multiple_of(at * 2 * HD, 2 * HD), 2 * HD)] = both
            s0[...] = nt(k2[:t, :], both[:t]) + bias[...]
            s1[:t, :] = nt(k2[:t, :], both[t:])
            s1[t:, :] = nt(k2[t:, :], both[t:]) + bias[...]

        def soft(h, s0, s1, g=g):
            at = g * group + h
            cols = pl.ds(pl.multiple_of(at * HD, HD), HD)
            for b, s_ref in ((0, s0), (1, s1)):
                rows = slice(b * t, (b + 1) * t)
                s = s_ref[...]
                top = jnp.max(s, axis=0, keepdims=True)
                e = jnp.exp(s - top)
                m_ref[pl.ds(at, 1), rows] = top
                l_ref[pl.ds(at, 1), rows] = jnp.sum(e, axis=0, keepdims=True)
                acc_ref[cols, rows] = nn(vt[:, : (b + 1) * t], e.astype(BF16))

        scores(0, s0a, s1a)

        def pair(i, _):
            scores(2 * i + 1, s0b, s1b)
            soft(2 * i, s0a, s1a)
            scores(jnp.minimum(2 * i + 2, group - 1), s0a, s1a)
            soft(2 * i + 1, s0b, s1b)
            return 0

        lax.fori_loop(0, group // 2, pair, 0)


def far_kernel(flag, qs_ref, kv_ref, acc_in, m_in, l_in, acc_ref, m_ref, l_ref, k2, vt, sa, sb):
    t = qs_ref.shape[0] // 2
    kw = kv_ref.shape[1] // 2
    kvh = kw // HD
    group = qs_ref.shape[1] // (2 * HD) // kvh

    @pl.when(flag[0] == 0)
    def _():
        acc_ref[...] = acc_in[...]
        m_ref[...] = m_in[...]
        l_ref[...] = l_in[...]

    @pl.when(flag[0] == 1)
    def _():
        for g in range(kvh):
            k2[...], vt[...] = keys_twice(kv_ref, g, kw)

            def scores(h, s_ref, g=g):
                at = g * group + h
                s_ref[...] = nt(k2[...], qs_ref[:, pl.ds(pl.multiple_of(at * 2 * HD, 2 * HD), 2 * HD)])

            def soft(h, s_ref, g=g):
                at = g * group + h
                cols = pl.ds(pl.multiple_of(at * HD, HD), HD)
                row = pl.ds(at, 1)
                for b in (0, 1):
                    rows = slice(b * t, (b + 1) * t)
                    s = s_ref[:, rows]
                    old = m_in[row, rows]
                    new = jnp.maximum(old, jnp.max(s, axis=0, keepdims=True))
                    e = jnp.exp(s - new)
                    fade = jnp.exp(old - new)
                    m_ref[row, rows] = new
                    l_ref[row, rows] = l_in[row, rows] * fade + jnp.sum(e, axis=0, keepdims=True)
                    acc_ref[cols, rows] = acc_in[cols, rows] * fade + nn(vt[...], e.astype(BF16))

            scores(0, sa)

            def pair(i, _):
                scores(2 * i + 1, sb)
                soft(2 * i, sa)
                scores(jnp.minimum(2 * i + 2, group - 1), sa)
                soft(2 * i + 1, sb)
                return 0

            lax.fori_loop(0, group // 2, pair, 0)


def residual_kernel(y_ref, acc_ref, l_ref, r_ref, fs_ref, sin_ref, res_ref, d1_ref, coded_ref):
    t = y_ref.shape[0] // 2
    width = y_ref.shape[1]
    n = r_ref.shape[1]
    state = sin_ref[...]
    first = fs_ref[t - 1 : t, :]
    parts = []
    for b in (0, 1):
        rows = slice(b * t, (b + 1) * t)
        fs = fs_ref[rows, :]
        r = r_ref[rows, :]
        heads = [
            (acc_ref[h * HD : (h + 1) * HD, rows] / l_ref[h : h + 1, rows]).astype(BF16).T
            for h in range(width // HD)
        ]
        teach = jnp.concatenate(heads, axis=1).astype(F32)
        res = y_ref[rows, :] + fs * nn(twice(r), stack2(state * first if b else state)) - teach
        res_ref[rows, :] = res
        hi, lo = split2(res * fs)
        parts.append(tn(r, hi) + tn(r, lo))
    d1_ref[...] = parts[1]
    coded_ref[:n, :], coded_ref[n:, :] = code_rows(parts[0] + first * parts[1], [])


def back_kernel(
    res_ref, x_ref, w_ref, r_ref, clsx_ref, crow_ref, fs_ref, wexp_ref, sin_ref, st0_ref, d1_ref,
    back_ref, gw_ref, gr_ref, a_ref, pair,
):
    t = x_ref.shape[0] // 2
    th = t // 2
    width = x_ref.shape[1]
    heads = crow_ref.shape[0]
    hw = width // heads
    per = 128 // hw
    first = fs_ref[t - 1 : t, :]
    for b in (0, 1):
        rows = slice(b * t, (b + 1) * t)
        keep = iota((t, t), 1) >= iota((t, t), 0)
        w = w_ref[rows, :]
        r = r_ref[rows, :]
        a_ref[...] = jnp.where(keep, nt(w, r), 0.0)
        pair[...] = jnp.zeros_like(pair)
        if b == 0:
            d1 = d1_ref[...]
            wexp = wexp_ref[rows, :]
            back_ref[rows, :] = wexp * nn(twice(w), stack2(d1))
            gw = nt3(x_ref[rows, :].astype(F32) * wexp, d1)
            state = sin_ref[...]
        else:
            gw = None
            state = first * sin_ref[...] + st0_ref[...]
        gr = nt3(res_ref[rows, :] * fs_ref[rows, :], state)

        def one(i, rows=rows, b=b):
            cols = pl.ds(pl.multiple_of(i * 128, 128), 128)
            xp = x_ref[rows, cols]
            rh, rl = split2(res_ref[rows, cols])
            both = jnp.concatenate([rh, rl], axis=1)
            cc = clsx_ref[rows, cols]
            lane = iota((t, 128), 1)
            out, above, below = None, 0.0, 0.0
            for a in range(per):
                cj = cc[:, a * hw : a * hw + 1]
                ci = crow_ref[pl.ds(i * per + a, 1), rows]
                xx = twice(jnp.where((lane // hw) == a, xp, jnp.zeros_like(xp)))
                e1 = jnp.exp(jnp.minimum(ci - cj[:th], 0.0))
                e2 = jnp.exp(jnp.minimum(ci[:, th:] - cj[th:], 0.0))
                h1, l1 = split2(e1 * a_ref[:th, :])
                h2, l2 = split2(e2 * a_ref[th:, th:])
                p1 = nn(h1, both)
                p2 = nn(h2, both[th:])
                u1 = p1[:, :128] + p1[:, 128:] + nn(l1, rh)
                u2 = p2[:, :128] + p2[:, 128:] + nn(l2, rh[th:])
                u = jnp.concatenate([u1, u2], axis=0)
                out = u if out is None else jnp.where(lane >= a * hw, u, out)
                above += e1 * nt(xx[:th], both)
                below += e2 * nt(xx[th:], both[th:])
            if b == 0:
                out = out + back_ref[rows, cols]
            return cols, out, above, below

        def two(i, _, rows=rows, one=one):
            done = [one(2 * i), one(2 * i + 1)]
            for cols, out, _, _ in done:
                back_ref[rows, cols] = out
            pair[:th, :] += done[0][2] + done[1][2]
            pair[th:, th:] += done[0][3] + done[1][3]
            return 0

        lax.fori_loop(0, width // 256, two, 0)
        ph, plo = split2(jnp.where(keep, pair[...], 0.0))
        gr_ref[rows, :] = gr + tn(ph, w) + tn(plo, w)
        mixed = nn(ph, r) + nn(plo, r)
        gw_ref[rows, :] = mixed if gw is None else mixed + gw


def ready_kernel(x_ref, ls_ref, ld_ref, extra_ref, wexp_ref, xh_ref, xl_ref):
    t = x_ref.shape[0]
    ccol = cum_col(ld_ref[...])
    wexp = spread(
        jnp.exp(ccol[t - 1 : t, :] + extra_ref[...] - ccol + turn(ls_ref[...])), x_ref.shape[1]
    )
    wexp_ref[...] = wexp
    xh_ref[...], xl_ref[...] = split2(x_ref[...].astype(F32) * wexp)


def write_kernel(xh_ref, xl_ref, g_ref, gw0_ref, gw_ref):
    gh, gl = split2(g_ref[...])
    n = gh.shape[0]
    both = nt(xh_ref[...], jnp.concatenate([gh, gl], axis=0))
    gw_ref[...] = gw0_ref[...] + both[:, :n] + both[:, n:] + nt(xl_ref[...], gh)


def final_kernel(back_ref, wexp_ref, x_ref, w_ref, g_ref, gi_ref, gls_ref):
    width = x_ref.shape[1]
    heads = gls_ref.shape[0]
    out = back_ref[...] + wexp_ref[...] * nn(twice(w_ref[...]), stack2(g_ref[...]))
    gi_ref[...] = out
    ph, plo = split2(x_ref[...].astype(F32) * out)
    mat = spread_matrix(heads, width)
    gls_ref[...] = nt(mat, ph) + nt(mat, plo)


VM = pl.BlockSpec(memory_space=pltpu.VMEM)


def call(kernel, outs, args, scratch=(), flops=0, in_specs=None, alias=None):
    shapes = [jax.ShapeDtypeStruct(s, d) for s, d in outs]
    moved = sum(a.size * a.dtype.itemsize for a in args)
    return pl.pallas_call(
        kernel,
        out_shape=shapes,
        in_specs=in_specs or [VM] * len(args),
        out_specs=[VM] * len(shapes),
        scratch_shapes=list(scratch),
        input_output_aliases=alias or {},
        cost_estimate=pl.CostEstimate(flops=flops, bytes_accessed=moved, transcendentals=0),
        compiler_params=pltpu.CompilerParams(vmem_limit_bytes=8 * 2**20),
    )(*args)


def decode(coded, rows, weight):
    power = coded[rows : rows + 1].astype(F32)
    return coded[:rows].astype(F32) * (jnp.exp2(power - 12.0) * weight)


def on_device(q, k, v, x, wr, rd, ls, ld):
    t = q.shape[0]
    count = lax.axis_size("seq")
    tp = lax.axis_size("tp")
    chips = count // 2
    index = lax.axis_index("seq")
    core, chip = index % 2, index // 2
    heads = ls.shape[0]
    hh = heads // 2
    n = wr.shape[1]
    hc = x.shape[1] // 2
    qc = q.shape[1] // 2
    kvh = k.shape[1] // HD
    kw = k.shape[1] // 2 if kvh % 2 == 0 else k.shape[1]

    def swap(a, bits):
        return lax.ppermute(a, "seq", [(i, i ^ bits) for i in range(count)])

    def half(a, which, width, axis=1):
        return lax.dynamic_slice_in_dim(a, which * width, width, axis=axis)

    def joined(own, other, axis=0):
        a = jnp.where(core == 0, own, other)
        b = jnp.where(core == 0, other, own)
        return jnp.concatenate([a, b], axis=axis)

    def near(a):
        got = {}
        for b in range(chips.bit_length() - 1):
            got[1 << b] = swap(a, 2 << b)
        return got

    def relay(got, token):
        got = dict(got)
        for d in range(1, chips):
            if d not in got:
                low = d & -d
                held, _ = lax.optimization_barrier((got[d - low], token))
                need = [c for c in range(chips) if c ^ d < c or c ^ low ^ d < c ^ low]
                pairs = [(2 * c + k, 2 * (c ^ low) + k) for c in need for k in (0, 1)]
                got[d] = lax.ppermute(held, "seq", pairs)
        return [got[d] for d in range(1, chips)]

    def kv_half(which):
        if kvh % 2 == 0:
            return jnp.concatenate([half(k, which, kw), half(v, which, kw)], axis=1)
        return jnp.concatenate([k, v], axis=1)

    kv = joined(kv_half(core), swap(kv_half(1 - core), 1))
    keys_near = near(kv)
    x1, q1, wr1, rd1, _ = lax.optimization_barrier((x, q, wr, rd, kv))
    rates = swap(jnp.concatenate([ls, ld], axis=0), 1)
    lsc = joined(half(ls, core, hh, 0), half(rates, core, hh, 0), 1)
    ldc = joined(half(ld, core, hh, 0), half(rates[heads:], core, hh, 0), 1)
    mates = swap(jnp.concatenate([half(x1, 1 - core, hc), wr1, rd1], axis=1), 1)
    xc = joined(half(x1, core, hc), mates[:, :hc])
    wc = joined(wr1, mates[:, hc : hc + n])
    rc = joined(rd1, mates[:, hc + n :])
    qg = joined(half(q1, core, qc), swap(half(q1, 1 - core, qc), 1))

    mm = 2 * 2 * t * hc * n
    code = ((n + 16, hc), F32)
    st0, coded, wexpc = call(
        state_kernel, [((n, hc), F32), code, ((2 * t, hc), F32)], (xc, wc, lsc, ldc),
        flops=4 * mm,
    )

    def state_stage(coded, bit):
        return swap(coded.astype(F16), 2 << bit).astype(F32)

    stages = [state_stage(coded, 0)] if chips > 1 else []
    qh = qc // HD
    carry = [((qc, 2 * t), F32), ((qh, 2 * t), F32), ((qh, 2 * t), F32)]
    qs, *soft = call(
        own_kernel, [((2 * t, 2 * qc), BF16), *carry], (qg, kv),
        scratch=[pltpu.VMEM((2 * t, 2 * HD), BF16), pltpu.VMEM((HD, 2 * t), BF16), pltpu.VMEM((t, t), F32)]
        + [pltpu.VMEM((t, t), F32), pltpu.VMEM((2 * t, t), F32)] * 2,
        flops=4 * (2 * t) ** 2 * qc,
    )
    ybase, fs, clsx, crow = call(
        local_kernel,
        [((2 * t, hc), F32), ((2 * t, hc), F32), ((2 * t, hc), F32), ((hh, 2 * t), F32)],
        (xc, wc, rc, lsc, ldc, st0),
        scratch=[pltpu.VMEM((t, hc), F32), pltpu.VMEM((hh, t), F32), pltpu.VMEM((t, t), F32)],
        flops=8 * mm,
    )
    for bit in range(1, chips.bit_length() - 1):
        flag = jnp.reshape((chip >> (bit - 1)) % 2, (1,)).astype(jnp.int32)
        (coded,) = call(
            functools.partial(merge_kernel, group=1 << (bit - 1)), [code], (flag, coded, stages[-1]),
            in_specs=[pl.BlockSpec(memory_space=pltpu.SMEM), VM, VM],
        )
        stages.append(state_stage(coded, bit))
    decays = {}
    for bit, got in enumerate(stages):
        for m in range(1 << bit):
            at = n + 1 + 3 * m
            decays[(1 << bit) + m] = jnp.sum(got[at : at + 3], axis=0, keepdims=True)

    def between(low, high, most):
        out = jnp.zeros((1, hc), F32)
        for m in range(1, most):
            at = chip ^ m
            out += jnp.where((at > low) & (at < high), decays[m], 0.0)
        return out

    incoming = jnp.zeros((n, hc), F32)
    for bit, got in enumerate(stages):
        fade = jnp.exp(between(-1, chip, 1 << bit))
        incoming += decode(got, n, jnp.where((chip >> bit) % 2 == 1, fade, 0.0))
    far = relay(keys_near, soft[1])

    def combine(got):
        out = 0.0
        for d, g in enumerate(got, 1):
            fade = jnp.exp(between(chip, chip ^ d, chips))
            out += decode(g, n, jnp.where((chip ^ d) > chip, fade, 0.0))
        return out

    for d, keys in enumerate(far, 1):
        flag = jnp.reshape((chip ^ d) < chip, (1,)).astype(jnp.int32)
        soft = call(
            far_kernel, carry, (flag, qs, keys, *soft),
            scratch=[pltpu.VMEM((2 * t, 2 * HD), BF16), pltpu.VMEM((HD, 2 * t), BF16)] + [pltpu.VMEM((2 * t, 2 * t), F32)] * 2,
            flops=4 * (2 * t) ** 2 * qc, alias={3: 0, 4: 1, 5: 2},
            in_specs=[pl.BlockSpec(memory_space=pltpu.SMEM)] + [VM] * 5,
        )
    res, d1, dcode = call(
        residual_kernel, [((2 * t, hc), F32), ((n, hc), F32), code],
        (ybase, soft[0], soft[2], rc, fs, incoming), flops=8 * mm,
    )
    sent = dcode.astype(F16)
    coming = [swap(sent, 2 * d) for d in range(1, chips)]
    back, gw, gr = call(
        back_kernel, [((2 * t, hc), F32), ((2 * t, n), F32), ((2 * t, n), F32)],
        (res, xc, wc, rc, clsx, crow, fs, wexpc, incoming, st0, d1),
        scratch=[pltpu.VMEM((t, t), F32), pltpu.VMEM((t, t), F32)],
        flops=16 * mm,
    )
    other_total = jnp.sum(rates[heads:], axis=1)[None, :]
    extra = jnp.where(core == 0, other_total, 0.0)
    wexp, xh, xl = call(
        ready_kernel, [((t, 2 * hc), F32), ((t, 2 * hc), BF16), ((t, 2 * hc), BF16)],
        (x, ls, ld, extra), flops=2 * mm,
    )

    def home(a):
        return half(a, core, t, 0), swap(half(a, 1 - core, t, 0), 1)

    def tp_sum(a):
        bit = 1
        while bit < tp:
            a = a + lax.ppermute(a, "tp", [(i, i ^ bit) for i in range(tp)])
            bit *= 2
        return a

    back_all = joined(*home(back), 1)
    own, other = home(jnp.concatenate([gw, gr], axis=1))
    grads = own + other
    gw0, gr0 = grads[:, :n], grads[:, n:]
    grad_read = tp_sum(gr0)
    arriving = combine(coming)
    arrived = joined(arriving, swap(arriving, 1), 1)
    (gwp,) = call(write_kernel, [((t, n), F32)], (xh, xl, arrived, gw0), flops=4 * mm)
    grad_write = tp_sum(gwp)
    gi, gls = call(
        final_kernel, [((t, 2 * hc), F32), ((heads, t), F32)], (back_all, wexp, x, wr, arrived),
        flops=8 * mm,
    )
    return (gi, grad_write, grad_read, gls)


def solution(mesh):
    in_specs = (
        P("seq", "tp"), P("seq", "tp"), P("seq", "tp"), P("seq", "tp"),
        P("seq", None), P("seq", None), P("tp", "seq"), P("tp", "seq"),
    )
    out_specs = (P("seq", "tp"), P("seq", None), P("seq", None), P("tp", "seq"))
    return jax.shard_map(
        on_device, mesh=mesh, in_specs=in_specs, out_specs=out_specs, check_vma=False
    )
```

```python
import functools
import math

import jax
import jax.numpy as jnp
from jax import lax
from jax.experimental import pallas as pl
from jax.experimental.pallas import tpu as pltpu
from jax.sharding import PartitionSpec as P


HD = 128
F32, BF16, F16 = jnp.float32, jnp.bfloat16, jnp.float16


def nn(a, b):
    return lax.dot_general(a, b, (((1,), (0,)), ((), ())), preferred_element_type=F32)


def nt(a, b):
    return lax.dot_general(a, b, (((1,), (1,)), ((), ())), preferred_element_type=F32)


def tn(a, b):
    return lax.dot_general(a, b, (((0,), (0,)), ((), ())), preferred_element_type=F32)


def split2(a):
    hi = a.astype(BF16)
    return hi, (a - hi.astype(F32)).astype(BF16)


def split3(a):
    hi = a.astype(BF16)
    rest = a - hi.astype(F32)
    mid = rest.astype(BF16)
    return hi, mid, (rest - mid.astype(F32)).astype(BF16)


def iota(shape, dim):
    return lax.broadcasted_iota(jnp.int32, shape, dim)


def lower(t):
    return (iota((t, t), 0) >= iota((t, t), 1)).astype(BF16)


def spread_matrix(heads, width, times=1):
    row = iota((times * heads, width), 0) % heads
    return (iota((times * heads, width), 1) // (width // heads) == row).astype(BF16)


def spread(col, width):
    pieces = [p.astype(F32) for p in split3(col)]
    stacked = jnp.concatenate(pieces, axis=1).astype(BF16)
    return nn(stacked, spread_matrix(col.shape[1], width, 3))


def stack2(a):
    return jnp.concatenate(split2(a), axis=0)


def twice(a):
    return jnp.concatenate([a, a], axis=1)


def nt3(a, b):
    ah, al = split2(a)
    bh, bl = split2(b)
    both = nt(ah, jnp.concatenate([bh, bl], axis=0))
    half = both.shape[1] // 2
    return both[:, :half] + both[:, half:] + nt(al, bh)


def code_rows(state, extra):
    top = jnp.max(jnp.abs(state), axis=0, keepdims=True)
    power = jnp.ceil(jnp.log2(jnp.maximum(top, 1e-30)))
    used = sum(e.shape[0] for e in extra)
    rest = jnp.zeros((15 - used, state.shape[1]), F32)
    return state * jnp.exp2(12.0 - power), jnp.concatenate([power, *extra, rest], axis=0)


def spread_row(row, width):
    return spread(jnp.broadcast_to(row, (8, row.shape[1])), width)[0:1]


def cum_col(ld):
    tri = lower(ld.shape[1])
    a, b, c = split3(ld)
    return nt(tri, a) + nt(tri, b) + nt(tri, c)


def cum_row(ld):
    tri = lower(ld.shape[1])
    a, b, c = split3(ld)
    return nt(a, tri) + nt(b, tri) + nt(c, tri)


def turn(rows):
    t = rows.shape[1]
    eye = (iota((t, t), 0) == iota((t, t), 1)).astype(BF16)
    a, b, c = split3(rows)
    return nt(eye, a) + nt(eye, b) + nt(eye, c)


def state_kernel(x_ref, w_ref, ls_ref, ld_ref, st0_ref, coded_ref, wexp_ref):
    t = x_ref.shape[0] // 2
    width = x_ref.shape[1]
    n = w_ref.shape[1]
    parts, tots = [], []
    for b in (0, 1):
        rows = slice(b * t, (b + 1) * t)
        ccol = cum_col(ld_ref[:, rows])
        tot = ccol[t - 1 : t, :]
        wexp = spread(jnp.exp(tot - ccol + turn(ls_ref[:, rows])), width)
        wexp_ref[rows, :] = wexp
        hi, lo = split2(x_ref[rows, :].astype(F32) * wexp)
        parts.append(tn(w_ref[rows, :], hi) + tn(w_ref[rows, :], lo))
        tots.append(tot)
    st0_ref[...] = parts[0]
    state = spread_row(jnp.exp(tots[1]), width) * parts[0] + parts[1]
    pieces = [p.astype(F32) for p in split3(spread_row(tots[0] + tots[1], width))]
    coded_ref[:n, :], coded_ref[n:, :] = code_rows(state, pieces)


def merge_kernel(flag, own_ref, got_ref, out_ref, *, group):
    n = own_ref.shape[0] - 16
    used = 3 * group
    own_rows = own_ref[n + 1 : n + 1 + used, :]
    got_rows = got_ref[n + 1 : n + 1 + used, :]
    own = own_ref[:n, :] * jnp.exp2(own_ref[n : n + 1, :] - 12.0)
    got = got_ref[:n, :] * jnp.exp2(got_ref[n : n + 1, :] - 12.0)
    own_fade = jnp.exp(jnp.sum(own_rows, axis=0, keepdims=True))
    got_fade = jnp.exp(jnp.sum(got_rows, axis=0, keepdims=True))
    earlier = flag[0] == 1
    merged = own * jnp.where(earlier, 1.0, got_fade) + got * jnp.where(earlier, own_fade, 1.0)
    out_ref[:n, :], out_ref[n:, :] = code_rows(merged, [own_rows, got_rows])


def local_kernel(
    x_ref, w_ref, r_ref, ls_ref, ld_ref, st0_ref,
    y_ref, fs_ref, clsx_ref, crow_ref, cexp, clsrow, a_ref,
):
    t = x_ref.shape[0] // 2
    th = t // 2
    width = x_ref.shape[1]
    heads = ls_ref.shape[0]
    hw = width // heads
    per = 128 // hw
    for b in (0, 1):
        rows = slice(b * t, (b + 1) * t)
        ccol = cum_col(ld_ref[:, rows])
        cexp[...] = spread(ccol, width)
        fs = spread(jnp.exp(ccol), width)
        fs_ref[rows, :] = fs
        clsx_ref[rows, :] = spread(ccol - turn(ls_ref[:, rows]), width)
        crow = cum_row(ld_ref[:, rows])
        crow_ref[:, rows] = crow
        clsrow[...] = crow - ls_ref[:, rows]
        keep = iota((t, t), 0) >= iota((t, t), 1)
        a_ref[...] = jnp.where(keep, nt(r_ref[rows, :], w_ref[rows, :]), 0.0)
        if b == 1:
            y_ref[rows, :] = fs * nn(twice(r_ref[rows, :]), stack2(st0_ref[...]))

        def one(i, rows=rows, b=b):
            cols = pl.ds(pl.multiple_of(i * 128, 128), 128)
            xp = x_ref[rows, cols]
            xtop = jnp.concatenate([xp[:th], xp[:th]], axis=0)
            cc = cexp[:, cols]
            lane = iota((t, 128), 1)
            out = None
            for a in range(per):
                ci = cc[:, a * hw : a * hw + 1]
                cj = clsrow[pl.ds(i * per + a, 1), :]
                top = jnp.exp(jnp.minimum(ci[:th] - cj[:, :th], 0.0)) * a_ref[:th, :th]
                bot = jnp.exp(jnp.minimum(ci[th:] - cj, 0.0)) * a_ref[th:, :]
                yt = nn(jnp.concatenate(split2(top), axis=1), xtop)
                b1, b2 = split2(bot)
                yb = nn(b1, xp) + nn(b2, xp)
                mine = jnp.concatenate([yt, yb], axis=0)
                out = mine if out is None else jnp.where(lane >= a * hw, mine, out)
            if b == 1:
                out = out + y_ref[rows, cols]
            return cols, out

        def two(i, _, rows=rows, one=one):
            done = [one(2 * i), one(2 * i + 1)]
            for cols, out in done:
                y_ref[rows, cols] = out
            return 0

        lax.fori_loop(0, width // 256, two, 0)


def keys_twice(kv_ref, g, kw):
    k = kv_ref[:, g * HD : (g + 1) * HD]
    return jnp.concatenate([k, k], axis=1), kv_ref[:, kw + g * HD : kw + (g + 1) * HD].T


def own_kernel(q_ref, kv_ref, qs_ref, acc_ref, m_ref, l_ref, k2, vt, bias, s0a, s1a, s0b, s1b):
    t = q_ref.shape[0] // 2
    kw = kv_ref.shape[1] // 2
    kvh = kw // HD
    group = q_ref.shape[1] // HD // kvh
    scale = 1.0 / math.sqrt(HD)
    bias[...] = jnp.where(iota((t, t), 0) <= iota((t, t), 1), 0.0, -1e30)
    for g in range(kvh):
        k2[...], vt[...] = keys_twice(kv_ref, g, kw)

        def scores(h, s0, s1, g=g):
            at = g * group + h
            q = q_ref[:, pl.ds(pl.multiple_of(at * HD, HD), HD)].astype(F32) * scale
            both = jnp.concatenate(split2(q), axis=1)
            qs_ref[:, pl.ds(pl.multiple_of(at * 2 * HD, 2 * HD), 2 * HD)] = both
            s0[...] = nt(k2[:t, :], both[:t]) + bias[...]
            s1[:t, :] = nt(k2[:t, :], both[t:])
            s1[t:, :] = nt(k2[t:, :], both[t:]) + bias[...]

        def soft(h, s0, s1, g=g):
            at = g * group + h
            cols = pl.ds(pl.multiple_of(at * HD, HD), HD)
            for b, s_ref in ((0, s0), (1, s1)):
                rows = slice(b * t, (b + 1) * t)
                s = s_ref[...]
                top = jnp.max(s, axis=0, keepdims=True)
                e = jnp.exp(s - top)
                m_ref[pl.ds(at, 1), rows] = top
                l_ref[pl.ds(at, 1), rows] = jnp.sum(e, axis=0, keepdims=True)
                acc_ref[cols, rows] = nn(vt[:, : (b + 1) * t], e.astype(BF16))

        scores(0, s0a, s1a)

        def pair(i, _):
            scores(2 * i + 1, s0b, s1b)
            soft(2 * i, s0a, s1a)
            scores(jnp.minimum(2 * i + 2, group - 1), s0a, s1a)
            soft(2 * i + 1, s0b, s1b)
            return 0

        lax.fori_loop(0, group // 2, pair, 0)


def far_kernel(flag, qs_ref, kv_ref, acc_in, m_in, l_in, acc_ref, m_ref, l_ref, k2, vt, sa, sb):
    t = qs_ref.shape[0] // 2
    kw = kv_ref.shape[1] // 2
    kvh = kw // HD
    group = qs_ref.shape[1] // (2 * HD) // kvh

    @pl.when(flag[0] == 0)
    def _():
        acc_ref[...] = acc_in[...]
        m_ref[...] = m_in[...]
        l_ref[...] = l_in[...]

    @pl.when(flag[0] == 1)
    def _():
        for g in range(kvh):
            k2[...], vt[...] = keys_twice(kv_ref, g, kw)

            def scores(h, s_ref, g=g):
                at = g * group + h
                s_ref[...] = nt(k2[...], qs_ref[:, pl.ds(pl.multiple_of(at * 2 * HD, 2 * HD), 2 * HD)])

            def soft(h, s_ref, g=g):
                at = g * group + h
                cols = pl.ds(pl.multiple_of(at * HD, HD), HD)
                row = pl.ds(at, 1)
                for b in (0, 1):
                    rows = slice(b * t, (b + 1) * t)
                    s = s_ref[:, rows]
                    old = m_in[row, rows]
                    new = jnp.maximum(old, jnp.max(s, axis=0, keepdims=True))
                    e = jnp.exp(s - new)
                    fade = jnp.exp(old - new)
                    m_ref[row, rows] = new
                    l_ref[row, rows] = l_in[row, rows] * fade + jnp.sum(e, axis=0, keepdims=True)
                    acc_ref[cols, rows] = acc_in[cols, rows] * fade + nn(vt[...], e.astype(BF16))

            scores(0, sa)

            def pair(i, _):
                scores(2 * i + 1, sb)
                soft(2 * i, sa)
                scores(jnp.minimum(2 * i + 2, group - 1), sa)
                soft(2 * i + 1, sb)
                return 0

            lax.fori_loop(0, group // 2, pair, 0)


def residual_kernel(y_ref, acc_ref, l_ref, r_ref, fs_ref, sin_ref, res_ref, d1_ref, coded_ref):
    t = y_ref.shape[0] // 2
    width = y_ref.shape[1]
    n = r_ref.shape[1]
    state = sin_ref[...]
    first = fs_ref[t - 1 : t, :]
    parts = []
    for b in (0, 1):
        rows = slice(b * t, (b + 1) * t)
        fs = fs_ref[rows, :]
        r = r_ref[rows, :]
        heads = [
            (acc_ref[h * HD : (h + 1) * HD, rows] / l_ref[h : h + 1, rows]).astype(BF16).T
            for h in range(width // HD)
        ]
        teach = jnp.concatenate(heads, axis=1).astype(F32)
        res = y_ref[rows, :] + fs * nn(twice(r), stack2(state * first if b else state)) - teach
        res_ref[rows, :] = res
        hi, lo = split2(res * fs)
        parts.append(tn(r, hi) + tn(r, lo))
    d1_ref[...] = parts[1]
    coded_ref[:n, :], coded_ref[n:, :] = code_rows(parts[0] + first * parts[1], [])


def back_kernel(
    res_ref, x_ref, w_ref, r_ref, clsx_ref, crow_ref, fs_ref, wexp_ref, sin_ref, st0_ref, d1_ref,
    back_ref, gw_ref, gr_ref, a_ref, pair,
):
    t = x_ref.shape[0] // 2
    th = t // 2
    width = x_ref.shape[1]
    heads = crow_ref.shape[0]
    hw = width // heads
    per = 128 // hw
    first = fs_ref[t - 1 : t, :]
    for b in (0, 1):
        rows = slice(b * t, (b + 1) * t)
        keep = iota((t, t), 1) >= iota((t, t), 0)
        w = w_ref[rows, :]
        r = r_ref[rows, :]
        a_ref[...] = jnp.where(keep, nt(w, r), 0.0)
        pair[...] = jnp.zeros_like(pair)
        if b == 0:
            d1 = d1_ref[...]
            wexp = wexp_ref[rows, :]
            back_ref[rows, :] = wexp * nn(twice(w), stack2(d1))
            gw = nt3(x_ref[rows, :].astype(F32) * wexp, d1)
            state = sin_ref[...]
        else:
            gw = None
            state = first * sin_ref[...] + st0_ref[...]
        gr = nt3(res_ref[rows, :] * fs_ref[rows, :], state)

        def one(i, rows=rows, b=b):
            cols = pl.ds(pl.multiple_of(i * 128, 128), 128)
            xp = x_ref[rows, cols]
            rh, rl = split2(res_ref[rows, cols])
            both = jnp.concatenate([rh, rl], axis=1)
            cc = clsx_ref[rows, cols]
            lane = iota((t, 128), 1)
            out, above, below = None, 0.0, 0.0
            for a in range(per):
                cj = cc[:, a * hw : a * hw + 1]
                ci = crow_ref[pl.ds(i * per + a, 1), rows]
                xx = twice(jnp.where((lane // hw) == a, xp, jnp.zeros_like(xp)))
                e1 = jnp.exp(jnp.minimum(ci - cj[:th], 0.0))
                e2 = jnp.exp(jnp.minimum(ci[:, th:] - cj[th:], 0.0))
                h1, l1 = split2(e1 * a_ref[:th, :])
                h2, l2 = split2(e2 * a_ref[th:, th:])
                p1 = nn(h1, both)
                p2 = nn(h2, both[th:])
                u1 = p1[:, :128] + p1[:, 128:] + nn(l1, rh)
                u2 = p2[:, :128] + p2[:, 128:] + nn(l2, rh[th:])
                u = jnp.concatenate([u1, u2], axis=0)
                out = u if out is None else jnp.where(lane >= a * hw, u, out)
                above += e1 * nt(xx[:th], both)
                below += e2 * nt(xx[th:], both[th:])
            if b == 0:
                out = out + back_ref[rows, cols]
            return cols, out, above, below

        def two(i, _, rows=rows, one=one):
            done = [one(2 * i), one(2 * i + 1)]
            for cols, out, _, _ in done:
                back_ref[rows, cols] = out
            pair[:th, :] += done[0][2] + done[1][2]
            pair[th:, th:] += done[0][3] + done[1][3]
            return 0

        lax.fori_loop(0, width // 256, two, 0)
        ph, plo = split2(jnp.where(keep, pair[...], 0.0))
        gr_ref[rows, :] = gr + tn(ph, w) + tn(plo, w)
        mixed = nn(ph, r) + nn(plo, r)
        gw_ref[rows, :] = mixed if gw is None else mixed + gw


def ready_kernel(x_ref, ls_ref, ld_ref, extra_ref, wexp_ref, xh_ref, xl_ref):
    t = x_ref.shape[0]
    ccol = cum_col(ld_ref[...])
    wexp = spread(
        jnp.exp(ccol[t - 1 : t, :] + extra_ref[...] - ccol + turn(ls_ref[...])), x_ref.shape[1]
    )
    wexp_ref[...] = wexp
    xh_ref[...], xl_ref[...] = split2(x_ref[...].astype(F32) * wexp)


def write_kernel(xh_ref, xl_ref, g_ref, gw0_ref, gw_ref):
    gh, gl = split2(g_ref[...])
    n = gh.shape[0]
    both = nt(xh_ref[...], jnp.concatenate([gh, gl], axis=0))
    gw_ref[...] = gw0_ref[...] + both[:, :n] + both[:, n:] + nt(xl_ref[...], gh)


def final_kernel(back_ref, wexp_ref, x_ref, w_ref, g_ref, gi_ref, gls_ref):
    width = x_ref.shape[1]
    heads = gls_ref.shape[0]
    out = back_ref[...] + wexp_ref[...] * nn(twice(w_ref[...]), stack2(g_ref[...]))
    gi_ref[...] = out
    ph, plo = split2(x_ref[...].astype(F32) * out)
    mat = spread_matrix(heads, width)
    gls_ref[...] = nt(mat, ph) + nt(mat, plo)


VM = pl.BlockSpec(memory_space=pltpu.VMEM)


def call(kernel, outs, args, scratch=(), flops=0, in_specs=None, alias=None):
    shapes = [jax.ShapeDtypeStruct(s, d) for s, d in outs]
    moved = sum(a.size * a.dtype.itemsize for a in args)
    return pl.pallas_call(
        kernel,
        out_shape=shapes,
        in_specs=in_specs or [VM] * len(args),
        out_specs=[VM] * len(shapes),
        scratch_shapes=list(scratch),
        input_output_aliases=alias or {},
        cost_estimate=pl.CostEstimate(flops=flops, bytes_accessed=moved, transcendentals=0),
        compiler_params=pltpu.CompilerParams(vmem_limit_bytes=8 * 2**20),
    )(*args)


def decode(coded, rows, weight):
    power = coded[rows : rows + 1].astype(F32)
    return coded[:rows].astype(F32) * (jnp.exp2(power - 12.0) * weight)


def on_device(q, k, v, x, wr, rd, ls, ld):
    t = q.shape[0]
    count = lax.axis_size("seq")
    tp = lax.axis_size("tp")
    chips = count // 2
    index = lax.axis_index("seq")
    core, chip = index % 2, index // 2
    heads = ls.shape[0]
    hh = heads // 2
    n = wr.shape[1]
    hc = x.shape[1] // 2
    qc = q.shape[1] // 2
    kvh = k.shape[1] // HD
    kw = k.shape[1] // 2 if kvh % 2 == 0 else k.shape[1]

    def swap(a, bits):
        return lax.ppermute(a, "seq", [(i, i ^ bits) for i in range(count)])

    def half(a, which, width, axis=1):
        return lax.dynamic_slice_in_dim(a, which * width, width, axis=axis)

    def joined(own, other, axis=0):
        a = jnp.where(core == 0, own, other)
        b = jnp.where(core == 0, other, own)
        return jnp.concatenate([a, b], axis=axis)

    def near(a):
        got = {}
        for b in range(chips.bit_length() - 1):
            got[1 << b] = swap(a, 2 << b)
        return got

    def relay(got, token):
        got = dict(got)
        for d in range(1, chips):
            if d not in got:
                low = d & -d
                held, _ = lax.optimization_barrier((got[d - low], token))
                need = [c for c in range(chips) if c ^ d < c or c ^ low ^ d < c ^ low]
                pairs = [(2 * c + k, 2 * (c ^ low) + k) for c in need for k in (0, 1)]
                got[d] = lax.ppermute(held, "seq", pairs)
        return [got[d] for d in range(1, chips)]

    def kv_half(which):
        if kvh % 2 == 0:
            return jnp.concatenate([half(k, which, kw), half(v, which, kw)], axis=1)
        return jnp.concatenate([k, v], axis=1)

    kv = joined(kv_half(core), swap(kv_half(1 - core), 1))
    keys_near = near(kv)
    x1, q1, wr1, rd1, _ = lax.optimization_barrier((x, q, wr, rd, kv))
    rates = swap(jnp.concatenate([ls, ld], axis=0), 1)
    lsc = joined(half(ls, core, hh, 0), half(rates, core, hh, 0), 1)
    ldc = joined(half(ld, core, hh, 0), half(rates[heads:], core, hh, 0), 1)
    mates = swap(jnp.concatenate([half(x1, 1 - core, hc), wr1, rd1], axis=1), 1)
    xc = joined(half(x1, core, hc), mates[:, :hc])
    wc = joined(wr1, mates[:, hc : hc + n])
    rc = joined(rd1, mates[:, hc + n :])
    qg = joined(half(q1, core, qc), swap(half(q1, 1 - core, qc), 1))

    mm = 2 * 2 * t * hc * n
    code = ((n + 16, hc), F32)
    st0, coded, wexpc = call(
        state_kernel, [((n, hc), F32), code, ((2 * t, hc), F32)], (xc, wc, lsc, ldc),
        flops=4 * mm,
    )

    def state_stage(coded, bit):
        return swap(coded.astype(F16), 2 << bit).astype(F32)

    stages = [state_stage(coded, 0)] if chips > 1 else []
    qh = qc // HD
    carry = [((qc, 2 * t), F32), ((qh, 2 * t), F32), ((qh, 2 * t), F32)]
    qs, *soft = call(
        own_kernel, [((2 * t, 2 * qc), BF16), *carry], (qg, kv),
        scratch=[pltpu.VMEM((2 * t, 2 * HD), BF16), pltpu.VMEM((HD, 2 * t), BF16), pltpu.VMEM((t, t), F32)]
        + [pltpu.VMEM((t, t), F32), pltpu.VMEM((2 * t, t), F32)] * 2,
        flops=4 * (2 * t) ** 2 * qc,
    )
    ybase, fs, clsx, crow = call(
        local_kernel,
        [((2 * t, hc), F32), ((2 * t, hc), F32), ((2 * t, hc), F32), ((hh, 2 * t), F32)],
        (xc, wc, rc, lsc, ldc, st0),
        scratch=[pltpu.VMEM((t, hc), F32), pltpu.VMEM((hh, t), F32), pltpu.VMEM((t, t), F32)],
        flops=8 * mm,
    )
    for bit in range(1, chips.bit_length() - 1):
        flag = jnp.reshape((chip >> (bit - 1)) % 2, (1,)).astype(jnp.int32)
        (coded,) = call(
            functools.partial(merge_kernel, group=1 << (bit - 1)), [code], (flag, coded, stages[-1]),
            in_specs=[pl.BlockSpec(memory_space=pltpu.SMEM), VM, VM],
        )
        stages.append(state_stage(coded, bit))
    decays = {}
    for bit, got in enumerate(stages):
        for m in range(1 << bit):
            at = n + 1 + 3 * m
            decays[(1 << bit) + m] = jnp.sum(got[at : at + 3], axis=0, keepdims=True)

    def between(low, high, most):
        out = jnp.zeros((1, hc), F32)
        for m in range(1, most):
            at = chip ^ m
            out += jnp.where((at > low) & (at < high), decays[m], 0.0)
        return out

    incoming = jnp.zeros((n, hc), F32)
    for bit, got in enumerate(stages):
        fade = jnp.exp(between(-1, chip, 1 << bit))
        incoming += decode(got, n, jnp.where((chip >> bit) % 2 == 1, fade, 0.0))
    far = relay(keys_near, soft[1])

    def combine(got):
        powers = jnp.concatenate([g[n : n + 1] for g in got], axis=0).astype(F32)
        fades = [
            jnp.where((chip ^ d) > chip, jnp.exp(between(chip, chip ^ d, chips)), 0.0)
            for d in range(1, chips)
        ]
        fades, _ = lax.optimization_barrier((jnp.concatenate(fades, axis=0), soft[1]))
        weights = lax.optimization_barrier(jnp.exp2(powers - 12.0) * fades)
        return sum(g[:n].astype(F32) * weights[d : d + 1] for d, g in enumerate(got))

    for d, keys in enumerate(far, 1):
        flag = jnp.reshape((chip ^ d) < chip, (1,)).astype(jnp.int32)
        soft = call(
            far_kernel, carry, (flag, qs, keys, *soft),
            scratch=[pltpu.VMEM((2 * t, 2 * HD), BF16), pltpu.VMEM((HD, 2 * t), BF16)] + [pltpu.VMEM((2 * t, 2 * t), F32)] * 2,
            flops=4 * (2 * t) ** 2 * qc, alias={3: 0, 4: 1, 5: 2},
            in_specs=[pl.BlockSpec(memory_space=pltpu.SMEM)] + [VM] * 5,
        )
    res, d1, dcode = call(
        residual_kernel, [((2 * t, hc), F32), ((n, hc), F32), code],
        (ybase, soft[0], soft[2], rc, fs, incoming), flops=8 * mm,
    )
    sent = dcode.astype(F16)
    coming = [swap(sent, 2 * d) for d in range(1, chips)]
    back, gw, gr = call(
        back_kernel, [((2 * t, hc), F32), ((2 * t, n), F32), ((2 * t, n), F32)],
        (res, xc, wc, rc, clsx, crow, fs, wexpc, incoming, st0, d1),
        scratch=[pltpu.VMEM((t, t), F32), pltpu.VMEM((t, t), F32)],
        flops=16 * mm,
    )
    other_total = jnp.sum(rates[heads:], axis=1)[None, :]
    extra = jnp.where(core == 0, other_total, 0.0)
    wexp, xh, xl = call(
        ready_kernel, [((t, 2 * hc), F32), ((t, 2 * hc), BF16), ((t, 2 * hc), BF16)],
        (x, ls, ld, extra), flops=2 * mm,
    )

    def home(a):
        return half(a, core, t, 0), swap(half(a, 1 - core, t, 0), 1)

    def tp_sum(a):
        bit = 1
        while bit < tp:
            a = a + lax.ppermute(a, "tp", [(i, i ^ bit) for i in range(tp)])
            bit *= 2
        return a

    back_all = joined(*home(back), 1)
    own, other = home(jnp.concatenate([gw, gr], axis=1))
    grads = own + other
    gw0, gr0 = grads[:, :n], grads[:, n:]
    grad_read = tp_sum(gr0)
    arriving = combine(coming)
    arrived = joined(arriving, swap(arriving, 1), 1)
    (gwp,) = call(write_kernel, [((t, n), F32)], (xh, xl, arrived, gw0), flops=4 * mm)
    grad_write = tp_sum(gwp)
    gi, gls = call(
        final_kernel, [((t, 2 * hc), F32), ((heads, t), F32)], (back_all, wexp, x, wr, arrived),
        flops=8 * mm,
    )
    return (gi, grad_write, grad_read, gls)


def solution(mesh):
    in_specs = (
        P("seq", "tp"), P("seq", "tp"), P("seq", "tp"), P("seq", "tp"),
        P("seq", None), P("seq", None), P("tp", "seq"), P("tp", "seq"),
    )
    out_specs = (P("seq", "tp"), P("seq", None), P("seq", None), P("tp", "seq"))
    return jax.shard_map(
        on_device, mesh=mesh, in_specs=in_specs, out_specs=out_specs, check_vma=False
    )
```

```python
import functools
import math

import jax
import jax.numpy as jnp
from jax import lax
from jax.experimental import pallas as pl
from jax.experimental.pallas import tpu as pltpu
from jax.sharding import PartitionSpec as P


HD = 128
F32, BF16, F16 = jnp.float32, jnp.bfloat16, jnp.float16


def nn(a, b):
    return lax.dot_general(a, b, (((1,), (0,)), ((), ())), preferred_element_type=F32)


def nt(a, b):
    return lax.dot_general(a, b, (((1,), (1,)), ((), ())), preferred_element_type=F32)


def tn(a, b):
    return lax.dot_general(a, b, (((0,), (0,)), ((), ())), preferred_element_type=F32)


def split2(a):
    hi = a.astype(BF16)
    return hi, (a - hi.astype(F32)).astype(BF16)


def split3(a):
    hi = a.astype(BF16)
    rest = a - hi.astype(F32)
    mid = rest.astype(BF16)
    return hi, mid, (rest - mid.astype(F32)).astype(BF16)


def iota(shape, dim):
    return lax.broadcasted_iota(jnp.int32, shape, dim)


def lower(t):
    return (iota((t, t), 0) >= iota((t, t), 1)).astype(BF16)


def spread_matrix(heads, width, times=1):
    row = iota((times * heads, width), 0) % heads
    return (iota((times * heads, width), 1) // (width // heads) == row).astype(BF16)


def spread(col, width):
    pieces = [p.astype(F32) for p in split3(col)]
    stacked = jnp.concatenate(pieces, axis=1).astype(BF16)
    return nn(stacked, spread_matrix(col.shape[1], width, 3))


def stack2(a):
    return jnp.concatenate(split2(a), axis=0)


def twice(a):
    return jnp.concatenate([a, a], axis=1)


def nt3(a, b):
    ah, al = split2(a)
    bh, bl = split2(b)
    both = nt(ah, jnp.concatenate([bh, bl], axis=0))
    half = both.shape[1] // 2
    return both[:, :half] + both[:, half:] + nt(al, bh)


def code_rows(state, extra):
    top = jnp.max(jnp.abs(state), axis=0, keepdims=True)
    power = jnp.ceil(jnp.log2(jnp.maximum(top, 1e-30)))
    used = sum(e.shape[0] for e in extra)
    rest = jnp.zeros((15 - used, state.shape[1]), F32)
    return state * jnp.exp2(12.0 - power), jnp.concatenate([power, *extra, rest], axis=0)


def spread_row(row, width):
    return spread(jnp.broadcast_to(row, (8, row.shape[1])), width)[0:1]


def cum_col(ld):
    tri = lower(ld.shape[1])
    a, b, c = split3(ld)
    return nt(tri, a) + nt(tri, b) + nt(tri, c)


def cum_row(ld):
    tri = lower(ld.shape[1])
    a, b, c = split3(ld)
    return nt(a, tri) + nt(b, tri) + nt(c, tri)


def turn(rows):
    t = rows.shape[1]
    eye = (iota((t, t), 0) == iota((t, t), 1)).astype(BF16)
    a, b, c = split3(rows)
    return nt(eye, a) + nt(eye, b) + nt(eye, c)


def state_kernel(x_ref, w_ref, ls_ref, ld_ref, st0_ref, coded_ref, wexp_ref):
    t = x_ref.shape[0] // 2
    width = x_ref.shape[1]
    n = w_ref.shape[1]
    parts, tots = [], []
    for b in (0, 1):
        rows = slice(b * t, (b + 1) * t)
        ccol = cum_col(ld_ref[:, rows])
        tot = ccol[t - 1 : t, :]
        wexp = spread(jnp.exp(tot - ccol + turn(ls_ref[:, rows])), width)
        wexp_ref[rows, :] = wexp
        hi, lo = split2(x_ref[rows, :].astype(F32) * wexp)
        parts.append(tn(w_ref[rows, :], hi) + tn(w_ref[rows, :], lo))
        tots.append(tot)
    st0_ref[...] = parts[0]
    state = spread_row(jnp.exp(tots[1]), width) * parts[0] + parts[1]
    pieces = [p.astype(F32) for p in split3(spread_row(tots[0] + tots[1], width))]
    coded_ref[:n, :], coded_ref[n:, :] = code_rows(state, pieces)


def merge_kernel(flag, own_ref, got_ref, out_ref, *, group):
    n = own_ref.shape[0] - 16
    used = 3 * group
    own_rows = own_ref[n + 1 : n + 1 + used, :]
    got_rows = got_ref[n + 1 : n + 1 + used, :]
    own = own_ref[:n, :] * jnp.exp2(own_ref[n : n + 1, :] - 12.0)
    got = got_ref[:n, :] * jnp.exp2(got_ref[n : n + 1, :] - 12.0)
    own_fade = jnp.exp(jnp.sum(own_rows, axis=0, keepdims=True))
    got_fade = jnp.exp(jnp.sum(got_rows, axis=0, keepdims=True))
    earlier = flag[0] == 1
    merged = own * jnp.where(earlier, 1.0, got_fade) + got * jnp.where(earlier, own_fade, 1.0)
    out_ref[:n, :], out_ref[n:, :] = code_rows(merged, [own_rows, got_rows])


def local_kernel(
    x_ref, w_ref, r_ref, ls_ref, ld_ref, st0_ref,
    y_ref, fs_ref, clsx_ref, crow_ref, cexp, clsrow, a_ref,
):
    t = x_ref.shape[0] // 2
    th = t // 2
    width = x_ref.shape[1]
    heads = ls_ref.shape[0]
    hw = width // heads
    per = 128 // hw
    for b in (0, 1):
        rows = slice(b * t, (b + 1) * t)
        ccol = cum_col(ld_ref[:, rows])
        cexp[...] = spread(ccol, width)
        fs = spread(jnp.exp(ccol), width)
        fs_ref[rows, :] = fs
        clsx_ref[rows, :] = spread(ccol - turn(ls_ref[:, rows]), width)
        crow = cum_row(ld_ref[:, rows])
        crow_ref[:, rows] = crow
        clsrow[...] = crow - ls_ref[:, rows]
        keep = iota((t, t), 0) >= iota((t, t), 1)
        a_ref[...] = jnp.where(keep, nt(r_ref[rows, :], w_ref[rows, :]), 0.0)
        if b == 1:
            y_ref[rows, :] = fs * nn(twice(r_ref[rows, :]), stack2(st0_ref[...]))

        def one(i, rows=rows, b=b):
            cols = pl.ds(pl.multiple_of(i * 128, 128), 128)
            xp = x_ref[rows, cols]
            xtop = jnp.concatenate([xp[:th], xp[:th]], axis=0)
            cc = cexp[:, cols]
            lane = iota((t, 128), 1)
            out = None
            for a in range(per):
                ci = cc[:, a * hw : a * hw + 1]
                cj = clsrow[pl.ds(i * per + a, 1), :]
                top = jnp.exp(jnp.minimum(ci[:th] - cj[:, :th], 0.0)) * a_ref[:th, :th]
                bot = jnp.exp(jnp.minimum(ci[th:] - cj, 0.0)) * a_ref[th:, :]
                yt = nn(jnp.concatenate(split2(top), axis=1), xtop)
                b1, b2 = split2(bot)
                yb = nn(b1, xp) + nn(b2, xp)
                mine = jnp.concatenate([yt, yb], axis=0)
                out = mine if out is None else jnp.where(lane >= a * hw, mine, out)
            if b == 1:
                out = out + y_ref[rows, cols]
            return cols, out

        def two(i, _, rows=rows, one=one):
            done = [one(2 * i), one(2 * i + 1)]
            for cols, out in done:
                y_ref[rows, cols] = out
            return 0

        lax.fori_loop(0, width // 256, two, 0)


def keys_twice(kv_ref, g, kw):
    k = kv_ref[:, g * HD : (g + 1) * HD]
    return jnp.concatenate([k, k], axis=1), kv_ref[:, kw + g * HD : kw + (g + 1) * HD].T


def own_kernel(q_ref, kv_ref, qs_ref, acc_ref, m_ref, l_ref, k2, vt, bias, s0a, s1a, s0b, s1b):
    t = q_ref.shape[0] // 2
    kw = kv_ref.shape[1] // 2
    kvh = kw // HD
    group = q_ref.shape[1] // HD // kvh
    scale = 1.0 / math.sqrt(HD)
    bias[...] = jnp.where(iota((t, t), 0) <= iota((t, t), 1), 0.0, -1e30)
    for g in range(kvh):
        k2[...], vt[...] = keys_twice(kv_ref, g, kw)

        def scores(h, s0, s1, g=g):
            at = g * group + h
            q = q_ref[:, pl.ds(pl.multiple_of(at * HD, HD), HD)].astype(F32) * scale
            both = jnp.concatenate(split2(q), axis=1)
            qs_ref[:, pl.ds(pl.multiple_of(at * 2 * HD, 2 * HD), 2 * HD)] = both
            s0[...] = nt(k2[:t, :], both[:t]) + bias[...]
            s1[:t, :] = nt(k2[:t, :], both[t:])
            s1[t:, :] = nt(k2[t:, :], both[t:]) + bias[...]

        def soft(h, s0, s1, g=g):
            at = g * group + h
            cols = pl.ds(pl.multiple_of(at * HD, HD), HD)
            for b, s_ref in ((0, s0), (1, s1)):
                rows = slice(b * t, (b + 1) * t)
                s = s_ref[...]
                top = jnp.max(s, axis=0, keepdims=True)
                e = jnp.exp(s - top)
                m_ref[pl.ds(at, 1), rows] = top
                l_ref[pl.ds(at, 1), rows] = jnp.sum(e, axis=0, keepdims=True)
                acc_ref[cols, rows] = nn(vt[:, : (b + 1) * t], e.astype(BF16))

        scores(0, s0a, s1a)

        def pair(i, _):
            scores(2 * i + 1, s0b, s1b)
            soft(2 * i, s0a, s1a)
            scores(jnp.minimum(2 * i + 2, group - 1), s0a, s1a)
            soft(2 * i + 1, s0b, s1b)
            return 0

        lax.fori_loop(0, group // 2, pair, 0)


def far_kernel(flag, qs_ref, kv_ref, acc_in, m_in, l_in, acc_ref, m_ref, l_ref, k2, vt, sa, sb):
    t = qs_ref.shape[0] // 2
    kw = kv_ref.shape[1] // 2
    kvh = kw // HD
    group = qs_ref.shape[1] // (2 * HD) // kvh

    @pl.when(flag[0] == 0)
    def _():
        acc_ref[...] = acc_in[...]
        m_ref[...] = m_in[...]
        l_ref[...] = l_in[...]

    @pl.when(flag[0] == 1)
    def _():
        for g in range(kvh):
            k2[...], vt[...] = keys_twice(kv_ref, g, kw)

            def scores(h, s_ref, g=g):
                at = g * group + h
                s_ref[...] = nt(k2[...], qs_ref[:, pl.ds(pl.multiple_of(at * 2 * HD, 2 * HD), 2 * HD)])

            def soft(h, s_ref, g=g):
                at = g * group + h
                cols = pl.ds(pl.multiple_of(at * HD, HD), HD)
                row = pl.ds(at, 1)
                for b in (0, 1):
                    rows = slice(b * t, (b + 1) * t)
                    s = s_ref[:, rows]
                    old = m_in[row, rows]
                    new = jnp.maximum(old, jnp.max(s, axis=0, keepdims=True))
                    e = jnp.exp(s - new)
                    fade = jnp.exp(old - new)
                    m_ref[row, rows] = new
                    l_ref[row, rows] = l_in[row, rows] * fade + jnp.sum(e, axis=0, keepdims=True)
                    acc_ref[cols, rows] = acc_in[cols, rows] * fade + nn(vt[...], e.astype(BF16))

            scores(0, sa)

            def pair(i, _):
                scores(2 * i + 1, sb)
                soft(2 * i, sa)
                scores(jnp.minimum(2 * i + 2, group - 1), sa)
                soft(2 * i + 1, sb)
                return 0

            lax.fori_loop(0, group // 2, pair, 0)


def residual_kernel(y_ref, acc_ref, l_ref, r_ref, fs_ref, sin_ref, res_ref, d1_ref, coded_ref):
    t = y_ref.shape[0] // 2
    width = y_ref.shape[1]
    n = r_ref.shape[1]
    state = sin_ref[...]
    first = fs_ref[t - 1 : t, :]
    parts = []
    for b in (0, 1):
        rows = slice(b * t, (b + 1) * t)
        fs = fs_ref[rows, :]
        r = r_ref[rows, :]
        heads = [
            (acc_ref[h * HD : (h + 1) * HD, rows] / l_ref[h : h + 1, rows]).astype(BF16).T
            for h in range(width // HD)
        ]
        teach = jnp.concatenate(heads, axis=1).astype(F32)
        res = y_ref[rows, :] + fs * nn(twice(r), stack2(state * first if b else state)) - teach
        res_ref[rows, :] = res
        hi, lo = split2(res * fs)
        parts.append(tn(r, hi) + tn(r, lo))
    d1_ref[...] = parts[1]
    coded_ref[:n, :], coded_ref[n:, :] = code_rows(parts[0] + first * parts[1], [])


def back_kernel(
    res_ref, x_ref, w_ref, r_ref, clsx_ref, crow_ref, fs_ref, wexp_ref, sin_ref, st0_ref, d1_ref,
    back_ref, gw_ref, gr_ref, a_ref, pair,
):
    t = x_ref.shape[0] // 2
    th = t // 2
    width = x_ref.shape[1]
    heads = crow_ref.shape[0]
    hw = width // heads
    per = 128 // hw
    first = fs_ref[t - 1 : t, :]
    for b in (0, 1):
        rows = slice(b * t, (b + 1) * t)
        keep = iota((t, t), 1) >= iota((t, t), 0)
        w = w_ref[rows, :]
        r = r_ref[rows, :]
        a_ref[...] = jnp.where(keep, nt(w, r), 0.0)
        pair[...] = jnp.zeros_like(pair)
        if b == 0:
            d1 = d1_ref[...]
            wexp = wexp_ref[rows, :]
            back_ref[rows, :] = wexp * nn(twice(w), stack2(d1))
            gw = nt3(x_ref[rows, :].astype(F32) * wexp, d1)
            state = sin_ref[...]
        else:
            gw = None
            state = first * sin_ref[...] + st0_ref[...]
        gr = nt3(res_ref[rows, :] * fs_ref[rows, :], state)

        def one(i, rows=rows, b=b):
            cols = pl.ds(pl.multiple_of(i * 128, 128), 128)
            xp = x_ref[rows, cols]
            rh, rl = split2(res_ref[rows, cols])
            both = jnp.concatenate([rh, rl], axis=1)
            cc = clsx_ref[rows, cols]
            lane = iota((t, 128), 1)
            out, above, below = None, 0.0, 0.0
            for a in range(per):
                cj = cc[:, a * hw : a * hw + 1]
                ci = crow_ref[pl.ds(i * per + a, 1), rows]
                xx = twice(jnp.where((lane // hw) == a, xp, jnp.zeros_like(xp)))
                e1 = jnp.exp(jnp.minimum(ci - cj[:th], 0.0))
                e2 = jnp.exp(jnp.minimum(ci[:, th:] - cj[th:], 0.0))
                h1, l1 = split2(e1 * a_ref[:th, :])
                h2, l2 = split2(e2 * a_ref[th:, th:])
                p1 = nn(h1, both)
                p2 = nn(h2, both[th:])
                u1 = p1[:, :128] + p1[:, 128:] + nn(l1, rh)
                u2 = p2[:, :128] + p2[:, 128:] + nn(l2, rh[th:])
                u = jnp.concatenate([u1, u2], axis=0)
                out = u if out is None else jnp.where(lane >= a * hw, u, out)
                above += e1 * nt(xx[:th], both)
                below += e2 * nt(xx[th:], both[th:])
            if b == 0:
                out = out + back_ref[rows, cols]
            return cols, out, above, below

        def two(i, _, rows=rows, one=one):
            done = [one(2 * i), one(2 * i + 1)]
            for cols, out, _, _ in done:
                back_ref[rows, cols] = out
            pair[:th, :] += done[0][2] + done[1][2]
            pair[th:, th:] += done[0][3] + done[1][3]
            return 0

        lax.fori_loop(0, width // 256, two, 0)
        ph, plo = split2(jnp.where(keep, pair[...], 0.0))
        gr_ref[rows, :] = gr + tn(ph, w) + tn(plo, w)
        mixed = nn(ph, r) + nn(plo, r)
        gw_ref[rows, :] = mixed if gw is None else mixed + gw


def ready_kernel(x_ref, ls_ref, ld_ref, extra_ref, wexp_ref, xh_ref, xl_ref):
    t = x_ref.shape[0]
    ccol = cum_col(ld_ref[...])
    wexp = spread(
        jnp.exp(ccol[t - 1 : t, :] + extra_ref[...] - ccol + turn(ls_ref[...])), x_ref.shape[1]
    )
    wexp_ref[...] = wexp
    xh_ref[...], xl_ref[...] = split2(x_ref[...].astype(F32) * wexp)


def write_kernel(xh_ref, xl_ref, g_ref, gw0_ref, gw_ref):
    gh, gl = split2(g_ref[...])
    n = gh.shape[0]
    both = nt(xh_ref[...], jnp.concatenate([gh, gl], axis=0))
    gw_ref[...] = gw0_ref[...] + both[:, :n] + both[:, n:] + nt(xl_ref[...], gh)


def final_kernel(back_ref, wexp_ref, x_ref, w_ref, g_ref, gi_ref, gls_ref):
    width = x_ref.shape[1]
    heads = gls_ref.shape[0]
    out = back_ref[...] + wexp_ref[...] * nn(twice(w_ref[...]), stack2(g_ref[...]))
    gi_ref[...] = out
    ph, plo = split2(x_ref[...].astype(F32) * out)
    mat = spread_matrix(heads, width)
    gls_ref[...] = nt(mat, ph) + nt(mat, plo)


VM = pl.BlockSpec(memory_space=pltpu.VMEM)


def call(kernel, outs, args, scratch=(), flops=0, in_specs=None, alias=None):
    shapes = [jax.ShapeDtypeStruct(s, d) for s, d in outs]
    moved = sum(a.size * a.dtype.itemsize for a in args)
    return pl.pallas_call(
        kernel,
        out_shape=shapes,
        in_specs=in_specs or [VM] * len(args),
        out_specs=[VM] * len(shapes),
        scratch_shapes=list(scratch),
        input_output_aliases=alias or {},
        cost_estimate=pl.CostEstimate(flops=flops, bytes_accessed=moved, transcendentals=0),
        compiler_params=pltpu.CompilerParams(vmem_limit_bytes=8 * 2**20),
    )(*args)


def decode(coded, rows, weight):
    power = coded[rows : rows + 1].astype(F32)
    return coded[:rows].astype(F32) * (jnp.exp2(power - 12.0) * weight)


def on_device(q, k, v, x, wr, rd, ls, ld):
    t = q.shape[0]
    count = lax.axis_size("seq")
    tp = lax.axis_size("tp")
    chips = count // 2
    index = lax.axis_index("seq")
    core, chip = index % 2, index // 2
    heads = ls.shape[0]
    hh = heads // 2
    n = wr.shape[1]
    hc = x.shape[1] // 2
    qc = q.shape[1] // 2
    kvh = k.shape[1] // HD
    kw = k.shape[1] // 2 if kvh % 2 == 0 else k.shape[1]

    def swap(a, bits):
        return lax.ppermute(a, "seq", [(i, i ^ bits) for i in range(count)])

    def half(a, which, width, axis=1):
        return lax.dynamic_slice_in_dim(a, which * width, width, axis=axis)

    def joined(own, other, axis=0):
        a = jnp.where(core == 0, own, other)
        b = jnp.where(core == 0, other, own)
        return jnp.concatenate([a, b], axis=axis)

    def near(a):
        got = {}
        for b in range(chips.bit_length() - 1):
            got[1 << b] = swap(a, 2 << b)
        return got

    def relay(got, token):
        got = dict(got)
        for d in range(1, chips):
            if d not in got:
                low = d & -d
                held, _ = lax.optimization_barrier((got[d - low], token))
                need = [c for c in range(chips) if c ^ d < c or c ^ low ^ d < c ^ low]
                pairs = [(2 * c + k, 2 * (c ^ low) + k) for c in need for k in (0, 1)]
                got[d] = lax.ppermute(held, "seq", pairs)
        return [got[d] for d in range(1, chips)]

    def kv_half(which):
        if kvh % 2 == 0:
            return jnp.concatenate([half(k, which, kw), half(v, which, kw)], axis=1)
        return jnp.concatenate([k, v], axis=1)

    kv = joined(kv_half(core), swap(kv_half(1 - core), 1))
    keys_near = near(kv)
    x1, q1, wr1, rd1, _ = lax.optimization_barrier((x, q, wr, rd, kv))
    rates = swap(jnp.concatenate([ls, ld], axis=0), 1)
    lsc = joined(half(ls, core, hh, 0), half(rates, core, hh, 0), 1)
    ldc = joined(half(ld, core, hh, 0), half(rates[heads:], core, hh, 0), 1)
    mates = swap(jnp.concatenate([half(x1, 1 - core, hc), wr1, rd1], axis=1), 1)
    xc = joined(half(x1, core, hc), mates[:, :hc])
    wc = joined(wr1, mates[:, hc : hc + n])
    rc = joined(rd1, mates[:, hc + n :])
    qg = joined(half(q1, core, qc), swap(half(q1, 1 - core, qc), 1))

    mm = 2 * 2 * t * hc * n
    code = ((n + 16, hc), F32)
    st0, coded, wexpc = call(
        state_kernel, [((n, hc), F32), code, ((2 * t, hc), F32)], (xc, wc, lsc, ldc),
        flops=4 * mm,
    )

    def state_stage(coded, bit):
        return swap(coded.astype(F16), 2 << bit).astype(F32)

    stages = [state_stage(coded, 0)] if chips > 1 else []
    qh = qc // HD
    carry = [((qc, 2 * t), F32), ((qh, 2 * t), F32), ((qh, 2 * t), F32)]
    qs, *soft = call(
        own_kernel, [((2 * t, 2 * qc), BF16), *carry], (qg, kv),
        scratch=[pltpu.VMEM((2 * t, 2 * HD), BF16), pltpu.VMEM((HD, 2 * t), BF16), pltpu.VMEM((t, t), F32)]
        + [pltpu.VMEM((t, t), F32), pltpu.VMEM((2 * t, t), F32)] * 2,
        flops=4 * (2 * t) ** 2 * qc,
    )
    ybase, fs, clsx, crow = call(
        local_kernel,
        [((2 * t, hc), F32), ((2 * t, hc), F32), ((2 * t, hc), F32), ((hh, 2 * t), F32)],
        (xc, wc, rc, lsc, ldc, st0),
        scratch=[pltpu.VMEM((t, hc), F32), pltpu.VMEM((hh, t), F32), pltpu.VMEM((t, t), F32)],
        flops=8 * mm,
    )
    for bit in range(1, chips.bit_length() - 1):
        flag = jnp.reshape((chip >> (bit - 1)) % 2, (1,)).astype(jnp.int32)
        (coded,) = call(
            functools.partial(merge_kernel, group=1 << (bit - 1)), [code], (flag, coded, stages[-1]),
            in_specs=[pl.BlockSpec(memory_space=pltpu.SMEM), VM, VM],
        )
        stages.append(state_stage(coded, bit))
    decays = {}
    for bit, got in enumerate(stages):
        for m in range(1 << bit):
            at = n + 1 + 3 * m
            decays[(1 << bit) + m] = jnp.sum(got[at : at + 3], axis=0, keepdims=True)

    def between(low, high, most):
        out = jnp.zeros((1, hc), F32)
        for m in range(1, most):
            at = chip ^ m
            out += jnp.where((at > low) & (at < high), decays[m], 0.0)
        return out

    incoming = jnp.zeros((n, hc), F32)
    for bit, got in enumerate(stages):
        fade = jnp.exp(between(-1, chip, 1 << bit))
        incoming += decode(got, n, jnp.where((chip >> bit) % 2 == 1, fade, 0.0))
    far = relay(keys_near, soft[1])

    def combine(got):
        out = 0.0
        for d, g in enumerate(got, 1):
            fade = jnp.exp(between(chip, chip ^ d, chips))
            out += decode(g, n, jnp.where((chip ^ d) > chip, fade, 0.0))
        return out

    nearer = [1 << b for b in reversed(range(chips.bit_length() - 1))]
    for d in nearer + [d for d in range(1, chips) if d not in nearer]:
        keys = far[d - 1]
        flag = jnp.reshape((chip ^ d) < chip, (1,)).astype(jnp.int32)
        soft = call(
            far_kernel, carry, (flag, qs, keys, *soft),
            scratch=[pltpu.VMEM((2 * t, 2 * HD), BF16), pltpu.VMEM((HD, 2 * t), BF16)] + [pltpu.VMEM((2 * t, 2 * t), F32)] * 2,
            flops=4 * (2 * t) ** 2 * qc, alias={3: 0, 4: 1, 5: 2},
            in_specs=[pl.BlockSpec(memory_space=pltpu.SMEM)] + [VM] * 5,
        )
    res, d1, dcode = call(
        residual_kernel, [((2 * t, hc), F32), ((n, hc), F32), code],
        (ybase, soft[0], soft[2], rc, fs, incoming), flops=8 * mm,
    )
    sent = dcode.astype(F16)
    coming = [swap(sent, 2 * d) for d in range(1, chips)]
    back, gw, gr = call(
        back_kernel, [((2 * t, hc), F32), ((2 * t, n), F32), ((2 * t, n), F32)],
        (res, xc, wc, rc, clsx, crow, fs, wexpc, incoming, st0, d1),
        scratch=[pltpu.VMEM((t, t), F32), pltpu.VMEM((t, t), F32)],
        flops=16 * mm,
    )
    other_total = jnp.sum(rates[heads:], axis=1)[None, :]
    extra = jnp.where(core == 0, other_total, 0.0)
    wexp, xh, xl = call(
        ready_kernel, [((t, 2 * hc), F32), ((t, 2 * hc), BF16), ((t, 2 * hc), BF16)],
        (x, ls, ld, extra), flops=2 * mm,
    )

    def home(a):
        return half(a, core, t, 0), swap(half(a, 1 - core, t, 0), 1)

    def tp_sum(a):
        for bit in range(tp.bit_length() - 1):
            a = a + lax.ppermute(a, "tp", [(i, i ^ (1 << bit)) for i in range(tp)])
        return a

    back_all = joined(*home(back), 1)
    own, other = home(jnp.concatenate([gw, gr], axis=1))
    grads = own + other
    gw0, gr0 = grads[:, :n], grads[:, n:]
    grad_read = tp_sum(gr0)
    arriving = combine(coming)
    arrived = joined(arriving, swap(arriving, 1), 1)
    (gwp,) = call(write_kernel, [((t, n), F32)], (xh, xl, arrived, gw0), flops=4 * mm)
    grad_write = tp_sum(gwp)
    gi, gls = call(
        final_kernel, [((t, 2 * hc), F32), ((heads, t), F32)], (back_all, wexp, x, wr, arrived),
        flops=8 * mm,
    )
    return (gi, grad_write, grad_read, gls)


def solution(mesh):
    in_specs = (
        P("seq", "tp"), P("seq", "tp"), P("seq", "tp"), P("seq", "tp"),
        P("seq", None), P("seq", None), P("tp", "seq"), P("tp", "seq"),
    )
    out_specs = (P("seq", "tp"), P("seq", None), P("seq", None), P("tp", "seq"))
    return jax.shard_map(
        on_device, mesh=mesh, in_specs=in_specs, out_specs=out_specs, check_vma=False
    )
```

```python
import functools
import math

import jax
import jax.numpy as jnp
from jax import lax
from jax.experimental import pallas as pl
from jax.experimental.pallas import tpu as pltpu
from jax.sharding import PartitionSpec as P


HD = 128
F32, BF16, F16 = jnp.float32, jnp.bfloat16, jnp.float16


def nn(a, b):
    return lax.dot_general(a, b, (((1,), (0,)), ((), ())), preferred_element_type=F32)


def nt(a, b):
    return lax.dot_general(a, b, (((1,), (1,)), ((), ())), preferred_element_type=F32)


def tn(a, b):
    return lax.dot_general(a, b, (((0,), (0,)), ((), ())), preferred_element_type=F32)


def split2(a):
    hi = a.astype(BF16)
    return hi, (a - hi.astype(F32)).astype(BF16)


def split3(a):
    hi = a.astype(BF16)
    rest = a - hi.astype(F32)
    mid = rest.astype(BF16)
    return hi, mid, (rest - mid.astype(F32)).astype(BF16)


def iota(shape, dim):
    return lax.broadcasted_iota(jnp.int32, shape, dim)


def lower(t):
    return (iota((t, t), 0) >= iota((t, t), 1)).astype(BF16)


def spread_matrix(heads, width, times=1):
    row = iota((times * heads, width), 0) % heads
    return (iota((times * heads, width), 1) // (width // heads) == row).astype(BF16)


def spread(col, width):
    pieces = [p.astype(F32) for p in split3(col)]
    stacked = jnp.concatenate(pieces, axis=1).astype(BF16)
    return nn(stacked, spread_matrix(col.shape[1], width, 3))


def stack2(a):
    return jnp.concatenate(split2(a), axis=0)


def twice(a):
    return jnp.concatenate([a, a], axis=1)


def nt3(a, b):
    ah, al = split2(a)
    bh, bl = split2(b)
    both = nt(ah, jnp.concatenate([bh, bl], axis=0))
    half = both.shape[1] // 2
    return both[:, :half] + both[:, half:] + nt(al, bh)


def code_rows(state, extra):
    top = jnp.max(jnp.abs(state), axis=0, keepdims=True)
    power = jnp.ceil(jnp.log2(jnp.maximum(top, 1e-30)))
    used = sum(e.shape[0] for e in extra)
    rest = jnp.zeros((15 - used, state.shape[1]), F32)
    return state * jnp.exp2(12.0 - power), jnp.concatenate([power, *extra, rest], axis=0)


def spread_row(row, width):
    return spread(jnp.broadcast_to(row, (8, row.shape[1])), width)[0:1]


def cum_col(ld):
    tri = lower(ld.shape[1])
    a, b, c = split3(ld)
    return nt(tri, a) + nt(tri, b) + nt(tri, c)


def cum_row(ld):
    tri = lower(ld.shape[1])
    a, b, c = split3(ld)
    return nt(a, tri) + nt(b, tri) + nt(c, tri)


def turn(rows):
    t = rows.shape[1]
    eye = (iota((t, t), 0) == iota((t, t), 1)).astype(BF16)
    a, b, c = split3(rows)
    return nt(eye, a) + nt(eye, b) + nt(eye, c)


def state_kernel(x_ref, w_ref, ls_ref, ld_ref, st0_ref, coded_ref, wexp_ref):
    t = x_ref.shape[0] // 2
    width = x_ref.shape[1]
    n = w_ref.shape[1]
    parts, tots = [], []
    for b in (0, 1):
        rows = slice(b * t, (b + 1) * t)
        ccol = cum_col(ld_ref[:, rows])
        tot = ccol[t - 1 : t, :]
        wexp = spread(jnp.exp(tot - ccol + turn(ls_ref[:, rows])), width)
        wexp_ref[rows, :] = wexp
        hi, lo = split2(x_ref[rows, :].astype(F32) * wexp)
        parts.append(tn(w_ref[rows, :], hi) + tn(w_ref[rows, :], lo))
        tots.append(tot)
    st0_ref[...] = parts[0]
    state = spread_row(jnp.exp(tots[1]), width) * parts[0] + parts[1]
    pieces = [p.astype(F32) for p in split3(spread_row(tots[0] + tots[1], width))]
    coded_ref[:n, :], coded_ref[n:, :] = code_rows(state, pieces)


def merge_kernel(flag, own_ref, got_ref, out_ref, *, group):
    n = own_ref.shape[0] - 16
    used = 3 * group
    own_rows = own_ref[n + 1 : n + 1 + used, :]
    got_rows = got_ref[n + 1 : n + 1 + used, :]
    own = own_ref[:n, :] * jnp.exp2(own_ref[n : n + 1, :] - 12.0)
    got = got_ref[:n, :] * jnp.exp2(got_ref[n : n + 1, :] - 12.0)
    own_fade = jnp.exp(jnp.sum(own_rows, axis=0, keepdims=True))
    got_fade = jnp.exp(jnp.sum(got_rows, axis=0, keepdims=True))
    earlier = flag[0] == 1
    merged = own * jnp.where(earlier, 1.0, got_fade) + got * jnp.where(earlier, own_fade, 1.0)
    out_ref[:n, :], out_ref[n:, :] = code_rows(merged, [own_rows, got_rows])


def local_kernel(
    x_ref, w_ref, r_ref, ls_ref, ld_ref, st0_ref,
    y_ref, fs_ref, clsx_ref, crow_ref, cexp, clsrow, a_ref,
):
    t = x_ref.shape[0] // 2
    th = t // 2
    width = x_ref.shape[1]
    heads = ls_ref.shape[0]
    hw = width // heads
    per = 128 // hw
    for b in (0, 1):
        rows = slice(b * t, (b + 1) * t)
        ccol = cum_col(ld_ref[:, rows])
        cexp[...] = spread(ccol, width)
        fs = spread(jnp.exp(ccol), width)
        fs_ref[rows, :] = fs
        clsx_ref[rows, :] = spread(ccol - turn(ls_ref[:, rows]), width)
        crow = cum_row(ld_ref[:, rows])
        crow_ref[:, rows] = crow
        clsrow[...] = crow - ls_ref[:, rows]
        keep = iota((t, t), 0) >= iota((t, t), 1)
        a_ref[...] = jnp.where(keep, nt(r_ref[rows, :], w_ref[rows, :]), 0.0)
        if b == 1:
            y_ref[rows, :] = fs * nn(twice(r_ref[rows, :]), stack2(st0_ref[...]))

        def one(i, rows=rows, b=b):
            cols = pl.ds(pl.multiple_of(i * 128, 128), 128)
            xp = x_ref[rows, cols]
            xtop = jnp.concatenate([xp[:th], xp[:th]], axis=0)
            cc = cexp[:, cols]
            lane = iota((t, 128), 1)
            out = None
            for a in range(per):
                ci = cc[:, a * hw : a * hw + 1]
                cj = clsrow[pl.ds(i * per + a, 1), :]
                top = jnp.exp(jnp.minimum(ci[:th] - cj[:, :th], 0.0)) * a_ref[:th, :th]
                bot = jnp.exp(jnp.minimum(ci[th:] - cj, 0.0)) * a_ref[th:, :]
                yt = nn(jnp.concatenate(split2(top), axis=1), xtop)
                b1, b2 = split2(bot)
                yb = nn(b1, xp) + nn(b2, xp)
                mine = jnp.concatenate([yt, yb], axis=0)
                out = mine if out is None else jnp.where(lane >= a * hw, mine, out)
            if b == 1:
                out = out + y_ref[rows, cols]
            return cols, out

        def two(i, _, rows=rows, one=one):
            done = [one(2 * i), one(2 * i + 1)]
            for cols, out in done:
                y_ref[rows, cols] = out
            return 0

        lax.fori_loop(0, width // 256, two, 0)


def keys_twice(kv_ref, g, kw):
    k = kv_ref[:, g * HD : (g + 1) * HD]
    return jnp.concatenate([k, k], axis=1), kv_ref[:, kw + g * HD : kw + (g + 1) * HD].T


def own_kernel(q_ref, kv_ref, qs_ref, acc_ref, m_ref, l_ref, k2, vt, bias, s0a, s1a, s0b, s1b):
    t = q_ref.shape[0] // 2
    kw = kv_ref.shape[1] // 2
    kvh = kw // HD
    group = q_ref.shape[1] // HD // kvh
    scale = 1.0 / math.sqrt(HD)
    bias[...] = jnp.where(iota((t, t), 0) <= iota((t, t), 1), 0.0, -1e30)
    for g in range(kvh):
        k2[...], vt[...] = keys_twice(kv_ref, g, kw)

        def scores(h, s0, s1, g=g):
            at = g * group + h
            q = q_ref[:, pl.ds(pl.multiple_of(at * HD, HD), HD)].astype(F32) * scale
            both = jnp.concatenate(split2(q), axis=1)
            qs_ref[:, pl.ds(pl.multiple_of(at * 2 * HD, 2 * HD), 2 * HD)] = both
            s0[...] = nt(k2[:t, :], both[:t]) + bias[...]
            s1[:t, :] = nt(k2[:t, :], both[t:])
            s1[t:, :] = nt(k2[t:, :], both[t:]) + bias[...]

        def soft(h, s0, s1, g=g):
            at = g * group + h
            cols = pl.ds(pl.multiple_of(at * HD, HD), HD)
            for b, s_ref in ((0, s0), (1, s1)):
                rows = slice(b * t, (b + 1) * t)
                s = s_ref[...]
                top = jnp.max(s, axis=0, keepdims=True)
                e = jnp.exp(s - top)
                m_ref[pl.ds(at, 1), rows] = top
                l_ref[pl.ds(at, 1), rows] = jnp.sum(e, axis=0, keepdims=True)
                acc_ref[cols, rows] = nn(vt[:, : (b + 1) * t], e.astype(BF16))

        scores(0, s0a, s1a)

        def pair(i, _):
            scores(2 * i + 1, s0b, s1b)
            soft(2 * i, s0a, s1a)
            scores(jnp.minimum(2 * i + 2, group - 1), s0a, s1a)
            soft(2 * i + 1, s0b, s1b)
            return 0

        lax.fori_loop(0, group // 2, pair, 0)


def far_kernel(flag, qs_ref, kv_ref, acc_in, m_in, l_in, acc_ref, m_ref, l_ref, k2, vt, sa, sb):
    t = qs_ref.shape[0] // 2
    kw = kv_ref.shape[1] // 2
    kvh = kw // HD
    group = qs_ref.shape[1] // (2 * HD) // kvh

    @pl.when(flag[0] == 0)
    def _():
        acc_ref[...] = acc_in[...]
        m_ref[...] = m_in[...]
        l_ref[...] = l_in[...]

    @pl.when(flag[0] == 1)
    def _():
        for g in range(kvh):
            k2[...], vt[...] = keys_twice(kv_ref, g, kw)

            def scores(h, s_ref, g=g):
                at = g * group + h
                s_ref[...] = nt(k2[...], qs_ref[:, pl.ds(pl.multiple_of(at * 2 * HD, 2 * HD), 2 * HD)])

            def soft(h, s_ref, g=g):
                at = g * group + h
                cols = pl.ds(pl.multiple_of(at * HD, HD), HD)
                row = pl.ds(at, 1)
                for b in (0, 1):
                    rows = slice(b * t, (b + 1) * t)
                    s = s_ref[:, rows]
                    old = m_in[row, rows]
                    new = jnp.maximum(old, jnp.max(s, axis=0, keepdims=True))
                    e = jnp.exp(s - new)
                    fade = jnp.exp(old - new)
                    m_ref[row, rows] = new
                    l_ref[row, rows] = l_in[row, rows] * fade + jnp.sum(e, axis=0, keepdims=True)
                    acc_ref[cols, rows] = acc_in[cols, rows] * fade + nn(vt[...], e.astype(BF16))

            scores(0, sa)

            def pair(i, _):
                scores(2 * i + 1, sb)
                soft(2 * i, sa)
                scores(jnp.minimum(2 * i + 2, group - 1), sa)
                soft(2 * i + 1, sb)
                return 0

            lax.fori_loop(0, group // 2, pair, 0)


def residual_kernel(y_ref, acc_ref, l_ref, r_ref, fs_ref, sin_ref, res_ref, d1_ref, coded_ref):
    t = y_ref.shape[0] // 2
    width = y_ref.shape[1]
    n = r_ref.shape[1]
    state = sin_ref[...]
    first = fs_ref[t - 1 : t, :]
    parts = []
    for b in (0, 1):
        rows = slice(b * t, (b + 1) * t)
        fs = fs_ref[rows, :]
        r = r_ref[rows, :]
        heads = [
            (acc_ref[h * HD : (h + 1) * HD, rows] / l_ref[h : h + 1, rows]).astype(BF16).T
            for h in range(width // HD)
        ]
        teach = jnp.concatenate(heads, axis=1).astype(F32)
        res = y_ref[rows, :] + fs * nn(twice(r), stack2(state * first if b else state)) - teach
        res_ref[rows, :] = res
        hi, lo = split2(res * fs)
        parts.append(tn(r, hi) + tn(r, lo))
    d1_ref[...] = parts[1]
    coded_ref[:n, :], coded_ref[n:, :] = code_rows(parts[0] + first * parts[1], [])


def back_kernel(
    res_ref, x_ref, w_ref, r_ref, clsx_ref, crow_ref, fs_ref, wexp_ref, sin_ref, st0_ref, d1_ref,
    back_ref, gw_ref, gr_ref, a_ref, pair,
):
    t = x_ref.shape[0] // 2
    th = t // 2
    width = x_ref.shape[1]
    heads = crow_ref.shape[0]
    hw = width // heads
    per = 128 // hw
    first = fs_ref[t - 1 : t, :]
    for b in (0, 1):
        rows = slice(b * t, (b + 1) * t)
        keep = iota((t, t), 1) >= iota((t, t), 0)
        w = w_ref[rows, :]
        r = r_ref[rows, :]
        a_ref[...] = jnp.where(keep, nt(w, r), 0.0)
        pair[...] = jnp.zeros_like(pair)
        if b == 0:
            d1 = d1_ref[...]
            wexp = wexp_ref[rows, :]
            back_ref[rows, :] = wexp * nn(twice(w), stack2(d1))
            gw = nt3(x_ref[rows, :].astype(F32) * wexp, d1)
            state = sin_ref[...]
        else:
            gw = None
            state = first * sin_ref[...] + st0_ref[...]
        gr = nt3(res_ref[rows, :] * fs_ref[rows, :], state)

        def one(i, rows=rows, b=b):
            cols = pl.ds(pl.multiple_of(i * 128, 128), 128)
            xp = x_ref[rows, cols]
            rh, rl = split2(res_ref[rows, cols])
            both = jnp.concatenate([rh, rl], axis=1)
            cc = clsx_ref[rows, cols]
            lane = iota((t, 128), 1)
            out, above, below = None, 0.0, 0.0
            for a in range(per):
                cj = cc[:, a * hw : a * hw + 1]
                ci = crow_ref[pl.ds(i * per + a, 1), rows]
                xx = twice(jnp.where((lane // hw) == a, xp, jnp.zeros_like(xp)))
                e1 = jnp.exp(jnp.minimum(ci - cj[:th], 0.0))
                e2 = jnp.exp(jnp.minimum(ci[:, th:] - cj[th:], 0.0))
                h1, l1 = split2(e1 * a_ref[:th, :])
                h2, l2 = split2(e2 * a_ref[th:, th:])
                p1 = nn(h1, both)
                p2 = nn(h2, both[th:])
                u1 = p1[:, :128] + p1[:, 128:] + nn(l1, rh)
                u2 = p2[:, :128] + p2[:, 128:] + nn(l2, rh[th:])
                u = jnp.concatenate([u1, u2], axis=0)
                out = u if out is None else jnp.where(lane >= a * hw, u, out)
                above += e1 * nt(xx[:th], both)
                below += e2 * nt(xx[th:], both[th:])
            if b == 0:
                out = out + back_ref[rows, cols]
            return cols, out, above, below

        def two(i, _, rows=rows, one=one):
            done = [one(2 * i), one(2 * i + 1)]
            for cols, out, _, _ in done:
                back_ref[rows, cols] = out
            pair[:th, :] += done[0][2] + done[1][2]
            pair[th:, th:] += done[0][3] + done[1][3]
            return 0

        lax.fori_loop(0, width // 256, two, 0)
        ph, plo = split2(jnp.where(keep, pair[...], 0.0))
        gr_ref[rows, :] = gr + tn(ph, w) + tn(plo, w)
        mixed = nn(ph, r) + nn(plo, r)
        gw_ref[rows, :] = mixed if gw is None else mixed + gw


def ready_kernel(x_ref, ls_ref, ld_ref, extra_ref, wexp_ref, xh_ref, xl_ref):
    t = x_ref.shape[0]
    ccol = cum_col(ld_ref[...])
    wexp = spread(
        jnp.exp(ccol[t - 1 : t, :] + extra_ref[...] - ccol + turn(ls_ref[...])), x_ref.shape[1]
    )
    wexp_ref[...] = wexp
    xh_ref[...], xl_ref[...] = split2(x_ref[...].astype(F32) * wexp)


def write_kernel(xh_ref, xl_ref, g_ref, gw0_ref, top_ref, low_ref):
    gh, gl = split2(g_ref[...])
    n = gh.shape[0]
    half = top_ref.shape[0]
    both = nt(xh_ref[...], jnp.concatenate([gh, gl], axis=0))
    out = gw0_ref[...] + both[:, :n] + both[:, n:] + nt(xl_ref[...], gh)
    top_ref[...] = out[:half]
    low_ref[...] = out[half:]


def final_kernel(back_ref, wexp_ref, x_ref, w_ref, g_ref, gi_ref, gls_ref):
    width = x_ref.shape[1]
    heads = gls_ref.shape[0]
    out = back_ref[...] + wexp_ref[...] * nn(twice(w_ref[...]), stack2(g_ref[...]))
    gi_ref[...] = out
    ph, plo = split2(x_ref[...].astype(F32) * out)
    mat = spread_matrix(heads, width)
    gls_ref[...] = nt(mat, ph) + nt(mat, plo)


VM = pl.BlockSpec(memory_space=pltpu.VMEM)


def call(kernel, outs, args, scratch=(), flops=0, in_specs=None, alias=None):
    shapes = [jax.ShapeDtypeStruct(s, d) for s, d in outs]
    moved = sum(a.size * a.dtype.itemsize for a in args)
    return pl.pallas_call(
        kernel,
        out_shape=shapes,
        in_specs=in_specs or [VM] * len(args),
        out_specs=[VM] * len(shapes),
        scratch_shapes=list(scratch),
        input_output_aliases=alias or {},
        cost_estimate=pl.CostEstimate(flops=flops, bytes_accessed=moved, transcendentals=0),
        compiler_params=pltpu.CompilerParams(vmem_limit_bytes=8 * 2**20),
    )(*args)


def decode(coded, rows, weight):
    power = coded[rows : rows + 1].astype(F32)
    return coded[:rows].astype(F32) * (jnp.exp2(power - 12.0) * weight)


def on_device(q, k, v, x, wr, rd, ls, ld):
    t = q.shape[0]
    count = lax.axis_size("seq")
    tp = lax.axis_size("tp")
    chips = count // 2
    index = lax.axis_index("seq")
    core, chip = index % 2, index // 2
    heads = ls.shape[0]
    hh = heads // 2
    n = wr.shape[1]
    hc = x.shape[1] // 2
    qc = q.shape[1] // 2
    kvh = k.shape[1] // HD
    kw = k.shape[1] // 2 if kvh % 2 == 0 else k.shape[1]

    def swap(a, bits):
        return lax.ppermute(a, "seq", [(i, i ^ bits) for i in range(count)])

    def half(a, which, width, axis=1):
        return lax.dynamic_slice_in_dim(a, which * width, width, axis=axis)

    def joined(own, other, axis=0):
        a = jnp.where(core == 0, own, other)
        b = jnp.where(core == 0, other, own)
        return jnp.concatenate([a, b], axis=axis)

    def near(a):
        got = {}
        for b in range(chips.bit_length() - 1):
            got[1 << b] = swap(a, 2 << b)
        return got

    def relay(got, token):
        got = dict(got)
        for d in range(1, chips):
            if d not in got:
                low = d & -d
                held, _ = lax.optimization_barrier((got[d - low], token))
                need = [c for c in range(chips) if c ^ d < c or c ^ low ^ d < c ^ low]
                pairs = [(2 * c + k, 2 * (c ^ low) + k) for c in need for k in (0, 1)]
                got[d] = lax.ppermute(held, "seq", pairs)
        return [got[d] for d in range(1, chips)]

    def kv_half(which):
        if kvh % 2 == 0:
            return jnp.concatenate([half(k, which, kw), half(v, which, kw)], axis=1)
        return jnp.concatenate([k, v], axis=1)

    kv = joined(kv_half(core), swap(kv_half(1 - core), 1))
    keys_near = near(kv)
    x1, q1, wr1, rd1, _ = lax.optimization_barrier((x, q, wr, rd, kv))
    rates = swap(jnp.concatenate([ls, ld], axis=0), 1)
    lsc = joined(half(ls, core, hh, 0), half(rates, core, hh, 0), 1)
    ldc = joined(half(ld, core, hh, 0), half(rates[heads:], core, hh, 0), 1)
    mates = swap(jnp.concatenate([half(x1, 1 - core, hc), wr1, rd1], axis=1), 1)
    xc = joined(half(x1, core, hc), mates[:, :hc])
    wc = joined(wr1, mates[:, hc : hc + n])
    rc = joined(rd1, mates[:, hc + n :])
    qg = joined(half(q1, core, qc), swap(half(q1, 1 - core, qc), 1))

    mm = 2 * 2 * t * hc * n
    code = ((n + 16, hc), F32)
    st0, coded, wexpc = call(
        state_kernel, [((n, hc), F32), code, ((2 * t, hc), F32)], (xc, wc, lsc, ldc),
        flops=4 * mm,
    )

    def state_stage(coded, bit):
        return swap(coded.astype(F16), 2 << bit).astype(F32)

    stages = [state_stage(coded, 0)] if chips > 1 else []
    qh = qc // HD
    carry = [((qc, 2 * t), F32), ((qh, 2 * t), F32), ((qh, 2 * t), F32)]
    qs, *soft = call(
        own_kernel, [((2 * t, 2 * qc), BF16), *carry], (qg, kv),
        scratch=[pltpu.VMEM((2 * t, 2 * HD), BF16), pltpu.VMEM((HD, 2 * t), BF16), pltpu.VMEM((t, t), F32)]
        + [pltpu.VMEM((t, t), F32), pltpu.VMEM((2 * t, t), F32)] * 2,
        flops=4 * (2 * t) ** 2 * qc,
    )
    ybase, fs, clsx, crow = call(
        local_kernel,
        [((2 * t, hc), F32), ((2 * t, hc), F32), ((2 * t, hc), F32), ((hh, 2 * t), F32)],
        (xc, wc, rc, lsc, ldc, st0),
        scratch=[pltpu.VMEM((t, hc), F32), pltpu.VMEM((hh, t), F32), pltpu.VMEM((t, t), F32)],
        flops=8 * mm,
    )
    for bit in range(1, chips.bit_length() - 1):
        flag = jnp.reshape((chip >> (bit - 1)) % 2, (1,)).astype(jnp.int32)
        (coded,) = call(
            functools.partial(merge_kernel, group=1 << (bit - 1)), [code], (flag, coded, stages[-1]),
            in_specs=[pl.BlockSpec(memory_space=pltpu.SMEM), VM, VM],
        )
        stages.append(state_stage(coded, bit))
    decays = {}
    for bit, got in enumerate(stages):
        for m in range(1 << bit):
            at = n + 1 + 3 * m
            decays[(1 << bit) + m] = jnp.sum(got[at : at + 3], axis=0, keepdims=True)

    def between(low, high, most):
        out = jnp.zeros((1, hc), F32)
        for m in range(1, most):
            at = chip ^ m
            out += jnp.where((at > low) & (at < high), decays[m], 0.0)
        return out

    incoming = jnp.zeros((n, hc), F32)
    for bit, got in enumerate(stages):
        fade = jnp.exp(between(-1, chip, 1 << bit))
        incoming += decode(got, n, jnp.where((chip >> bit) % 2 == 1, fade, 0.0))
    far = relay(keys_near, soft[1])

    def combine(got):
        out = 0.0
        for d, g in enumerate(got, 1):
            fade = jnp.exp(between(chip, chip ^ d, chips))
            out += decode(g, n, jnp.where((chip ^ d) > chip, fade, 0.0))
        return out

    for d, keys in enumerate(far, 1):
        flag = jnp.reshape((chip ^ d) < chip, (1,)).astype(jnp.int32)
        soft = call(
            far_kernel, carry, (flag, qs, keys, *soft),
            scratch=[pltpu.VMEM((2 * t, 2 * HD), BF16), pltpu.VMEM((HD, 2 * t), BF16)] + [pltpu.VMEM((2 * t, 2 * t), F32)] * 2,
            flops=4 * (2 * t) ** 2 * qc, alias={3: 0, 4: 1, 5: 2},
            in_specs=[pl.BlockSpec(memory_space=pltpu.SMEM)] + [VM] * 5,
        )
    res, d1, dcode = call(
        residual_kernel, [((2 * t, hc), F32), ((n, hc), F32), code],
        (ybase, soft[0], soft[2], rc, fs, incoming), flops=8 * mm,
    )
    sent = dcode.astype(F16)
    coming = [swap(sent, 2 * d) for d in range(1, chips)]
    back, gw, gr = call(
        back_kernel, [((2 * t, hc), F32), ((2 * t, n), F32), ((2 * t, n), F32)],
        (res, xc, wc, rc, clsx, crow, fs, wexpc, incoming, st0, d1),
        scratch=[pltpu.VMEM((t, t), F32), pltpu.VMEM((t, t), F32)],
        flops=16 * mm,
    )
    other_total = jnp.sum(rates[heads:], axis=1)[None, :]
    extra = jnp.where(core == 0, other_total, 0.0)
    wexp, xh, xl = call(
        ready_kernel, [((t, 2 * hc), F32), ((t, 2 * hc), BF16), ((t, 2 * hc), BF16)],
        (x, ls, ld, extra), flops=2 * mm,
    )

    def home(a):
        return half(a, core, t, 0), swap(half(a, 1 - core, t, 0), 1)

    def tp_sum(parts):
        bits = tp.bit_length() - 1
        parts = list(parts)
        for step in range(bits):
            sent = [
                lax.ppermute(a, "tp", [(i, i ^ (1 << ((step + k) % bits))) for i in range(tp)])
                for k, a in enumerate(parts)
            ]
            parts = [a + b for a, b in zip(parts, sent)]
        return parts

    back_all = joined(*home(back), 1)
    own, other = home(jnp.concatenate([gw, gr], axis=1))
    grads = own + other
    gw0, gr0 = grads[:, :n], grads[:, n:]
    grad_read = jnp.concatenate(tp_sum([gr0[: t // 2], gr0[t // 2 :]]), axis=0)
    arriving = combine(coming)
    arrived = joined(arriving, swap(arriving, 1), 1)
    gwp = call(write_kernel, [((t // 2, n), F32)] * 2, (xh, xl, arrived, gw0), flops=4 * mm)
    grad_write = jnp.concatenate(tp_sum(gwp), axis=0)
    gi, gls = call(
        final_kernel, [((t, 2 * hc), F32), ((heads, t), F32)], (back_all, wexp, x, wr, arrived),
        flops=8 * mm,
    )
    return (gi, grad_write, grad_read, gls)


def solution(mesh):
    in_specs = (
        P("seq", "tp"), P("seq", "tp"), P("seq", "tp"), P("seq", "tp"),
        P("seq", None), P("seq", None), P("tp", "seq"), P("tp", "seq"),
    )
    out_specs = (P("seq", "tp"), P("seq", None), P("seq", None), P("tp", "seq"))
    return jax.shard_map(
        on_device, mesh=mesh, in_specs=in_specs, out_specs=out_specs, check_vma=False
    )
```

```python
import functools
import math

import jax
import jax.numpy as jnp
from jax import lax
from jax.experimental import pallas as pl
from jax.experimental.pallas import tpu as pltpu
from jax.sharding import PartitionSpec as P


HD = 128
F32, BF16, F16 = jnp.float32, jnp.bfloat16, jnp.float16


def nn(a, b):
    return lax.dot_general(a, b, (((1,), (0,)), ((), ())), preferred_element_type=F32)


def nt(a, b):
    return lax.dot_general(a, b, (((1,), (1,)), ((), ())), preferred_element_type=F32)


def tn(a, b):
    return lax.dot_general(a, b, (((0,), (0,)), ((), ())), preferred_element_type=F32)


def split2(a):
    hi = a.astype(BF16)
    return hi, (a - hi.astype(F32)).astype(BF16)


def split3(a):
    hi = a.astype(BF16)
    rest = a - hi.astype(F32)
    mid = rest.astype(BF16)
    return hi, mid, (rest - mid.astype(F32)).astype(BF16)


def iota(shape, dim):
    return lax.broadcasted_iota(jnp.int32, shape, dim)


def lower(t):
    return (iota((t, t), 0) >= iota((t, t), 1)).astype(BF16)


def spread_matrix(heads, width, times=1):
    row = iota((times * heads, width), 0) % heads
    return (iota((times * heads, width), 1) // (width // heads) == row).astype(BF16)


def spread(col, width):
    pieces = [p.astype(F32) for p in split3(col)]
    stacked = jnp.concatenate(pieces, axis=1).astype(BF16)
    return nn(stacked, spread_matrix(col.shape[1], width, 3))


def stack2(a):
    return jnp.concatenate(split2(a), axis=0)


def twice(a):
    return jnp.concatenate([a, a], axis=1)


def nt3(a, b):
    ah, al = split2(a)
    bh, bl = split2(b)
    both = nt(ah, jnp.concatenate([bh, bl], axis=0))
    half = both.shape[1] // 2
    return both[:, :half] + both[:, half:] + nt(al, bh)


def code_rows(state, extra):
    top = jnp.max(jnp.abs(state), axis=0, keepdims=True)
    power = jnp.ceil(jnp.log2(jnp.maximum(top, 1e-30)))
    used = sum(e.shape[0] for e in extra)
    rest = jnp.zeros((15 - used, state.shape[1]), F32)
    return state * jnp.exp2(12.0 - power), jnp.concatenate([power, *extra, rest], axis=0)


def spread_row(row, width):
    return spread(jnp.broadcast_to(row, (8, row.shape[1])), width)[0:1]


def cum_col(ld):
    tri = lower(ld.shape[1])
    a, b, c = split3(ld)
    return nt(tri, a) + nt(tri, b) + nt(tri, c)


def cum_row(ld):
    tri = lower(ld.shape[1])
    a, b, c = split3(ld)
    return nt(a, tri) + nt(b, tri) + nt(c, tri)


def turn(rows):
    t = rows.shape[1]
    eye = (iota((t, t), 0) == iota((t, t), 1)).astype(BF16)
    a, b, c = split3(rows)
    return nt(eye, a) + nt(eye, b) + nt(eye, c)


def state_kernel(x_ref, w_ref, ls_ref, ld_ref, st0_ref, coded_ref, wexp_ref):
    t = x_ref.shape[0] // 2
    width = x_ref.shape[1]
    n = w_ref.shape[1]
    parts, tots = [], []
    for b in (0, 1):
        rows = slice(b * t, (b + 1) * t)
        ccol = cum_col(ld_ref[:, rows])
        tot = ccol[t - 1 : t, :]
        wexp = spread(jnp.exp(tot - ccol + turn(ls_ref[:, rows])), width)
        wexp_ref[rows, :] = wexp
        hi, lo = split2(x_ref[rows, :].astype(F32) * wexp)
        parts.append(tn(w_ref[rows, :], hi) + tn(w_ref[rows, :], lo))
        tots.append(tot)
    st0_ref[...] = parts[0]
    state = spread_row(jnp.exp(tots[1]), width) * parts[0] + parts[1]
    pieces = [p.astype(F32) for p in split3(spread_row(tots[0] + tots[1], width))]
    coded_ref[:n, :], coded_ref[n:, :] = code_rows(state, pieces)


def merge_kernel(flag, own_ref, got_ref, out_ref, *, group):
    n = own_ref.shape[0] - 16
    used = 3 * group
    own_rows = own_ref[n + 1 : n + 1 + used, :]
    got_rows = got_ref[n + 1 : n + 1 + used, :]
    own = own_ref[:n, :] * jnp.exp2(own_ref[n : n + 1, :] - 12.0)
    got = got_ref[:n, :] * jnp.exp2(got_ref[n : n + 1, :] - 12.0)
    own_fade = jnp.exp(jnp.sum(own_rows, axis=0, keepdims=True))
    got_fade = jnp.exp(jnp.sum(got_rows, axis=0, keepdims=True))
    earlier = flag[0] == 1
    merged = own * jnp.where(earlier, 1.0, got_fade) + got * jnp.where(earlier, own_fade, 1.0)
    out_ref[:n, :], out_ref[n:, :] = code_rows(merged, [own_rows, got_rows])


def local_kernel(
    x_ref, w_ref, r_ref, ls_ref, ld_ref, st0_ref,
    y_ref, fs_ref, clsx_ref, crow_ref, cexp, clsrow, a_ref,
):
    t = x_ref.shape[0] // 2
    th = t // 2
    width = x_ref.shape[1]
    heads = ls_ref.shape[0]
    hw = width // heads
    per = 128 // hw
    for b in (0, 1):
        rows = slice(b * t, (b + 1) * t)
        ccol = cum_col(ld_ref[:, rows])
        cexp[...] = spread(ccol, width)
        fs = spread(jnp.exp(ccol), width)
        fs_ref[rows, :] = fs
        clsx_ref[rows, :] = spread(ccol - turn(ls_ref[:, rows]), width)
        crow = cum_row(ld_ref[:, rows])
        crow_ref[:, rows] = crow
        clsrow[...] = crow - ls_ref[:, rows]
        keep = iota((t, t), 0) >= iota((t, t), 1)
        a_ref[...] = jnp.where(keep, nt(r_ref[rows, :], w_ref[rows, :]), 0.0)
        if b == 1:
            y_ref[rows, :] = fs * nn(twice(r_ref[rows, :]), stack2(st0_ref[...]))

        def one(i, rows=rows, b=b):
            cols = pl.ds(pl.multiple_of(i * 128, 128), 128)
            xp = x_ref[rows, cols]
            xtop = jnp.concatenate([xp[:th], xp[:th]], axis=0)
            cc = cexp[:, cols]
            lane = iota((t, 128), 1)
            out = None
            for a in range(per):
                ci = cc[:, a * hw : a * hw + 1]
                cj = clsrow[pl.ds(i * per + a, 1), :]
                top = jnp.exp(jnp.minimum(ci[:th] - cj[:, :th], 0.0)) * a_ref[:th, :th]
                bot = jnp.exp(jnp.minimum(ci[th:] - cj, 0.0)) * a_ref[th:, :]
                yt = nn(jnp.concatenate(split2(top), axis=1), xtop)
                b1, b2 = split2(bot)
                yb = nn(b1, xp) + nn(b2, xp)
                mine = jnp.concatenate([yt, yb], axis=0)
                out = mine if out is None else jnp.where(lane >= a * hw, mine, out)
            if b == 1:
                out = out + y_ref[rows, cols]
            return cols, out

        def two(i, _, rows=rows, one=one):
            done = [one(2 * i), one(2 * i + 1)]
            for cols, out in done:
                y_ref[rows, cols] = out
            return 0

        lax.fori_loop(0, width // 256, two, 0)


def keys_twice(kv_ref, g, kw):
    k = kv_ref[:, g * HD : (g + 1) * HD]
    return jnp.concatenate([k, k], axis=1), kv_ref[:, kw + g * HD : kw + (g + 1) * HD].T


def own_kernel(q_ref, kv_ref, qs_ref, acc_ref, m_ref, l_ref, k2, vt, bias, s0a, s1a, s0b, s1b):
    t = q_ref.shape[0] // 2
    kw = kv_ref.shape[1] // 2
    kvh = kw // HD
    group = q_ref.shape[1] // HD // kvh
    scale = 1.0 / math.sqrt(HD)
    bias[...] = jnp.where(iota((t, t), 0) <= iota((t, t), 1), 0.0, -1e30)
    for g in range(kvh):
        k2[...], vt[...] = keys_twice(kv_ref, g, kw)

        def scores(h, s0, s1, g=g):
            at = g * group + h
            q = q_ref[:, pl.ds(pl.multiple_of(at * HD, HD), HD)].astype(F32) * scale
            both = jnp.concatenate(split2(q), axis=1)
            qs_ref[:, pl.ds(pl.multiple_of(at * 2 * HD, 2 * HD), 2 * HD)] = both
            s0[...] = nt(k2[:t, :], both[:t]) + bias[...]
            s1[:t, :] = nt(k2[:t, :], both[t:])
            s1[t:, :] = nt(k2[t:, :], both[t:]) + bias[...]

        def soft(h, s0, s1, g=g):
            at = g * group + h
            cols = pl.ds(pl.multiple_of(at * HD, HD), HD)
            for b, s_ref in ((0, s0), (1, s1)):
                rows = slice(b * t, (b + 1) * t)
                s = s_ref[...]
                top = jnp.max(s, axis=0, keepdims=True)
                e = jnp.exp(s - top)
                m_ref[pl.ds(at, 1), rows] = top
                l_ref[pl.ds(at, 1), rows] = jnp.sum(e, axis=0, keepdims=True)
                acc_ref[cols, rows] = nn(vt[:, : (b + 1) * t], e.astype(BF16))

        scores(0, s0a, s1a)

        def pair(i, _):
            scores(2 * i + 1, s0b, s1b)
            soft(2 * i, s0a, s1a)
            scores(jnp.minimum(2 * i + 2, group - 1), s0a, s1a)
            soft(2 * i + 1, s0b, s1b)
            return 0

        lax.fori_loop(0, group // 2, pair, 0)


def far_kernel(flag, qs_ref, kv_ref, acc_in, m_in, l_in, acc_ref, m_ref, l_ref, k2, vt, sa, sb):
    t = qs_ref.shape[0] // 2
    kw = kv_ref.shape[1] // 2
    kvh = kw // HD
    group = qs_ref.shape[1] // (2 * HD) // kvh

    @pl.when(flag[0] == 0)
    def _():
        acc_ref[...] = acc_in[...]
        m_ref[...] = m_in[...]
        l_ref[...] = l_in[...]

    @pl.when(flag[0] == 1)
    def _():
        for g in range(kvh):
            k2[...], vt[...] = keys_twice(kv_ref, g, kw)

            def scores(h, s_ref, g=g):
                at = g * group + h
                s_ref[...] = nt(k2[...], qs_ref[:, pl.ds(pl.multiple_of(at * 2 * HD, 2 * HD), 2 * HD)])

            def soft(h, s_ref, g=g):
                at = g * group + h
                cols = pl.ds(pl.multiple_of(at * HD, HD), HD)
                row = pl.ds(at, 1)
                for b in (0, 1):
                    rows = slice(b * t, (b + 1) * t)
                    s = s_ref[:, rows]
                    old = m_in[row, rows]
                    new = jnp.maximum(old, jnp.max(s, axis=0, keepdims=True))
                    e = jnp.exp(s - new)
                    fade = jnp.exp(old - new)
                    m_ref[row, rows] = new
                    l_ref[row, rows] = l_in[row, rows] * fade + jnp.sum(e, axis=0, keepdims=True)
                    acc_ref[cols, rows] = acc_in[cols, rows] * fade + nn(vt[...], e.astype(BF16))

            scores(0, sa)

            def pair(i, _):
                scores(2 * i + 1, sb)
                soft(2 * i, sa)
                scores(jnp.minimum(2 * i + 2, group - 1), sa)
                soft(2 * i + 1, sb)
                return 0

            lax.fori_loop(0, group // 2, pair, 0)


def residual_kernel(y_ref, acc_ref, l_ref, r_ref, fs_ref, sin_ref, res_ref, d1_ref, coded_ref):
    t = y_ref.shape[0] // 2
    width = y_ref.shape[1]
    n = r_ref.shape[1]
    state = sin_ref[...]
    first = fs_ref[t - 1 : t, :]
    parts = []
    for b in (0, 1):
        rows = slice(b * t, (b + 1) * t)
        fs = fs_ref[rows, :]
        r = r_ref[rows, :]
        heads = [
            (acc_ref[h * HD : (h + 1) * HD, rows] / l_ref[h : h + 1, rows]).astype(BF16).T
            for h in range(width // HD)
        ]
        teach = jnp.concatenate(heads, axis=1).astype(F32)
        res = y_ref[rows, :] + fs * nn(twice(r), stack2(state * first if b else state)) - teach
        res_ref[rows, :] = res
        hi, lo = split2(res * fs)
        parts.append(tn(r, hi) + tn(r, lo))
    d1_ref[...] = parts[1]
    coded_ref[:n, :], coded_ref[n:, :] = code_rows(parts[0] + first * parts[1], [])


def back_kernel(
    res_ref, x_ref, w_ref, r_ref, clsx_ref, crow_ref, fs_ref, wexp_ref, sin_ref, st0_ref, d1_ref,
    back_ref, shared_ref, a_ref, pair,
):
    t = x_ref.shape[0] // 2
    th = t // 2
    width = x_ref.shape[1]
    heads = crow_ref.shape[0]
    hw = width // heads
    per = 128 // hw
    first = fs_ref[t - 1 : t, :]
    for b in (0, 1):
        rows = slice(b * t, (b + 1) * t)
        keep = iota((t, t), 1) >= iota((t, t), 0)
        w = w_ref[rows, :]
        r = r_ref[rows, :]
        a_ref[...] = jnp.where(keep, nt(w, r), 0.0)
        pair[...] = jnp.zeros_like(pair)
        if b == 0:
            d1 = d1_ref[...]
            wexp = wexp_ref[rows, :]
            back_ref[rows, :] = wexp * nn(twice(w), stack2(d1))
            gw = nt3(x_ref[rows, :].astype(F32) * wexp, d1)
            state = sin_ref[...]
        else:
            gw = None
            state = first * sin_ref[...] + st0_ref[...]
        gr = nt3(res_ref[rows, :] * fs_ref[rows, :], state)

        def one(i, rows=rows, b=b):
            cols = pl.ds(pl.multiple_of(i * 128, 128), 128)
            xp = x_ref[rows, cols]
            rh, rl = split2(res_ref[rows, cols])
            both = jnp.concatenate([rh, rl], axis=1)
            cc = clsx_ref[rows, cols]
            lane = iota((t, 128), 1)
            out, above, below = None, 0.0, 0.0
            for a in range(per):
                cj = cc[:, a * hw : a * hw + 1]
                ci = crow_ref[pl.ds(i * per + a, 1), rows]
                xx = twice(jnp.where((lane // hw) == a, xp, jnp.zeros_like(xp)))
                e1 = jnp.exp(jnp.minimum(ci - cj[:th], 0.0))
                e2 = jnp.exp(jnp.minimum(ci[:, th:] - cj[th:], 0.0))
                h1, l1 = split2(e1 * a_ref[:th, :])
                h2, l2 = split2(e2 * a_ref[th:, th:])
                p1 = nn(h1, both)
                p2 = nn(h2, both[th:])
                u1 = p1[:, :128] + p1[:, 128:] + nn(l1, rh)
                u2 = p2[:, :128] + p2[:, 128:] + nn(l2, rh[th:])
                u = jnp.concatenate([u1, u2], axis=0)
                out = u if out is None else jnp.where(lane >= a * hw, u, out)
                above += e1 * nt(xx[:th], both)
                below += e2 * nt(xx[th:], both[th:])
            if b == 0:
                out = out + back_ref[rows, cols]
            return cols, out, above, below

        def two(i, _, rows=rows, one=one):
            done = [one(2 * i), one(2 * i + 1)]
            for cols, out, _, _ in done:
                back_ref[rows, cols] = out
            pair[:th, :] += done[0][2] + done[1][2]
            pair[th:, th:] += done[0][3] + done[1][3]
            return 0

        lax.fori_loop(0, width // 256, two, 0)
        ph, plo = split2(jnp.where(keep, pair[...], 0.0))
        n = w.shape[1]
        mixed = nn(ph, r) + nn(plo, r)
        shared_ref[rows, :n] = mixed if gw is None else mixed + gw
        shared_ref[rows, n:] = gr + tn(ph, w) + tn(plo, w)


def ready_kernel(x_ref, ls_ref, ld_ref, extra_ref, wexp_ref, xh_ref, xl_ref):
    t = x_ref.shape[0]
    ccol = cum_col(ld_ref[...])
    wexp = spread(
        jnp.exp(ccol[t - 1 : t, :] + extra_ref[...] - ccol + turn(ls_ref[...])), x_ref.shape[1]
    )
    wexp_ref[...] = wexp
    xh_ref[...], xl_ref[...] = split2(x_ref[...].astype(F32) * wexp)


def write_kernel(xh_ref, xl_ref, g_ref, gw0_ref, top_ref, low_ref):
    gh, gl = split2(g_ref[...])
    n = gh.shape[0]
    half = top_ref.shape[0]
    both = nt(xh_ref[...], jnp.concatenate([gh, gl], axis=0))
    out = gw0_ref[...] + both[:, :n] + both[:, n:] + nt(xl_ref[...], gh)
    top_ref[...] = out[:half]
    low_ref[...] = out[half:]


def final_kernel(back_ref, wexp_ref, x_ref, w_ref, g_ref, gi_ref, gls_ref):
    width = x_ref.shape[1]
    heads = gls_ref.shape[0]
    out = back_ref[...] + wexp_ref[...] * nn(twice(w_ref[...]), stack2(g_ref[...]))
    gi_ref[...] = out
    ph, plo = split2(x_ref[...].astype(F32) * out)
    mat = spread_matrix(heads, width)
    gls_ref[...] = nt(mat, ph) + nt(mat, plo)


VM = pl.BlockSpec(memory_space=pltpu.VMEM)


def call(kernel, outs, args, scratch=(), flops=0, in_specs=None, alias=None):
    shapes = [jax.ShapeDtypeStruct(s, d) for s, d in outs]
    moved = sum(a.size * a.dtype.itemsize for a in args)
    return pl.pallas_call(
        kernel,
        out_shape=shapes,
        in_specs=in_specs or [VM] * len(args),
        out_specs=[VM] * len(shapes),
        scratch_shapes=list(scratch),
        input_output_aliases=alias or {},
        cost_estimate=pl.CostEstimate(flops=flops, bytes_accessed=moved, transcendentals=0),
        compiler_params=pltpu.CompilerParams(vmem_limit_bytes=8 * 2**20),
    )(*args)


def decode(coded, rows, weight):
    power = coded[rows : rows + 1].astype(F32)
    return coded[:rows].astype(F32) * (jnp.exp2(power - 12.0) * weight)


def on_device(q, k, v, x, wr, rd, ls, ld):
    t = q.shape[0]
    count = lax.axis_size("seq")
    tp = lax.axis_size("tp")
    chips = count // 2
    index = lax.axis_index("seq")
    core, chip = index % 2, index // 2
    heads = ls.shape[0]
    hh = heads // 2
    n = wr.shape[1]
    hc = x.shape[1] // 2
    qc = q.shape[1] // 2
    kvh = k.shape[1] // HD
    kw = k.shape[1] // 2 if kvh % 2 == 0 else k.shape[1]

    def swap(a, bits):
        return lax.ppermute(a, "seq", [(i, i ^ bits) for i in range(count)])

    def half(a, which, width, axis=1):
        return lax.dynamic_slice_in_dim(a, which * width, width, axis=axis)

    def joined(own, other, axis=0):
        a = jnp.where(core == 0, own, other)
        b = jnp.where(core == 0, other, own)
        return jnp.concatenate([a, b], axis=axis)

    def near(a):
        got = {}
        for b in range(chips.bit_length() - 1):
            got[1 << b] = swap(a, 2 << b)
        return got

    def relay(got, token):
        got = dict(got)
        for d in range(1, chips):
            if d not in got:
                low = d & -d
                held, _ = lax.optimization_barrier((got[d - low], token))
                need = [c for c in range(chips) if c ^ d < c or c ^ low ^ d < c ^ low]
                pairs = [(2 * c + k, 2 * (c ^ low) + k) for c in need for k in (0, 1)]
                got[d] = lax.ppermute(held, "seq", pairs)
        return [got[d] for d in range(1, chips)]

    def kv_half(which):
        if kvh % 2 == 0:
            return jnp.concatenate([half(k, which, kw), half(v, which, kw)], axis=1)
        return jnp.concatenate([k, v], axis=1)

    kv = joined(kv_half(core), swap(kv_half(1 - core), 1))
    keys_near = near(kv)
    x1, q1, wr1, rd1, ls1, ld1, _ = lax.optimization_barrier((x, q, wr, rd, ls, ld, kv))
    rates = swap(jnp.concatenate([ls1, ld1], axis=0), 1)
    lsc = joined(half(ls1, core, hh, 0), half(rates, core, hh, 0), 1)
    ldc = joined(half(ld1, core, hh, 0), half(rates[heads:], core, hh, 0), 1)
    mates = swap(jnp.concatenate([half(x1, 1 - core, hc), wr1, rd1], axis=1), 1)
    xc = joined(half(x1, core, hc), mates[:, :hc])
    wc = joined(wr1, mates[:, hc : hc + n])
    rc = joined(rd1, mates[:, hc + n :])
    qg = joined(half(q1, core, qc), swap(half(q1, 1 - core, qc), 1))

    mm = 2 * 2 * t * hc * n
    code = ((n + 16, hc), F32)
    st0, coded, wexpc = call(
        state_kernel, [((n, hc), F32), code, ((2 * t, hc), F32)], (xc, wc, lsc, ldc),
        flops=4 * mm,
    )

    def state_stage(coded, bit):
        return swap(coded.astype(F16), 2 << bit).astype(F32)

    stages = [state_stage(coded, 0)] if chips > 1 else []
    qh = qc // HD
    carry = [((qc, 2 * t), F32), ((qh, 2 * t), F32), ((qh, 2 * t), F32)]
    qs, *soft = call(
        own_kernel, [((2 * t, 2 * qc), BF16), *carry], (qg, kv),
        scratch=[pltpu.VMEM((2 * t, 2 * HD), BF16), pltpu.VMEM((HD, 2 * t), BF16), pltpu.VMEM((t, t), F32)]
        + [pltpu.VMEM((t, t), F32), pltpu.VMEM((2 * t, t), F32)] * 2,
        flops=4 * (2 * t) ** 2 * qc,
    )
    ybase, fs, clsx, crow = call(
        local_kernel,
        [((2 * t, hc), F32), ((2 * t, hc), F32), ((2 * t, hc), F32), ((hh, 2 * t), F32)],
        (xc, wc, rc, lsc, ldc, st0),
        scratch=[pltpu.VMEM((t, hc), F32), pltpu.VMEM((hh, t), F32), pltpu.VMEM((t, t), F32)],
        flops=8 * mm,
    )
    for bit in range(1, chips.bit_length() - 1):
        flag = jnp.reshape((chip >> (bit - 1)) % 2, (1,)).astype(jnp.int32)
        (coded,) = call(
            functools.partial(merge_kernel, group=1 << (bit - 1)), [code], (flag, coded, stages[-1]),
            in_specs=[pl.BlockSpec(memory_space=pltpu.SMEM), VM, VM],
        )
        stages.append(state_stage(coded, bit))
    decays = {}
    for bit, got in enumerate(stages):
        for m in range(1 << bit):
            at = n + 1 + 3 * m
            decays[(1 << bit) + m] = jnp.sum(got[at : at + 3], axis=0, keepdims=True)

    def between(low, high, most):
        out = jnp.zeros((1, hc), F32)
        for m in range(1, most):
            at = chip ^ m
            out += jnp.where((at > low) & (at < high), decays[m], 0.0)
        return out

    incoming = jnp.zeros((n, hc), F32)
    for bit, got in enumerate(stages):
        fade = jnp.exp(between(-1, chip, 1 << bit))
        incoming += decode(got, n, jnp.where((chip >> bit) % 2 == 1, fade, 0.0))
    far = relay(keys_near, soft[1])

    def combine(got):
        flat = jnp.concatenate([g.astype(F32) for g in got], axis=0)
        flat = lax.optimization_barrier(flat)
        out = 0.0
        for d in range(1, chips):
            fade = jnp.exp(between(chip, chip ^ d, chips))
            at = (d - 1) * (n + 16)
            out += decode(flat[at : at + n + 16], n, jnp.where((chip ^ d) > chip, fade, 0.0))
        return out

    for d, keys in enumerate(far, 1):
        flag = jnp.reshape((chip ^ d) < chip, (1,)).astype(jnp.int32)
        soft = call(
            far_kernel, carry, (flag, qs, keys, *soft),
            scratch=[pltpu.VMEM((2 * t, 2 * HD), BF16), pltpu.VMEM((HD, 2 * t), BF16)] + [pltpu.VMEM((2 * t, 2 * t), F32)] * 2,
            flops=4 * (2 * t) ** 2 * qc, alias={3: 0, 4: 1, 5: 2},
            in_specs=[pl.BlockSpec(memory_space=pltpu.SMEM)] + [VM] * 5,
        )
    res, d1, dcode = call(
        residual_kernel, [((2 * t, hc), F32), ((n, hc), F32), code],
        (ybase, soft[0], soft[2], rc, fs, incoming), flops=8 * mm,
    )
    sent = dcode.astype(F16)
    coming = []
    for d in range(1, chips):
        coming.append(swap(sent, 2 * d))
    back, shared = call(
        back_kernel, [((2 * t, hc), F32), ((2 * t, 2 * n), F32)],
        (res, xc, wc, rc, clsx, crow, fs, wexpc, incoming, st0, d1),
        scratch=[pltpu.VMEM((t, t), F32), pltpu.VMEM((t, t), F32)],
        flops=16 * mm,
    )
    other_total = jnp.sum(rates[heads:], axis=1)[None, :]
    extra = jnp.where(core == 0, other_total, 0.0)
    wexp, xh, xl = call(
        ready_kernel, [((t, 2 * hc), F32), ((t, 2 * hc), BF16), ((t, 2 * hc), BF16)],
        (x, ls, ld, extra), flops=2 * mm,
    )

    def home(a):
        return half(a, core, t, 0), swap(half(a, 1 - core, t, 0), 1)

    def tp_sum(parts):
        bits = tp.bit_length() - 1
        parts = list(parts)
        for step in range(bits):
            sent = [
                lax.ppermute(a, "tp", [(i, i ^ (1 << ((step + k) % bits))) for i in range(tp)])
                for k, a in enumerate(parts)
            ]
            parts = [a + b for a, b in zip(parts, sent)]
        return parts

    back_all = joined(*home(back), 1)
    own, other = home(shared)
    grads = own + other
    gw0, gr0 = grads[:, :n], grads[:, n:]
    grad_read = jnp.concatenate(tp_sum([gr0[: t // 2], gr0[t // 2 :]]), axis=0)
    arriving = combine(coming)
    arrived = joined(arriving, swap(arriving, 1), 1)
    gwp = call(write_kernel, [((t // 2, n), F32)] * 2, (xh, xl, arrived, gw0), flops=4 * mm)
    grad_write = jnp.concatenate(tp_sum(gwp), axis=0)
    gi, gls = call(
        final_kernel, [((t, 2 * hc), F32), ((heads, t), F32)], (back_all, wexp, x, wr, arrived),
        flops=8 * mm,
    )
    return (gi, grad_write, grad_read, gls)


def solution(mesh):
    in_specs = (
        P("seq", "tp"), P("seq", "tp"), P("seq", "tp"), P("seq", "tp"),
        P("seq", None), P("seq", None), P("tp", "seq"), P("tp", "seq"),
    )
    out_specs = (P("seq", "tp"), P("seq", None), P("seq", None), P("tp", "seq"))
    return jax.shard_map(
        on_device, mesh=mesh, in_specs=in_specs, out_specs=out_specs, check_vma=False
    )
```

```python
import functools
import math

import jax
import jax.numpy as jnp
from jax import lax
from jax.experimental import pallas as pl
from jax.experimental.pallas import tpu as pltpu
from jax.sharding import PartitionSpec as P


HD = 128
F32, BF16, F16 = jnp.float32, jnp.bfloat16, jnp.float16


def nn(a, b):
    return lax.dot_general(a, b, (((1,), (0,)), ((), ())), preferred_element_type=F32)


def nt(a, b):
    return lax.dot_general(a, b, (((1,), (1,)), ((), ())), preferred_element_type=F32)


def tn(a, b):
    return lax.dot_general(a, b, (((0,), (0,)), ((), ())), preferred_element_type=F32)


def split2(a):
    hi = a.astype(BF16)
    return hi, (a - hi.astype(F32)).astype(BF16)


def split3(a):
    hi = a.astype(BF16)
    rest = a - hi.astype(F32)
    mid = rest.astype(BF16)
    return hi, mid, (rest - mid.astype(F32)).astype(BF16)


def iota(shape, dim):
    return lax.broadcasted_iota(jnp.int32, shape, dim)


def lower(t):
    return (iota((t, t), 0) >= iota((t, t), 1)).astype(BF16)


def spread_matrix(heads, width, times=1):
    row = iota((times * heads, width), 0) % heads
    return (iota((times * heads, width), 1) // (width // heads) == row).astype(BF16)


def spread(col, width):
    pieces = [p.astype(F32) for p in split3(col)]
    stacked = jnp.concatenate(pieces, axis=1).astype(BF16)
    return nn(stacked, spread_matrix(col.shape[1], width, 3))


def stack2(a):
    return jnp.concatenate(split2(a), axis=0)


def twice(a):
    return jnp.concatenate([a, a], axis=1)


def nt3(a, b):
    ah, al = split2(a)
    bh, bl = split2(b)
    both = nt(ah, jnp.concatenate([bh, bl], axis=0))
    half = both.shape[1] // 2
    return both[:, :half] + both[:, half:] + nt(al, bh)


def code_rows(state, extra):
    top = jnp.max(jnp.abs(state), axis=0, keepdims=True)
    power = jnp.ceil(jnp.log2(jnp.maximum(top, 1e-30)))
    used = sum(e.shape[0] for e in extra)
    rest = jnp.zeros((15 - used, state.shape[1]), F32)
    return state * jnp.exp2(12.0 - power), jnp.concatenate([power, *extra, rest], axis=0)


def spread_row(row, width):
    return spread(jnp.broadcast_to(row, (8, row.shape[1])), width)[0:1]


def cum_col(ld):
    tri = lower(ld.shape[1])
    a, b, c = split3(ld)
    return nt(tri, a) + nt(tri, b) + nt(tri, c)


def cum_row(ld):
    tri = lower(ld.shape[1])
    a, b, c = split3(ld)
    return nt(a, tri) + nt(b, tri) + nt(c, tri)


def turn(rows):
    t = rows.shape[1]
    eye = (iota((t, t), 0) == iota((t, t), 1)).astype(BF16)
    a, b, c = split3(rows)
    return nt(eye, a) + nt(eye, b) + nt(eye, c)


def state_kernel(x_ref, w_ref, ls_ref, ld_ref, st0_ref, coded_ref, wexp_ref):
    t = x_ref.shape[0] // 2
    width = x_ref.shape[1]
    n = w_ref.shape[1]
    parts, tots = [], []
    for b in (0, 1):
        rows = slice(b * t, (b + 1) * t)
        ccol = cum_col(ld_ref[:, rows])
        tot = ccol[t - 1 : t, :]
        wexp = spread(jnp.exp(tot - ccol + turn(ls_ref[:, rows])), width)
        wexp_ref[rows, :] = wexp
        hi, lo = split2(x_ref[rows, :].astype(F32) * wexp)
        parts.append(tn(w_ref[rows, :], hi) + tn(w_ref[rows, :], lo))
        tots.append(tot)
    st0_ref[...] = parts[0]
    state = spread_row(jnp.exp(tots[1]), width) * parts[0] + parts[1]
    pieces = [p.astype(F32) for p in split3(spread_row(tots[0] + tots[1], width))]
    coded_ref[:n, :], coded_ref[n:, :] = code_rows(state, pieces)


def merge_kernel(flag, own_ref, got_ref, out_ref, *, group):
    n = own_ref.shape[0] - 16
    used = 3 * group
    own_rows = own_ref[n + 1 : n + 1 + used, :]
    got_rows = got_ref[n + 1 : n + 1 + used, :]
    own = own_ref[:n, :] * jnp.exp2(own_ref[n : n + 1, :] - 12.0)
    got = got_ref[:n, :] * jnp.exp2(got_ref[n : n + 1, :] - 12.0)
    own_fade = jnp.exp(jnp.sum(own_rows, axis=0, keepdims=True))
    got_fade = jnp.exp(jnp.sum(got_rows, axis=0, keepdims=True))
    earlier = flag[0] == 1
    merged = own * jnp.where(earlier, 1.0, got_fade) + got * jnp.where(earlier, own_fade, 1.0)
    out_ref[:n, :], out_ref[n:, :] = code_rows(merged, [own_rows, got_rows])


def local_kernel(
    x_ref, w_ref, r_ref, ls_ref, ld_ref, st0_ref,
    y_ref, fs_ref, clsx_ref, crow_ref, cexp, clsrow, a_ref,
):
    t = x_ref.shape[0] // 2
    th = t // 2
    width = x_ref.shape[1]
    heads = ls_ref.shape[0]
    hw = width // heads
    per = 128 // hw
    for b in (0, 1):
        rows = slice(b * t, (b + 1) * t)
        ccol = cum_col(ld_ref[:, rows])
        cexp[...] = spread(ccol, width)
        fs = spread(jnp.exp(ccol), width)
        fs_ref[rows, :] = fs
        clsx_ref[rows, :] = spread(ccol - turn(ls_ref[:, rows]), width)
        crow = cum_row(ld_ref[:, rows])
        crow_ref[:, rows] = crow
        clsrow[...] = crow - ls_ref[:, rows]
        keep = iota((t, t), 0) >= iota((t, t), 1)
        a_ref[...] = jnp.where(keep, nt(r_ref[rows, :], w_ref[rows, :]), 0.0)
        if b == 1:
            y_ref[rows, :] = fs * nn(twice(r_ref[rows, :]), stack2(st0_ref[...]))

        def one(i, rows=rows, b=b):
            cols = pl.ds(pl.multiple_of(i * 128, 128), 128)
            xp = x_ref[rows, cols]
            xtop = jnp.concatenate([xp[:th], xp[:th]], axis=0)
            cc = cexp[:, cols]
            lane = iota((t, 128), 1)
            out = None
            for a in range(per):
                ci = cc[:, a * hw : a * hw + 1]
                cj = clsrow[pl.ds(i * per + a, 1), :]
                top = jnp.exp(jnp.minimum(ci[:th] - cj[:, :th], 0.0)) * a_ref[:th, :th]
                bot = jnp.exp(jnp.minimum(ci[th:] - cj, 0.0)) * a_ref[th:, :]
                yt = nn(jnp.concatenate(split2(top), axis=1), xtop)
                b1, b2 = split2(bot)
                yb = nn(b1, xp) + nn(b2, xp)
                mine = jnp.concatenate([yt, yb], axis=0)
                out = mine if out is None else jnp.where(lane >= a * hw, mine, out)
            if b == 1:
                out = out + y_ref[rows, cols]
            return cols, out

        def two(i, _, rows=rows, one=one):
            done = [one(2 * i), one(2 * i + 1)]
            for cols, out in done:
                y_ref[rows, cols] = out
            return 0

        lax.fori_loop(0, width // 256, two, 0)


def keys_twice(kv_ref, g, kw):
    k = kv_ref[:, g * HD : (g + 1) * HD]
    return jnp.concatenate([k, k], axis=1), kv_ref[:, kw + g * HD : kw + (g + 1) * HD].T


def own_kernel(q_ref, kv_ref, qs_ref, acc_ref, m_ref, l_ref, k2, vt, bias, s0a, s1a, s0b, s1b):
    t = q_ref.shape[0] // 2
    kw = kv_ref.shape[1] // 2
    kvh = kw // HD
    group = q_ref.shape[1] // HD // kvh
    scale = 1.0 / math.sqrt(HD)
    bias[...] = jnp.where(iota((t, t), 0) <= iota((t, t), 1), 0.0, -1e30)
    for g in range(kvh):
        k2[...], vt[...] = keys_twice(kv_ref, g, kw)

        def scores(h, s0, s1, g=g):
            at = g * group + h
            q = q_ref[:, pl.ds(pl.multiple_of(at * HD, HD), HD)].astype(F32) * scale
            both = jnp.concatenate(split2(q), axis=1)
            qs_ref[:, pl.ds(pl.multiple_of(at * 2 * HD, 2 * HD), 2 * HD)] = both
            s0[...] = nt(k2[:t, :], both[:t]) + bias[...]
            s1[:t, :] = nt(k2[:t, :], both[t:])
            s1[t:, :] = nt(k2[t:, :], both[t:]) + bias[...]

        def soft(h, s0, s1, g=g):
            at = g * group + h
            cols = pl.ds(pl.multiple_of(at * HD, HD), HD)
            for b, s_ref in ((0, s0), (1, s1)):
                rows = slice(b * t, (b + 1) * t)
                s = s_ref[...]
                top = jnp.max(s, axis=0, keepdims=True)
                e = jnp.exp(s - top)
                m_ref[pl.ds(at, 1), rows] = top
                l_ref[pl.ds(at, 1), rows] = jnp.sum(e, axis=0, keepdims=True)
                acc_ref[cols, rows] = nn(vt[:, : (b + 1) * t], e.astype(BF16))

        scores(0, s0a, s1a)

        def pair(i, _):
            scores(2 * i + 1, s0b, s1b)
            soft(2 * i, s0a, s1a)
            scores(jnp.minimum(2 * i + 2, group - 1), s0a, s1a)
            soft(2 * i + 1, s0b, s1b)
            return 0

        lax.fori_loop(0, group // 2, pair, 0)


def far_kernel(flag, qs_ref, kv_ref, acc_in, m_in, l_in, acc_ref, m_ref, l_ref, k2, vt, sa, sb):
    t = qs_ref.shape[0] // 2
    kw = kv_ref.shape[1] // 2
    kvh = kw // HD
    group = qs_ref.shape[1] // (2 * HD) // kvh

    @pl.when(flag[0] == 0)
    def _():
        acc_ref[...] = acc_in[...]
        m_ref[...] = m_in[...]
        l_ref[...] = l_in[...]

    @pl.when(flag[0] == 1)
    def _():
        for g in range(kvh):
            k2[...], vt[...] = keys_twice(kv_ref, g, kw)

            def scores(h, s_ref, g=g):
                at = g * group + h
                s_ref[...] = nt(k2[...], qs_ref[:, pl.ds(pl.multiple_of(at * 2 * HD, 2 * HD), 2 * HD)])

            def soft(h, s_ref, g=g):
                at = g * group + h
                cols = pl.ds(pl.multiple_of(at * HD, HD), HD)
                row = pl.ds(at, 1)
                for b in (0, 1):
                    rows = slice(b * t, (b + 1) * t)
                    s = s_ref[:, rows]
                    old = m_in[row, rows]
                    new = jnp.maximum(old, jnp.max(s, axis=0, keepdims=True))
                    e = jnp.exp(s - new)
                    fade = jnp.exp(old - new)
                    m_ref[row, rows] = new
                    l_ref[row, rows] = l_in[row, rows] * fade + jnp.sum(e, axis=0, keepdims=True)
                    acc_ref[cols, rows] = acc_in[cols, rows] * fade + nn(vt[...], e.astype(BF16))

            scores(0, sa)

            def pair(i, _):
                scores(2 * i + 1, sb)
                soft(2 * i, sa)
                scores(jnp.minimum(2 * i + 2, group - 1), sa)
                soft(2 * i + 1, sb)
                return 0

            lax.fori_loop(0, group // 2, pair, 0)


def residual_kernel(y_ref, acc_ref, l_ref, r_ref, fs_ref, sin_ref, res_ref, d1_ref, coded_ref):
    t = y_ref.shape[0] // 2
    width = y_ref.shape[1]
    n = r_ref.shape[1]
    state = sin_ref[...]
    first = fs_ref[t - 1 : t, :]
    parts = []
    for b in (0, 1):
        rows = slice(b * t, (b + 1) * t)
        fs = fs_ref[rows, :]
        r = r_ref[rows, :]
        heads = [
            (acc_ref[h * HD : (h + 1) * HD, rows] / l_ref[h : h + 1, rows]).astype(BF16).T
            for h in range(width // HD)
        ]
        teach = jnp.concatenate(heads, axis=1).astype(F32)
        res = y_ref[rows, :] + fs * nn(twice(r), stack2(state * first if b else state)) - teach
        res_ref[rows, :] = res
        hi, lo = split2(res * fs)
        parts.append(tn(r, hi) + tn(r, lo))
    d1_ref[...] = parts[1]
    coded_ref[:n, :], coded_ref[n:, :] = code_rows(parts[0] + first * parts[1], [])


def back_kernel(
    res_ref, x_ref, w_ref, r_ref, clsx_ref, crow_ref, fs_ref, wexp_ref, sin_ref, st0_ref, d1_ref,
    back_ref, shared_ref, a_ref, pair,
):
    t = x_ref.shape[0] // 2
    th = t // 2
    width = x_ref.shape[1]
    heads = crow_ref.shape[0]
    hw = width // heads
    per = 128 // hw
    first = fs_ref[t - 1 : t, :]
    for b in (0, 1):
        rows = slice(b * t, (b + 1) * t)
        keep = iota((t, t), 1) >= iota((t, t), 0)
        w = w_ref[rows, :]
        r = r_ref[rows, :]
        a_ref[...] = jnp.where(keep, nt(w, r), 0.0)
        pair[...] = jnp.zeros_like(pair)
        if b == 0:
            d1 = d1_ref[...]
            wexp = wexp_ref[rows, :]
            back_ref[rows, :] = wexp * nn(twice(w), stack2(d1))
            gw = nt3(x_ref[rows, :].astype(F32) * wexp, d1)
            state = sin_ref[...]
        else:
            gw = None
            state = first * sin_ref[...] + st0_ref[...]
        gr = nt3(res_ref[rows, :] * fs_ref[rows, :], state)

        def one(i, rows=rows, b=b):
            cols = pl.ds(pl.multiple_of(i * 128, 128), 128)
            xp = x_ref[rows, cols]
            rh, rl = split2(res_ref[rows, cols])
            both = jnp.concatenate([rh, rl], axis=1)
            cc = clsx_ref[rows, cols]
            lane = iota((t, 128), 1)
            out, above, below = None, 0.0, 0.0
            for a in range(per):
                cj = cc[:, a * hw : a * hw + 1]
                ci = crow_ref[pl.ds(i * per + a, 1), rows]
                xx = twice(jnp.where((lane // hw) == a, xp, jnp.zeros_like(xp)))
                e1 = jnp.exp(jnp.minimum(ci - cj[:th], 0.0))
                e2 = jnp.exp(jnp.minimum(ci[:, th:] - cj[th:], 0.0))
                h1, l1 = split2(e1 * a_ref[:th, :])
                h2, l2 = split2(e2 * a_ref[th:, th:])
                p1 = nn(h1, both)
                p2 = nn(h2, both[th:])
                u1 = p1[:, :128] + p1[:, 128:] + nn(l1, rh)
                u2 = p2[:, :128] + p2[:, 128:] + nn(l2, rh[th:])
                u = jnp.concatenate([u1, u2], axis=0)
                out = u if out is None else jnp.where(lane >= a * hw, u, out)
                above += e1 * nt(xx[:th], both)
                below += e2 * nt(xx[th:], both[th:])
            if b == 0:
                out = out + back_ref[rows, cols]
            return cols, out, above, below

        def two(i, _, rows=rows, one=one):
            done = [one(2 * i), one(2 * i + 1)]
            for cols, out, _, _ in done:
                back_ref[rows, cols] = out
            pair[:th, :] += done[0][2] + done[1][2]
            pair[th:, th:] += done[0][3] + done[1][3]
            return 0

        lax.fori_loop(0, width // 256, two, 0)
        ph, plo = split2(jnp.where(keep, pair[...], 0.0))
        n = w.shape[1]
        mixed = nn(ph, r) + nn(plo, r)
        shared_ref[rows, :n] = mixed if gw is None else mixed + gw
        shared_ref[rows, n:] = gr + tn(ph, w) + tn(plo, w)


def ready_kernel(x_ref, ls_ref, ld_ref, extra_ref, wexp_ref, xh_ref, xl_ref):
    t = x_ref.shape[0]
    ccol = cum_col(ld_ref[...])
    wexp = spread(
        jnp.exp(ccol[t - 1 : t, :] + extra_ref[...] - ccol + turn(ls_ref[...])), x_ref.shape[1]
    )
    wexp_ref[...] = wexp
    xh_ref[...], xl_ref[...] = split2(x_ref[...].astype(F32) * wexp)


def write_kernel(xh_ref, xl_ref, g_ref, gw0_ref, top_ref, low_ref):
    gh, gl = split2(g_ref[...])
    n = gh.shape[0]
    half = top_ref.shape[0]
    both = nt(xh_ref[...], jnp.concatenate([gh, gl], axis=0))
    out = gw0_ref[...] + both[:, :n] + both[:, n:] + nt(xl_ref[...], gh)
    top_ref[...] = out[:half]
    low_ref[...] = out[half:]


def final_kernel(back_ref, wexp_ref, x_ref, w_ref, g_ref, gi_ref, gls_ref):
    width = x_ref.shape[1]
    heads = gls_ref.shape[0]
    out = back_ref[...] + wexp_ref[...] * nn(twice(w_ref[...]), stack2(g_ref[...]))
    gi_ref[...] = out
    ph, plo = split2(x_ref[...].astype(F32) * out)
    mat = spread_matrix(heads, width)
    gls_ref[...] = nt(mat, ph) + nt(mat, plo)


VM = pl.BlockSpec(memory_space=pltpu.VMEM)


def call(kernel, outs, args, scratch=(), flops=0, in_specs=None, alias=None):
    shapes = [jax.ShapeDtypeStruct(s, d) for s, d in outs]
    moved = sum(a.size * a.dtype.itemsize for a in args)
    return pl.pallas_call(
        kernel,
        out_shape=shapes,
        in_specs=in_specs or [VM] * len(args),
        out_specs=[VM] * len(shapes),
        scratch_shapes=list(scratch),
        input_output_aliases=alias or {},
        cost_estimate=pl.CostEstimate(flops=flops, bytes_accessed=moved, transcendentals=0),
        compiler_params=pltpu.CompilerParams(vmem_limit_bytes=8 * 2**20),
    )(*args)


def decode(coded, rows, weight):
    power = coded[rows : rows + 1].astype(F32)
    return coded[:rows].astype(F32) * (jnp.exp2(power - 12.0) * weight)


def on_device(q, k, v, x, wr, rd, ls, ld):
    t = q.shape[0]
    count = lax.axis_size("seq")
    tp = lax.axis_size("tp")
    chips = count // 2
    index = lax.axis_index("seq")
    core, chip = index % 2, index // 2
    heads = ls.shape[0]
    hh = heads // 2
    n = wr.shape[1]
    hc = x.shape[1] // 2
    qc = q.shape[1] // 2
    kvh = k.shape[1] // HD
    kw = k.shape[1] // 2 if kvh % 2 == 0 else k.shape[1]

    def swap(a, bits):
        return lax.ppermute(a, "seq", [(i, i ^ bits) for i in range(count)])

    def half(a, which, width, axis=1):
        return lax.dynamic_slice_in_dim(a, which * width, width, axis=axis)

    def joined(own, other, axis=0):
        a = jnp.where(core == 0, own, other)
        b = jnp.where(core == 0, other, own)
        return jnp.concatenate([a, b], axis=axis)

    def near(a):
        got = {}
        for b in range(chips.bit_length() - 1):
            got[1 << b] = swap(a, 2 << b)
        return got

    def relay(got, token):
        got = dict(got)
        for d in range(1, chips):
            if d not in got:
                low = d & -d
                held, _ = lax.optimization_barrier((got[d - low], token))
                need = [c for c in range(chips) if c ^ d < c or c ^ low ^ d < c ^ low]
                pairs = [(2 * c + k, 2 * (c ^ low) + k) for c in need for k in (0, 1)]
                got[d] = lax.ppermute(held, "seq", pairs)
        return [got[d] for d in range(1, chips)]

    def kv_half(which):
        if kvh % 2 == 0:
            return jnp.concatenate([half(k, which, kw), half(v, which, kw)], axis=1)
        return jnp.concatenate([k, v], axis=1)

    kv = joined(kv_half(core), swap(kv_half(1 - core), 1))
    keys_near = near(kv)
    x1, q1, wr1, rd1, _ = lax.optimization_barrier((x, q, wr, rd, kv))
    rates = swap(jnp.concatenate([ls, ld], axis=0), 1)
    lsc = joined(half(ls, core, hh, 0), half(rates, core, hh, 0), 1)
    ldc = joined(half(ld, core, hh, 0), half(rates[heads:], core, hh, 0), 1)
    mates = swap(jnp.concatenate([half(x1, 1 - core, hc), wr1, rd1], axis=1), 1)
    xc = joined(half(x1, core, hc), mates[:, :hc])
    wc = joined(wr1, mates[:, hc : hc + n])
    rc = joined(rd1, mates[:, hc + n :])
    qg = joined(half(q1, core, qc), swap(half(q1, 1 - core, qc), 1))

    mm = 2 * 2 * t * hc * n
    code = ((n + 16, hc), F32)
    st0, coded, wexpc = call(
        state_kernel, [((n, hc), F32), code, ((2 * t, hc), F32)], (xc, wc, lsc, ldc),
        flops=4 * mm,
    )

    def state_stage(coded, bit):
        return swap(coded.astype(F16), 2 << bit).astype(F32)

    stages = [state_stage(coded, 0)] if chips > 1 else []
    qh = qc // HD
    carry = [((qc, 2 * t), F32), ((qh, 2 * t), F32), ((qh, 2 * t), F32)]
    qs, *soft = call(
        own_kernel, [((2 * t, 2 * qc), BF16), *carry], (qg, kv),
        scratch=[pltpu.VMEM((2 * t, 2 * HD), BF16), pltpu.VMEM((HD, 2 * t), BF16), pltpu.VMEM((t, t), F32)]
        + [pltpu.VMEM((t, t), F32), pltpu.VMEM((2 * t, t), F32)] * 2,
        flops=4 * (2 * t) ** 2 * qc,
    )
    ybase, fs, clsx, crow = call(
        local_kernel,
        [((2 * t, hc), F32), ((2 * t, hc), F32), ((2 * t, hc), F32), ((hh, 2 * t), F32)],
        (xc, wc, rc, lsc, ldc, st0),
        scratch=[pltpu.VMEM((t, hc), F32), pltpu.VMEM((hh, t), F32), pltpu.VMEM((t, t), F32)],
        flops=8 * mm,
    )
    for bit in range(1, chips.bit_length() - 1):
        flag = jnp.reshape((chip >> (bit - 1)) % 2, (1,)).astype(jnp.int32)
        (coded,) = call(
            functools.partial(merge_kernel, group=1 << (bit - 1)), [code], (flag, coded, stages[-1]),
            in_specs=[pl.BlockSpec(memory_space=pltpu.SMEM), VM, VM],
        )
        stages.append(state_stage(coded, bit))
    decays = {}
    for bit, got in enumerate(stages):
        for m in range(1 << bit):
            at = n + 1 + 3 * m
            decays[(1 << bit) + m] = jnp.sum(got[at : at + 3], axis=0, keepdims=True)

    def between(low, high, most):
        out = jnp.zeros((1, hc), F32)
        for m in range(1, most):
            at = chip ^ m
            out += jnp.where((at > low) & (at < high), decays[m], 0.0)
        return out

    incoming = jnp.zeros((n, hc), F32)
    for bit, got in enumerate(stages):
        fade = jnp.exp(between(-1, chip, 1 << bit))
        incoming += decode(got, n, jnp.where((chip >> bit) % 2 == 1, fade, 0.0))
    far = relay(keys_near, soft[1])

    def combine(got):
        flat = jnp.concatenate([g.astype(F32) for g in got], axis=0)
        flat = lax.optimization_barrier(flat)
        out = 0.0
        for d in range(1, chips):
            fade = jnp.exp(between(chip, chip ^ d, chips))
            at = (d - 1) * (n + 16)
            out += decode(flat[at : at + n + 16], n, jnp.where((chip ^ d) > chip, fade, 0.0))
        return out

    for d, keys in enumerate(far, 1):
        flag = jnp.reshape((chip ^ d) < chip, (1,)).astype(jnp.int32)
        soft = call(
            far_kernel, carry, (flag, qs, keys, *soft),
            scratch=[pltpu.VMEM((2 * t, 2 * HD), BF16), pltpu.VMEM((HD, 2 * t), BF16)] + [pltpu.VMEM((2 * t, 2 * t), F32)] * 2,
            flops=4 * (2 * t) ** 2 * qc, alias={3: 0, 4: 1, 5: 2},
            in_specs=[pl.BlockSpec(memory_space=pltpu.SMEM)] + [VM] * 5,
        )
    res, d1, dcode = call(
        residual_kernel, [((2 * t, hc), F32), ((n, hc), F32), code],
        (ybase, soft[0], soft[2], rc, fs, incoming), flops=8 * mm,
    )
    sent = dcode.astype(F16)
    coming = []
    for d in range(1, chips):
        coming.append(swap(sent, 2 * d))
    back, shared = call(
        back_kernel, [((2 * t, hc), F32), ((2 * t, 2 * n), F32)],
        (res, xc, wc, rc, clsx, crow, fs, wexpc, incoming, st0, d1),
        scratch=[pltpu.VMEM((t, t), F32), pltpu.VMEM((t, t), F32)],
        flops=16 * mm,
    )
    other_total = jnp.sum(rates[heads:], axis=1)[None, :]
    extra = jnp.where(core == 0, other_total, 0.0)
    wexp, xh, xl = call(
        ready_kernel, [((t, 2 * hc), F32), ((t, 2 * hc), BF16), ((t, 2 * hc), BF16)],
        (x, ls, ld, extra), flops=2 * mm,
    )

    def home(a):
        return half(a, core, t, 0), swap(half(a, 1 - core, t, 0), 1)

    def tp_sum(parts):
        bits = tp.bit_length() - 1
        parts = list(parts)
        for step in range(bits):
            sent = [
                lax.ppermute(a, "tp", [(i, i ^ (1 << ((step + k) % bits))) for i in range(tp)])
                for k, a in enumerate(parts)
            ]
            parts = [a + b for a, b in zip(parts, sent)]
        return parts

    back_all = joined(*home(back), 1)
    own, other = home(shared)
    grads = own + other
    gw0, gr0 = grads[:, :n], grads[:, n:]
    grad_read = jnp.concatenate(tp_sum([gr0[: t // 2], gr0[t // 2 :]]), axis=0)
    arriving = combine(coming)
    arrived = joined(arriving, swap(arriving, 1), 1)
    gwp = call(write_kernel, [((t // 2, n), F32)] * 2, (xh, xl, arrived, gw0), flops=4 * mm)
    grad_write = jnp.concatenate(tp_sum(gwp), axis=0)
    gi, gls = call(
        final_kernel, [((t, 2 * hc), F32), ((heads, t), F32)], (back_all, wexp, x, wr, arrived),
        flops=8 * mm,
    )
    return (gi, grad_write, grad_read, gls)


def solution(mesh):
    in_specs = (
        P("seq", "tp"), P("seq", "tp"), P("seq", "tp"), P("seq", "tp"),
        P("seq", None), P("seq", None), P("tp", "seq"), P("tp", "seq"),
    )
    out_specs = (P("seq", "tp"), P("seq", None), P("seq", None), P("tp", "seq"))
    return jax.shard_map(
        on_device, mesh=mesh, in_specs=in_specs, out_specs=out_specs, check_vma=False
    )
```

```python
import functools
import math

import jax
import jax.numpy as jnp
from jax import lax
from jax.experimental import pallas as pl
from jax.experimental.pallas import tpu as pltpu
from jax.sharding import PartitionSpec as P


HD = 128
F32, BF16, F16 = jnp.float32, jnp.bfloat16, jnp.float16


def nn(a, b):
    return lax.dot_general(a, b, (((1,), (0,)), ((), ())), preferred_element_type=F32)


def nt(a, b):
    return lax.dot_general(a, b, (((1,), (1,)), ((), ())), preferred_element_type=F32)


def tn(a, b):
    return lax.dot_general(a, b, (((0,), (0,)), ((), ())), preferred_element_type=F32)


def split2(a):
    hi = a.astype(BF16)
    return hi, (a - hi.astype(F32)).astype(BF16)


def split3(a):
    hi = a.astype(BF16)
    rest = a - hi.astype(F32)
    mid = rest.astype(BF16)
    return hi, mid, (rest - mid.astype(F32)).astype(BF16)


def iota(shape, dim):
    return lax.broadcasted_iota(jnp.int32, shape, dim)


def lower(t):
    return (iota((t, t), 0) >= iota((t, t), 1)).astype(BF16)


def spread_matrix(heads, width, times=1):
    row = iota((times * heads, width), 0) % heads
    return (iota((times * heads, width), 1) // (width // heads) == row).astype(BF16)


def spread(col, width):
    pieces = [p.astype(F32) for p in split3(col)]
    stacked = jnp.concatenate(pieces, axis=1).astype(BF16)
    return nn(stacked, spread_matrix(col.shape[1], width, 3))


def stack2(a):
    return jnp.concatenate(split2(a), axis=0)


def twice(a):
    return jnp.concatenate([a, a], axis=1)


def nt3(a, b):
    ah, al = split2(a)
    bh, bl = split2(b)
    both = nt(ah, jnp.concatenate([bh, bl], axis=0))
    half = both.shape[1] // 2
    return both[:, :half] + both[:, half:] + nt(al, bh)


def code_rows(state, extra):
    top = jnp.max(jnp.abs(state), axis=0, keepdims=True)
    power = jnp.ceil(jnp.log2(jnp.maximum(top, 1e-30)))
    used = sum(e.shape[0] for e in extra)
    rest = jnp.zeros((15 - used, state.shape[1]), F32)
    return state * jnp.exp2(12.0 - power), jnp.concatenate([power, *extra, rest], axis=0)


def spread_row(row, width):
    return spread(jnp.broadcast_to(row, (8, row.shape[1])), width)[0:1]


def cum_col(ld):
    tri = lower(ld.shape[1])
    a, b, c = split3(ld)
    return nt(tri, a) + nt(tri, b) + nt(tri, c)


def cum_row(ld):
    tri = lower(ld.shape[1])
    a, b, c = split3(ld)
    return nt(a, tri) + nt(b, tri) + nt(c, tri)


def turn(rows):
    t = rows.shape[1]
    eye = (iota((t, t), 0) == iota((t, t), 1)).astype(BF16)
    a, b, c = split3(rows)
    return nt(eye, a) + nt(eye, b) + nt(eye, c)


def state_kernel(x_ref, w_ref, ls_ref, ld_ref, st0_ref, coded_ref, wexp_ref):
    t = x_ref.shape[0] // 2
    width = x_ref.shape[1]
    n = w_ref.shape[1]
    parts, tots = [], []
    for b in (0, 1):
        rows = slice(b * t, (b + 1) * t)
        ccol = cum_col(ld_ref[:, rows])
        tot = ccol[t - 1 : t, :]
        wexp = spread(jnp.exp(tot - ccol + turn(ls_ref[:, rows])), width)
        wexp_ref[rows, :] = wexp
        hi, lo = split2(x_ref[rows, :].astype(F32) * wexp)
        parts.append(tn(w_ref[rows, :], hi) + tn(w_ref[rows, :], lo))
        tots.append(tot)
    st0_ref[...] = parts[0]
    state = spread_row(jnp.exp(tots[1]), width) * parts[0] + parts[1]
    pieces = [p.astype(F32) for p in split3(spread_row(tots[0] + tots[1], width))]
    coded_ref[:n, :], coded_ref[n:, :] = code_rows(state, pieces)


def merge_kernel(flag, own_ref, got_ref, out_ref, *, group):
    n = own_ref.shape[0] - 16
    used = 3 * group
    own_rows = own_ref[n + 1 : n + 1 + used, :]
    got_rows = got_ref[n + 1 : n + 1 + used, :]
    own = own_ref[:n, :] * jnp.exp2(own_ref[n : n + 1, :] - 12.0)
    got = got_ref[:n, :] * jnp.exp2(got_ref[n : n + 1, :] - 12.0)
    own_fade = jnp.exp(jnp.sum(own_rows, axis=0, keepdims=True))
    got_fade = jnp.exp(jnp.sum(got_rows, axis=0, keepdims=True))
    earlier = flag[0] == 1
    merged = own * jnp.where(earlier, 1.0, got_fade) + got * jnp.where(earlier, own_fade, 1.0)
    out_ref[:n, :], out_ref[n:, :] = code_rows(merged, [own_rows, got_rows])


def local_kernel(
    x_ref, w_ref, r_ref, ls_ref, ld_ref, st0_ref,
    y_ref, fs_ref, clsx_ref, crow_ref, cexp, clsrow, a_ref,
):
    t = x_ref.shape[0] // 2
    th = t // 2
    width = x_ref.shape[1]
    heads = ls_ref.shape[0]
    hw = width // heads
    per = 128 // hw
    for b in (0, 1):
        rows = slice(b * t, (b + 1) * t)
        ccol = cum_col(ld_ref[:, rows])
        cexp[...] = spread(ccol, width)
        fs = spread(jnp.exp(ccol), width)
        fs_ref[rows, :] = fs
        clsx_ref[rows, :] = spread(ccol - turn(ls_ref[:, rows]), width)
        crow = cum_row(ld_ref[:, rows])
        crow_ref[:, rows] = crow
        clsrow[...] = crow - ls_ref[:, rows]
        keep = iota((t, t), 0) >= iota((t, t), 1)
        a_ref[...] = jnp.where(keep, nt(r_ref[rows, :], w_ref[rows, :]), 0.0)
        if b == 1:
            y_ref[rows, :] = fs * nn(twice(r_ref[rows, :]), stack2(st0_ref[...]))

        def one(i, rows=rows, b=b):
            cols = pl.ds(pl.multiple_of(i * 128, 128), 128)
            xp = x_ref[rows, cols]
            xtop = jnp.concatenate([xp[:th], xp[:th]], axis=0)
            cc = cexp[:, cols]
            lane = iota((t, 128), 1)
            out = None
            for a in range(per):
                ci = cc[:, a * hw : a * hw + 1]
                cj = clsrow[pl.ds(i * per + a, 1), :]
                top = jnp.exp(jnp.minimum(ci[:th] - cj[:, :th], 0.0)) * a_ref[:th, :th]
                bot = jnp.exp(jnp.minimum(ci[th:] - cj, 0.0)) * a_ref[th:, :]
                yt = nn(jnp.concatenate(split2(top), axis=1), xtop)
                b1, b2 = split2(bot)
                yb = nn(b1, xp) + nn(b2, xp)
                mine = jnp.concatenate([yt, yb], axis=0)
                out = mine if out is None else jnp.where(lane >= a * hw, mine, out)
            if b == 1:
                out = out + y_ref[rows, cols]
            return cols, out

        def two(i, _, rows=rows, one=one):
            done = [one(2 * i), one(2 * i + 1)]
            for cols, out in done:
                y_ref[rows, cols] = out
            return 0

        lax.fori_loop(0, width // 256, two, 0)


def keys_twice(kv_ref, g, kw):
    k = kv_ref[:, g * HD : (g + 1) * HD]
    return jnp.concatenate([k, k], axis=1), kv_ref[:, kw + g * HD : kw + (g + 1) * HD].T


def own_kernel(q_ref, kv_ref, qs_ref, acc_ref, m_ref, l_ref, k2, vt, bias, s0a, s1a, s0b, s1b):
    t = q_ref.shape[0] // 2
    kw = kv_ref.shape[1] // 2
    kvh = kw // HD
    group = q_ref.shape[1] // HD // kvh
    scale = 1.0 / math.sqrt(HD)
    bias[...] = jnp.where(iota((t, t), 0) <= iota((t, t), 1), 0.0, -1e30)
    for g in range(kvh):
        k2[...], vt[...] = keys_twice(kv_ref, g, kw)

        def scores(h, s0, s1, g=g):
            at = g * group + h
            q = q_ref[:, pl.ds(pl.multiple_of(at * HD, HD), HD)].astype(F32) * scale
            both = jnp.concatenate(split2(q), axis=1)
            qs_ref[:, pl.ds(pl.multiple_of(at * 2 * HD, 2 * HD), 2 * HD)] = both
            s0[...] = nt(k2[:t, :], both[:t]) + bias[...]
            s1[:t, :] = nt(k2[:t, :], both[t:])
            s1[t:, :] = nt(k2[t:, :], both[t:]) + bias[...]

        def soft(h, s0, s1, g=g):
            at = g * group + h
            cols = pl.ds(pl.multiple_of(at * HD, HD), HD)
            for b, s_ref in ((0, s0), (1, s1)):
                rows = slice(b * t, (b + 1) * t)
                s = s_ref[...]
                top = jnp.max(s, axis=0, keepdims=True)
                e = jnp.exp(s - top)
                m_ref[pl.ds(at, 1), rows] = top
                l_ref[pl.ds(at, 1), rows] = jnp.sum(e, axis=0, keepdims=True)
                acc_ref[cols, rows] = nn(vt[:, : (b + 1) * t], e.astype(BF16))

        scores(0, s0a, s1a)

        def pair(i, _):
            scores(2 * i + 1, s0b, s1b)
            soft(2 * i, s0a, s1a)
            scores(jnp.minimum(2 * i + 2, group - 1), s0a, s1a)
            soft(2 * i + 1, s0b, s1b)
            return 0

        lax.fori_loop(0, group // 2, pair, 0)


def far_kernel(flag, qs_ref, kv_ref, acc_in, m_in, l_in, acc_ref, m_ref, l_ref, k2, vt, sa, sb):
    t = qs_ref.shape[0] // 2
    kw = kv_ref.shape[1] // 2
    kvh = kw // HD
    group = qs_ref.shape[1] // (2 * HD) // kvh

    @pl.when(flag[0] == 0)
    def _():
        acc_ref[...] = acc_in[...]
        m_ref[...] = m_in[...]
        l_ref[...] = l_in[...]

    @pl.when(flag[0] == 1)
    def _():
        for g in range(kvh):
            k2[...], vt[...] = keys_twice(kv_ref, g, kw)

            def scores(h, s_ref, g=g):
                at = g * group + h
                s_ref[...] = nt(k2[...], qs_ref[:, pl.ds(pl.multiple_of(at * 2 * HD, 2 * HD), 2 * HD)])

            def soft(h, s_ref, g=g):
                at = g * group + h
                cols = pl.ds(pl.multiple_of(at * HD, HD), HD)
                row = pl.ds(at, 1)
                for b in (0, 1):
                    rows = slice(b * t, (b + 1) * t)
                    s = s_ref[:, rows]
                    old = m_in[row, rows]
                    new = jnp.maximum(old, jnp.max(s, axis=0, keepdims=True))
                    e = jnp.exp(s - new)
                    fade = jnp.exp(old - new)
                    m_ref[row, rows] = new
                    l_ref[row, rows] = l_in[row, rows] * fade + jnp.sum(e, axis=0, keepdims=True)
                    acc_ref[cols, rows] = acc_in[cols, rows] * fade + nn(vt[...], e.astype(BF16))

            scores(0, sa)

            def pair(i, _):
                scores(2 * i + 1, sb)
                soft(2 * i, sa)
                scores(jnp.minimum(2 * i + 2, group - 1), sa)
                soft(2 * i + 1, sb)
                return 0

            lax.fori_loop(0, group // 2, pair, 0)


def residual_kernel(y_ref, acc_ref, l_ref, r_ref, fs_ref, sin_ref, res_ref, d1_ref, coded_ref):
    t = y_ref.shape[0] // 2
    width = y_ref.shape[1]
    n = r_ref.shape[1]
    state = sin_ref[...]
    first = fs_ref[t - 1 : t, :]
    parts = []
    for b in (0, 1):
        rows = slice(b * t, (b + 1) * t)
        fs = fs_ref[rows, :]
        r = r_ref[rows, :]
        heads = [
            (acc_ref[h * HD : (h + 1) * HD, rows] / l_ref[h : h + 1, rows]).astype(BF16).T
            for h in range(width // HD)
        ]
        teach = jnp.concatenate(heads, axis=1).astype(F32)
        res = y_ref[rows, :] + fs * nn(twice(r), stack2(state * first if b else state)) - teach
        res_ref[rows, :] = res
        hi, lo = split2(res * fs)
        parts.append(tn(r, hi) + tn(r, lo))
    d1_ref[...] = parts[1]
    coded_ref[:n, :], coded_ref[n:, :] = code_rows(parts[0] + first * parts[1], [])


def back_kernel(
    res_ref, x_ref, w_ref, r_ref, clsx_ref, crow_ref, fs_ref, wexp_ref, sin_ref, st0_ref, d1_ref,
    back_ref, first_ref, second_ref, a_ref, pair,
):
    t = x_ref.shape[0] // 2
    th = t // 2
    width = x_ref.shape[1]
    heads = crow_ref.shape[0]
    hw = width // heads
    per = 128 // hw
    first = fs_ref[t - 1 : t, :]
    for b in (0, 1):
        rows = slice(b * t, (b + 1) * t)
        keep = iota((t, t), 1) >= iota((t, t), 0)
        w = w_ref[rows, :]
        r = r_ref[rows, :]
        a_ref[...] = jnp.where(keep, nt(w, r), 0.0)
        pair[...] = jnp.zeros_like(pair)
        if b == 0:
            d1 = d1_ref[...]
            wexp = wexp_ref[rows, :]
            back_ref[rows, :] = wexp * nn(twice(w), stack2(d1))
            gw = nt3(x_ref[rows, :].astype(F32) * wexp, d1)
            state = sin_ref[...]
        else:
            gw = None
            state = first * sin_ref[...] + st0_ref[...]
        gr = nt3(res_ref[rows, :] * fs_ref[rows, :], state)

        def one(i, rows=rows, b=b):
            cols = pl.ds(pl.multiple_of(i * 128, 128), 128)
            xp = x_ref[rows, cols]
            rh, rl = split2(res_ref[rows, cols])
            both = jnp.concatenate([rh, rl], axis=1)
            cc = clsx_ref[rows, cols]
            lane = iota((t, 128), 1)
            out, above, below = None, 0.0, 0.0
            for a in range(per):
                cj = cc[:, a * hw : a * hw + 1]
                ci = crow_ref[pl.ds(i * per + a, 1), rows]
                xx = twice(jnp.where((lane // hw) == a, xp, jnp.zeros_like(xp)))
                e1 = jnp.exp(jnp.minimum(ci - cj[:th], 0.0))
                e2 = jnp.exp(jnp.minimum(ci[:, th:] - cj[th:], 0.0))
                h1, l1 = split2(e1 * a_ref[:th, :])
                h2, l2 = split2(e2 * a_ref[th:, th:])
                p1 = nn(h1, both)
                p2 = nn(h2, both[th:])
                u1 = p1[:, :128] + p1[:, 128:] + nn(l1, rh)
                u2 = p2[:, :128] + p2[:, 128:] + nn(l2, rh[th:])
                u = jnp.concatenate([u1, u2], axis=0)
                out = u if out is None else jnp.where(lane >= a * hw, u, out)
                above += e1 * nt(xx[:th], both)
                below += e2 * nt(xx[th:], both[th:])
            if b == 0:
                out = out + back_ref[rows, cols]
            return cols, out, above, below

        def two(i, _, rows=rows, one=one):
            done = [one(2 * i), one(2 * i + 1)]
            for cols, out, _, _ in done:
                back_ref[rows, cols] = out
            pair[:th, :] += done[0][2] + done[1][2]
            pair[th:, th:] += done[0][3] + done[1][3]
            return 0

        lax.fori_loop(0, width // 256, two, 0)
        ph, plo = split2(jnp.where(keep, pair[...], 0.0))
        n = w.shape[1]
        mixed = nn(ph, r) + nn(plo, r)
        shared_ref = second_ref if b else first_ref
        shared_ref[:, :n] = mixed if gw is None else mixed + gw
        shared_ref[:, n:] = gr + tn(ph, w) + tn(plo, w)


def ready_kernel(x_ref, ls_ref, ld_ref, extra_ref, wexp_ref, xh_ref, xl_ref):
    t = x_ref.shape[0]
    ccol = cum_col(ld_ref[...])
    wexp = spread(
        jnp.exp(ccol[t - 1 : t, :] + extra_ref[...] - ccol + turn(ls_ref[...])), x_ref.shape[1]
    )
    wexp_ref[...] = wexp
    xh_ref[...], xl_ref[...] = split2(x_ref[...].astype(F32) * wexp)


def write_kernel(xh_ref, xl_ref, g_ref, gw0_ref, top_ref, low_ref):
    gh, gl = split2(g_ref[...])
    n = gh.shape[0]
    half = top_ref.shape[0]
    both = nt(xh_ref[...], jnp.concatenate([gh, gl], axis=0))
    out = gw0_ref[...] + both[:, :n] + both[:, n:] + nt(xl_ref[...], gh)
    top_ref[...] = out[:half]
    low_ref[...] = out[half:]


def final_kernel(back_ref, wexp_ref, x_ref, w_ref, g_ref, gi_ref, gls_ref):
    width = x_ref.shape[1]
    heads = gls_ref.shape[0]
    out = back_ref[...] + wexp_ref[...] * nn(twice(w_ref[...]), stack2(g_ref[...]))
    gi_ref[...] = out
    ph, plo = split2(x_ref[...].astype(F32) * out)
    mat = spread_matrix(heads, width)
    gls_ref[...] = nt(mat, ph) + nt(mat, plo)


VM = pl.BlockSpec(memory_space=pltpu.VMEM)


def call(kernel, outs, args, scratch=(), flops=0, in_specs=None, alias=None):
    shapes = [jax.ShapeDtypeStruct(s, d) for s, d in outs]
    moved = sum(a.size * a.dtype.itemsize for a in args)
    return pl.pallas_call(
        kernel,
        out_shape=shapes,
        in_specs=in_specs or [VM] * len(args),
        out_specs=[VM] * len(shapes),
        scratch_shapes=list(scratch),
        input_output_aliases=alias or {},
        cost_estimate=pl.CostEstimate(flops=flops, bytes_accessed=moved, transcendentals=0),
        compiler_params=pltpu.CompilerParams(vmem_limit_bytes=8 * 2**20),
    )(*args)


def decode(coded, rows, weight):
    power = coded[rows : rows + 1].astype(F32)
    return coded[:rows].astype(F32) * (jnp.exp2(power - 12.0) * weight)


def on_device(q, k, v, x, wr, rd, ls, ld):
    t = q.shape[0]
    count = lax.axis_size("seq")
    tp = lax.axis_size("tp")
    chips = count // 2
    index = lax.axis_index("seq")
    core, chip = index % 2, index // 2
    heads = ls.shape[0]
    hh = heads // 2
    n = wr.shape[1]
    hc = x.shape[1] // 2
    qc = q.shape[1] // 2
    kvh = k.shape[1] // HD
    kw = k.shape[1] // 2 if kvh % 2 == 0 else k.shape[1]

    def swap(a, bits):
        return lax.ppermute(a, "seq", [(i, i ^ bits) for i in range(count)])

    def half(a, which, width, axis=1):
        return lax.dynamic_slice_in_dim(a, which * width, width, axis=axis)

    def joined(own, other, axis=0):
        a = jnp.where(core == 0, own, other)
        b = jnp.where(core == 0, other, own)
        return jnp.concatenate([a, b], axis=axis)

    def near(a):
        got = {}
        for b in range(chips.bit_length() - 1):
            got[1 << b] = swap(a, 2 << b)
        return got

    def relay(got, token):
        got = dict(got)
        for d in range(1, chips):
            if d not in got:
                low = d & -d
                held, _ = lax.optimization_barrier((got[d - low], token))
                need = [c for c in range(chips) if c ^ d < c or c ^ low ^ d < c ^ low]
                pairs = [(2 * c + k, 2 * (c ^ low) + k) for c in need for k in (0, 1)]
                got[d] = lax.ppermute(held, "seq", pairs)
        return [got[d] for d in range(1, chips)]

    def kv_half(which):
        if kvh % 2 == 0:
            return jnp.concatenate([half(k, which, kw), half(v, which, kw)], axis=1)
        return jnp.concatenate([k, v], axis=1)

    kv = joined(kv_half(core), swap(kv_half(1 - core), 1))
    keys_near = near(kv)
    x1, q1, wr1, rd1, _ = lax.optimization_barrier((x, q, wr, rd, kv))
    rates = swap(jnp.concatenate([ls, ld], axis=0), 1)
    lsc = joined(half(ls, core, hh, 0), half(rates, core, hh, 0), 1)
    ldc = joined(half(ld, core, hh, 0), half(rates[heads:], core, hh, 0), 1)
    mates = swap(jnp.concatenate([half(x1, 1 - core, hc), wr1, rd1], axis=1), 1)
    xc = joined(half(x1, core, hc), mates[:, :hc])
    wc = joined(wr1, mates[:, hc : hc + n])
    rc = joined(rd1, mates[:, hc + n :])
    qg = joined(half(q1, core, qc), swap(half(q1, 1 - core, qc), 1))

    mm = 2 * 2 * t * hc * n
    code = ((n + 16, hc), F32)
    st0, coded, wexpc = call(
        state_kernel, [((n, hc), F32), code, ((2 * t, hc), F32)], (xc, wc, lsc, ldc),
        flops=4 * mm,
    )

    def state_stage(coded, bit):
        return swap(coded.astype(F16), 2 << bit).astype(F32)

    stages = [state_stage(coded, 0)] if chips > 1 else []
    qh = qc // HD
    carry = [((qc, 2 * t), F32), ((qh, 2 * t), F32), ((qh, 2 * t), F32)]
    qs, *soft = call(
        own_kernel, [((2 * t, 2 * qc), BF16), *carry], (qg, kv),
        scratch=[pltpu.VMEM((2 * t, 2 * HD), BF16), pltpu.VMEM((HD, 2 * t), BF16), pltpu.VMEM((t, t), F32)]
        + [pltpu.VMEM((t, t), F32), pltpu.VMEM((2 * t, t), F32)] * 2,
        flops=4 * (2 * t) ** 2 * qc,
    )
    ybase, fs, clsx, crow = call(
        local_kernel,
        [((2 * t, hc), F32), ((2 * t, hc), F32), ((2 * t, hc), F32), ((hh, 2 * t), F32)],
        (xc, wc, rc, lsc, ldc, st0),
        scratch=[pltpu.VMEM((t, hc), F32), pltpu.VMEM((hh, t), F32), pltpu.VMEM((t, t), F32)],
        flops=8 * mm,
    )
    for bit in range(1, chips.bit_length() - 1):
        flag = jnp.reshape((chip >> (bit - 1)) % 2, (1,)).astype(jnp.int32)
        (coded,) = call(
            functools.partial(merge_kernel, group=1 << (bit - 1)), [code], (flag, coded, stages[-1]),
            in_specs=[pl.BlockSpec(memory_space=pltpu.SMEM), VM, VM],
        )
        stages.append(state_stage(coded, bit))
    decays = {}
    for bit, got in enumerate(stages):
        for m in range(1 << bit):
            at = n + 1 + 3 * m
            decays[(1 << bit) + m] = jnp.sum(got[at : at + 3], axis=0, keepdims=True)

    def between(low, high, most):
        out = jnp.zeros((1, hc), F32)
        for m in range(1, most):
            at = chip ^ m
            out += jnp.where((at > low) & (at < high), decays[m], 0.0)
        return out

    incoming = jnp.zeros((n, hc), F32)
    for bit, got in enumerate(stages):
        fade = jnp.exp(between(-1, chip, 1 << bit))
        incoming += decode(got, n, jnp.where((chip >> bit) % 2 == 1, fade, 0.0))
    far = relay(keys_near, soft[1])

    def combine(got):
        flat = jnp.concatenate([g.astype(F32) for g in got], axis=0)
        flat = lax.optimization_barrier(flat)
        out = 0.0
        for d in range(1, chips):
            fade = jnp.exp(between(chip, chip ^ d, chips))
            at = (d - 1) * (n + 16)
            out += decode(flat[at : at + n + 16], n, jnp.where((chip ^ d) > chip, fade, 0.0))
        return out

    for d, keys in enumerate(far, 1):
        flag = jnp.reshape((chip ^ d) < chip, (1,)).astype(jnp.int32)
        soft = call(
            far_kernel, carry, (flag, qs, keys, *soft),
            scratch=[pltpu.VMEM((2 * t, 2 * HD), BF16), pltpu.VMEM((HD, 2 * t), BF16)] + [pltpu.VMEM((2 * t, 2 * t), F32)] * 2,
            flops=4 * (2 * t) ** 2 * qc, alias={3: 0, 4: 1, 5: 2},
            in_specs=[pl.BlockSpec(memory_space=pltpu.SMEM)] + [VM] * 5,
        )
    res, d1, dcode = call(
        residual_kernel, [((2 * t, hc), F32), ((n, hc), F32), code],
        (ybase, soft[0], soft[2], rc, fs, incoming), flops=8 * mm,
    )
    sent = dcode.astype(F16)
    coming = []
    for d in range(1, chips):
        coming.append(swap(sent, 2 * d))
    back, *shared = call(
        back_kernel, [((2 * t, hc), F32), ((t, 2 * n), F32), ((t, 2 * n), F32)],
        (res, xc, wc, rc, clsx, crow, fs, wexpc, incoming, st0, d1),
        scratch=[pltpu.VMEM((t, t), F32), pltpu.VMEM((t, t), F32)],
        flops=16 * mm,
    )
    other_total = jnp.sum(rates[heads:], axis=1)[None, :]
    extra = jnp.where(core == 0, other_total, 0.0)
    wexp, xh, xl = call(
        ready_kernel, [((t, 2 * hc), F32), ((t, 2 * hc), BF16), ((t, 2 * hc), BF16)],
        (x, ls, ld, extra), flops=2 * mm,
    )

    def home(a):
        return half(a, core, t, 0), swap(half(a, 1 - core, t, 0), 1)

    def tp_sum(parts):
        bits = tp.bit_length() - 1
        parts = list(parts)
        for step in range(bits):
            sent = [
                lax.ppermute(a, "tp", [(i, i ^ (1 << ((step + k) % bits))) for i in range(tp)])
                for k, a in enumerate(parts)
            ]
            parts = [a + b for a, b in zip(parts, sent)]
        return parts

    back_all = joined(*home(back), 1)
    grads = jnp.where(core == 0, *shared) + swap(jnp.where(core == 0, *shared[::-1]), 1)
    gw0, gr0 = grads[:, :n], grads[:, n:]
    (grad_read,) = tp_sum([gr0])
    arriving = combine(coming)
    met = swap(arriving, 1)
    arrived = joined(arriving, met, 1)
    gwp = call(write_kernel, [((t // 2, n), F32)] * 2, (xh, xl, arrived, gw0), flops=4 * mm)
    grad_write = jnp.concatenate(tp_sum(gwp), axis=0)
    gi, gls = call(
        final_kernel, [((t, 2 * hc), F32), ((heads, t), F32)], (back_all, wexp, x, wr, arrived),
        flops=8 * mm,
    )
    return (gi, grad_write, grad_read, gls)


def solution(mesh):
    in_specs = (
        P("seq", "tp"), P("seq", "tp"), P("seq", "tp"), P("seq", "tp"),
        P("seq", None), P("seq", None), P("tp", "seq"), P("tp", "seq"),
    )
    out_specs = (P("seq", "tp"), P("seq", None), P("seq", None), P("tp", "seq"))
    return jax.shard_map(
        on_device, mesh=mesh, in_specs=in_specs, out_specs=out_specs, check_vma=False
    )
```

```python
import functools
import math

import jax
import jax.numpy as jnp
from jax import lax
from jax.experimental import pallas as pl
from jax.experimental.pallas import tpu as pltpu
from jax.sharding import PartitionSpec as P


HD = 128
F32, BF16, F16 = jnp.float32, jnp.bfloat16, jnp.float16


def nn(a, b):
    return lax.dot_general(a, b, (((1,), (0,)), ((), ())), preferred_element_type=F32)


def nt(a, b):
    return lax.dot_general(a, b, (((1,), (1,)), ((), ())), preferred_element_type=F32)


def tn(a, b):
    return lax.dot_general(a, b, (((0,), (0,)), ((), ())), preferred_element_type=F32)


def split2(a):
    hi = a.astype(BF16)
    return hi, (a - hi.astype(F32)).astype(BF16)


def split3(a):
    hi = a.astype(BF16)
    rest = a - hi.astype(F32)
    mid = rest.astype(BF16)
    return hi, mid, (rest - mid.astype(F32)).astype(BF16)


def iota(shape, dim):
    return lax.broadcasted_iota(jnp.int32, shape, dim)


def lower(t):
    return (iota((t, t), 0) >= iota((t, t), 1)).astype(BF16)


def spread_matrix(heads, width, times=1):
    row = iota((times * heads, width), 0) % heads
    return (iota((times * heads, width), 1) // (width // heads) == row).astype(BF16)


def spread(col, width):
    pieces = [p.astype(F32) for p in split3(col)]
    stacked = jnp.concatenate(pieces, axis=1).astype(BF16)
    return nn(stacked, spread_matrix(col.shape[1], width, 3))


def stack2(a):
    return jnp.concatenate(split2(a), axis=0)


def twice(a):
    return jnp.concatenate([a, a], axis=1)


def nt3(a, b):
    ah, al = split2(a)
    bh, bl = split2(b)
    both = nt(ah, jnp.concatenate([bh, bl], axis=0))
    half = both.shape[1] // 2
    return both[:, :half] + both[:, half:] + nt(al, bh)


def code_rows(state, extra):
    top = jnp.max(jnp.abs(state), axis=0, keepdims=True)
    power = jnp.ceil(jnp.log2(jnp.maximum(top, 1e-30)))
    used = sum(e.shape[0] for e in extra)
    rest = jnp.zeros((15 - used, state.shape[1]), F32)
    return state * jnp.exp2(12.0 - power), jnp.concatenate([power, *extra, rest], axis=0)


def spread_row(row, width):
    return spread(jnp.broadcast_to(row, (8, row.shape[1])), width)[0:1]


def cum_col(ld):
    tri = lower(ld.shape[1])
    a, b, c = split3(ld)
    return nt(tri, a) + nt(tri, b) + nt(tri, c)


def cum_row(ld):
    tri = lower(ld.shape[1])
    a, b, c = split3(ld)
    return nt(a, tri) + nt(b, tri) + nt(c, tri)


def turn(rows):
    t = rows.shape[1]
    eye = (iota((t, t), 0) == iota((t, t), 1)).astype(BF16)
    a, b, c = split3(rows)
    return nt(eye, a) + nt(eye, b) + nt(eye, c)


def state_kernel(x_ref, w_ref, ls_ref, ld_ref, st0_ref, coded_ref, wexp_ref):
    t = x_ref.shape[0] // 2
    width = x_ref.shape[1]
    n = w_ref.shape[1]
    parts, tots = [], []
    for b in (0, 1):
        rows = slice(b * t, (b + 1) * t)
        ccol = cum_col(ld_ref[:, rows])
        tot = ccol[t - 1 : t, :]
        wexp = spread(jnp.exp(tot - ccol + turn(ls_ref[:, rows])), width)
        wexp_ref[rows, :] = wexp
        hi, lo = split2(x_ref[rows, :].astype(F32) * wexp)
        parts.append(tn(w_ref[rows, :], hi) + tn(w_ref[rows, :], lo))
        tots.append(tot)
    st0_ref[...] = parts[0]
    state = spread_row(jnp.exp(tots[1]), width) * parts[0] + parts[1]
    pieces = [p.astype(F32) for p in split3(spread_row(tots[0] + tots[1], width))]
    coded_ref[:n, :], coded_ref[n:, :] = code_rows(state, pieces)


def merge_kernel(flag, own_ref, got_ref, out_ref, *, group):
    n = own_ref.shape[0] - 16
    used = 3 * group
    own_rows = own_ref[n + 1 : n + 1 + used, :]
    got_rows = got_ref[n + 1 : n + 1 + used, :]
    own = own_ref[:n, :] * jnp.exp2(own_ref[n : n + 1, :] - 12.0)
    got = got_ref[:n, :] * jnp.exp2(got_ref[n : n + 1, :] - 12.0)
    own_fade = jnp.exp(jnp.sum(own_rows, axis=0, keepdims=True))
    got_fade = jnp.exp(jnp.sum(got_rows, axis=0, keepdims=True))
    earlier = flag[0] == 1
    merged = own * jnp.where(earlier, 1.0, got_fade) + got * jnp.where(earlier, own_fade, 1.0)
    out_ref[:n, :], out_ref[n:, :] = code_rows(merged, [own_rows, got_rows])


def local_kernel(
    x_ref, w_ref, r_ref, ls_ref, ld_ref, st0_ref,
    y_ref, fs_ref, clsx_ref, crow_ref, cexp, clsrow, a_ref,
):
    t = x_ref.shape[0] // 2
    th = t // 2
    width = x_ref.shape[1]
    heads = ls_ref.shape[0]
    hw = width // heads
    per = 128 // hw
    for b in (0, 1):
        rows = slice(b * t, (b + 1) * t)
        ccol = cum_col(ld_ref[:, rows])
        cexp[...] = spread(ccol, width)
        fs = spread(jnp.exp(ccol), width)
        fs_ref[rows, :] = fs
        clsx_ref[rows, :] = spread(ccol - turn(ls_ref[:, rows]), width)
        crow = cum_row(ld_ref[:, rows])
        crow_ref[:, rows] = crow
        clsrow[...] = crow - ls_ref[:, rows]
        keep = iota((t, t), 0) >= iota((t, t), 1)
        a_ref[...] = jnp.where(keep, nt(r_ref[rows, :], w_ref[rows, :]), 0.0)
        if b == 1:
            y_ref[rows, :] = fs * nn(twice(r_ref[rows, :]), stack2(st0_ref[...]))

        def one(i, rows=rows, b=b):
            cols = pl.ds(pl.multiple_of(i * 128, 128), 128)
            xp = x_ref[rows, cols]
            xtop = jnp.concatenate([xp[:th], xp[:th]], axis=0)
            cc = cexp[:, cols]
            lane = iota((t, 128), 1)
            out = None
            for a in range(per):
                ci = cc[:, a * hw : a * hw + 1]
                cj = clsrow[pl.ds(i * per + a, 1), :]
                top = jnp.exp(jnp.minimum(ci[:th] - cj[:, :th], 0.0)) * a_ref[:th, :th]
                bot = jnp.exp(jnp.minimum(ci[th:] - cj, 0.0)) * a_ref[th:, :]
                yt = nn(jnp.concatenate(split2(top), axis=1), xtop)
                b1, b2 = split2(bot)
                yb = nn(b1, xp) + nn(b2, xp)
                mine = jnp.concatenate([yt, yb], axis=0)
                out = mine if out is None else jnp.where(lane >= a * hw, mine, out)
            if b == 1:
                out = out + y_ref[rows, cols]
            return cols, out

        def two(i, _, rows=rows, one=one):
            done = [one(2 * i), one(2 * i + 1)]
            for cols, out in done:
                y_ref[rows, cols] = out
            return 0

        lax.fori_loop(0, width // 256, two, 0)


def keys_twice(kv_ref, g, kw):
    k = kv_ref[:, g * HD : (g + 1) * HD]
    return jnp.concatenate([k, k], axis=1), kv_ref[:, kw + g * HD : kw + (g + 1) * HD].T


def own_kernel(q_ref, kv_ref, qs_ref, acc_ref, m_ref, l_ref, k2, vt, bias, s0a, s1a, s0b, s1b):
    t = q_ref.shape[0] // 2
    kw = kv_ref.shape[1] // 2
    kvh = kw // HD
    group = q_ref.shape[1] // HD // kvh
    scale = 1.0 / math.sqrt(HD)
    bias[...] = jnp.where(iota((t, t), 0) <= iota((t, t), 1), 0.0, -1e30)
    for g in range(kvh):
        k2[...], vt[...] = keys_twice(kv_ref, g, kw)

        def scores(h, s0, s1, g=g):
            at = g * group + h
            q = q_ref[:, pl.ds(pl.multiple_of(at * HD, HD), HD)].astype(F32) * scale
            both = jnp.concatenate(split2(q), axis=1)
            qs_ref[:, pl.ds(pl.multiple_of(at * 2 * HD, 2 * HD), 2 * HD)] = both
            s0[...] = nt(k2[:t, :], both[:t]) + bias[...]
            s1[:t, :] = nt(k2[:t, :], both[t:])
            s1[t:, :] = nt(k2[t:, :], both[t:]) + bias[...]

        def soft(h, s0, s1, g=g):
            at = g * group + h
            cols = pl.ds(pl.multiple_of(at * HD, HD), HD)
            for b, s_ref in ((0, s0), (1, s1)):
                rows = slice(b * t, (b + 1) * t)
                s = s_ref[...]
                top = jnp.max(s, axis=0, keepdims=True)
                e = jnp.exp(s - top)
                m_ref[pl.ds(at, 1), rows] = top
                l_ref[pl.ds(at, 1), rows] = jnp.sum(e, axis=0, keepdims=True)
                acc_ref[cols, rows] = nn(vt[:, : (b + 1) * t], e.astype(BF16))

        scores(0, s0a, s1a)

        def pair(i, _):
            scores(2 * i + 1, s0b, s1b)
            soft(2 * i, s0a, s1a)
            scores(jnp.minimum(2 * i + 2, group - 1), s0a, s1a)
            soft(2 * i + 1, s0b, s1b)
            return 0

        lax.fori_loop(0, group // 2, pair, 0)


def far_kernel(flag, qs_ref, kv_ref, acc_in, m_in, l_in, acc_ref, m_ref, l_ref, k2, vt, sa, sb):
    t = qs_ref.shape[0] // 2
    kw = kv_ref.shape[1] // 2
    kvh = kw // HD
    group = qs_ref.shape[1] // (2 * HD) // kvh

    @pl.when(flag[0] == 0)
    def _():
        acc_ref[...] = acc_in[...]
        m_ref[...] = m_in[...]
        l_ref[...] = l_in[...]

    @pl.when(flag[0] == 1)
    def _():
        for g in range(kvh):
            k2[...], vt[...] = keys_twice(kv_ref, g, kw)

            def scores(h, s_ref, g=g):
                at = g * group + h
                s_ref[...] = nt(k2[...], qs_ref[:, pl.ds(pl.multiple_of(at * 2 * HD, 2 * HD), 2 * HD)])

            def soft(h, s_ref, g=g):
                at = g * group + h
                cols = pl.ds(pl.multiple_of(at * HD, HD), HD)
                row = pl.ds(at, 1)
                for b in (0, 1):
                    rows = slice(b * t, (b + 1) * t)
                    s = s_ref[:, rows]
                    old = m_in[row, rows]
                    new = jnp.maximum(old, jnp.max(s, axis=0, keepdims=True))
                    e = jnp.exp(s - new)
                    fade = jnp.exp(old - new)
                    m_ref[row, rows] = new
                    l_ref[row, rows] = l_in[row, rows] * fade + jnp.sum(e, axis=0, keepdims=True)
                    acc_ref[cols, rows] = acc_in[cols, rows] * fade + nn(vt[...], e.astype(BF16))

            scores(0, sa)

            def pair(i, _):
                scores(2 * i + 1, sb)
                soft(2 * i, sa)
                scores(jnp.minimum(2 * i + 2, group - 1), sa)
                soft(2 * i + 1, sb)
                return 0

            lax.fori_loop(0, group // 2, pair, 0)


def residual_kernel(y_ref, acc_ref, l_ref, r_ref, fs_ref, sin_ref, res_ref, d1_ref, coded_ref):
    t = y_ref.shape[0] // 2
    width = y_ref.shape[1]
    n = r_ref.shape[1]
    state = sin_ref[...]
    first = fs_ref[t - 1 : t, :]
    parts = []
    for b in (0, 1):
        rows = slice(b * t, (b + 1) * t)
        fs = fs_ref[rows, :]
        r = r_ref[rows, :]
        heads = [
            (acc_ref[h * HD : (h + 1) * HD, rows] / l_ref[h : h + 1, rows]).astype(BF16).T
            for h in range(width // HD)
        ]
        teach = jnp.concatenate(heads, axis=1).astype(F32)
        res = y_ref[rows, :] + fs * nn(twice(r), stack2(state * first if b else state)) - teach
        res_ref[rows, :] = res
        hi, lo = split2(res * fs)
        parts.append(tn(r, hi) + tn(r, lo))
    d1_ref[...] = parts[1]
    coded_ref[:n, :], coded_ref[n:, :] = code_rows(parts[0] + first * parts[1], [])


def back_kernel(
    res_ref, x_ref, w_ref, r_ref, clsx_ref, crow_ref, fs_ref, wexp_ref, sin_ref, st0_ref, d1_ref,
    back_ref, shared_ref, a_ref, pair,
):
    t = x_ref.shape[0] // 2
    th = t // 2
    width = x_ref.shape[1]
    heads = crow_ref.shape[0]
    hw = width // heads
    per = 128 // hw
    first = fs_ref[t - 1 : t, :]
    for b in (0, 1):
        rows = slice(b * t, (b + 1) * t)
        keep = iota((t, t), 1) >= iota((t, t), 0)
        w = w_ref[rows, :]
        r = r_ref[rows, :]
        a_ref[...] = jnp.where(keep, nt(w, r), 0.0)
        pair[...] = jnp.zeros_like(pair)
        if b == 0:
            d1 = d1_ref[...]
            wexp = wexp_ref[rows, :]
            back_ref[rows, :] = wexp * nn(twice(w), stack2(d1))
            gw = nt3(x_ref[rows, :].astype(F32) * wexp, d1)
            state = sin_ref[...]
        else:
            gw = None
            state = first * sin_ref[...] + st0_ref[...]
        gr = nt3(res_ref[rows, :] * fs_ref[rows, :], state)

        def one(i, rows=rows, b=b):
            cols = pl.ds(pl.multiple_of(i * 128, 128), 128)
            xp = x_ref[rows, cols]
            rh, rl = split2(res_ref[rows, cols])
            both = jnp.concatenate([rh, rl], axis=1)
            cc = clsx_ref[rows, cols]
            lane = iota((t, 128), 1)
            out, above, below = None, 0.0, 0.0
            for a in range(per):
                cj = cc[:, a * hw : a * hw + 1]
                ci = crow_ref[pl.ds(i * per + a, 1), rows]
                xx = twice(jnp.where((lane // hw) == a, xp, jnp.zeros_like(xp)))
                e1 = jnp.exp(jnp.minimum(ci - cj[:th], 0.0))
                e2 = jnp.exp(jnp.minimum(ci[:, th:] - cj[th:], 0.0))
                h1, l1 = split2(e1 * a_ref[:th, :])
                h2, l2 = split2(e2 * a_ref[th:, th:])
                p1 = nn(h1, both)
                p2 = nn(h2, both[th:])
                u1 = p1[:, :128] + p1[:, 128:] + nn(l1, rh)
                u2 = p2[:, :128] + p2[:, 128:] + nn(l2, rh[th:])
                u = jnp.concatenate([u1, u2], axis=0)
                out = u if out is None else jnp.where(lane >= a * hw, u, out)
                above += e1 * nt(xx[:th], both)
                below += e2 * nt(xx[th:], both[th:])
            if b == 0:
                out = out + back_ref[rows, cols]
            return cols, out, above, below

        def two(i, _, rows=rows, one=one):
            done = [one(2 * i), one(2 * i + 1)]
            for cols, out, _, _ in done:
                back_ref[rows, cols] = out
            pair[:th, :] += done[0][2] + done[1][2]
            pair[th:, th:] += done[0][3] + done[1][3]
            return 0

        lax.fori_loop(0, width // 256, two, 0)
        ph, plo = split2(jnp.where(keep, pair[...], 0.0))
        n = w.shape[1]
        mixed = nn(ph, r) + nn(plo, r)
        shared_ref[rows, :n] = mixed if gw is None else mixed + gw
        shared_ref[rows, n:] = gr + tn(ph, w) + tn(plo, w)


def ready_kernel(x_ref, ls_ref, ld_ref, extra_ref, wexp_ref, xh_ref, xl_ref):
    t = x_ref.shape[0]
    ccol = cum_col(ld_ref[...])
    wexp = spread(
        jnp.exp(ccol[t - 1 : t, :] + extra_ref[...] - ccol + turn(ls_ref[...])), x_ref.shape[1]
    )
    wexp_ref[...] = wexp
    xh_ref[...], xl_ref[...] = split2(x_ref[...].astype(F32) * wexp)


def write_kernel(xh_ref, xl_ref, g_ref, gw0_ref, top_ref, low_ref):
    gh, gl = split2(g_ref[...])
    n = gh.shape[0]
    half = top_ref.shape[0]
    both = nt(xh_ref[...], jnp.concatenate([gh, gl], axis=0))
    out = gw0_ref[...] + both[:, :n] + both[:, n:] + nt(xl_ref[...], gh)
    top_ref[...] = out[:half]
    low_ref[...] = out[half:]


def final_kernel(back_ref, wexp_ref, x_ref, w_ref, g_ref, gi_ref, gls_ref):
    width = x_ref.shape[1]
    heads = gls_ref.shape[0]
    out = back_ref[...] + wexp_ref[...] * nn(twice(w_ref[...]), stack2(g_ref[...]))
    gi_ref[...] = out
    ph, plo = split2(x_ref[...].astype(F32) * out)
    mat = spread_matrix(heads, width)
    gls_ref[...] = nt(mat, ph) + nt(mat, plo)


VM = pl.BlockSpec(memory_space=pltpu.VMEM)


def call(kernel, outs, args, scratch=(), flops=0, in_specs=None, alias=None):
    shapes = [jax.ShapeDtypeStruct(s, d) for s, d in outs]
    moved = sum(a.size * a.dtype.itemsize for a in args)
    return pl.pallas_call(
        kernel,
        out_shape=shapes,
        in_specs=in_specs or [VM] * len(args),
        out_specs=[VM] * len(shapes),
        scratch_shapes=list(scratch),
        input_output_aliases=alias or {},
        cost_estimate=pl.CostEstimate(flops=flops, bytes_accessed=moved, transcendentals=0),
        compiler_params=pltpu.CompilerParams(vmem_limit_bytes=8 * 2**20),
    )(*args)


def decode(coded, rows, weight):
    power = coded[rows : rows + 1].astype(F32)
    return coded[:rows].astype(F32) * (jnp.exp2(power - 12.0) * weight)


def on_device(q, k, v, x, wr, rd, ls, ld):
    t = q.shape[0]
    count = lax.axis_size("seq")
    tp = lax.axis_size("tp")
    chips = count // 2
    index = lax.axis_index("seq")
    core, chip = index % 2, index // 2
    heads = ls.shape[0]
    hh = heads // 2
    n = wr.shape[1]
    hc = x.shape[1] // 2
    qc = q.shape[1] // 2
    kvh = k.shape[1] // HD
    kw = k.shape[1] // 2 if kvh % 2 == 0 else k.shape[1]

    def swap(a, bits):
        return lax.ppermute(a, "seq", [(i, i ^ bits) for i in range(count)])

    def half(a, which, width, axis=1):
        return lax.dynamic_slice_in_dim(a, which * width, width, axis=axis)

    def joined(own, other, axis=0):
        a = jnp.where(core == 0, own, other)
        b = jnp.where(core == 0, other, own)
        return jnp.concatenate([a, b], axis=axis)

    def near(a):
        got = {}
        for b in range(chips.bit_length() - 1):
            got[1 << b] = swap(a, 2 << b)
        return got

    def relay(got, token):
        got = dict(got)
        for d in range(1, chips):
            if d not in got:
                low = d & -d
                held, _ = lax.optimization_barrier((got[d - low], token))
                need = [c for c in range(chips) if c ^ d < c or c ^ low ^ d < c ^ low]
                pairs = [(2 * c + k, 2 * (c ^ low) + k) for c in need for k in (0, 1)]
                got[d] = lax.ppermute(held, "seq", pairs)
        return [got[d] for d in range(1, chips)]

    def kv_half(which):
        if kvh % 2 == 0:
            return jnp.concatenate([half(k, which, kw), half(v, which, kw)], axis=1)
        return jnp.concatenate([k, v], axis=1)

    kv = joined(kv_half(core), swap(kv_half(1 - core), 1))
    keys_near = near(kv)
    x1, q1, wr1, rd1, _ = lax.optimization_barrier((x, q, wr, rd, kv))
    rates = swap(jnp.concatenate([ls, ld], axis=0), 1)
    lsc = joined(half(ls, core, hh, 0), half(rates, core, hh, 0), 1)
    ldc = joined(half(ld, core, hh, 0), half(rates[heads:], core, hh, 0), 1)
    mates = swap(jnp.concatenate([half(x1, 1 - core, hc), wr1, rd1], axis=1), 1)
    xc = joined(half(x1, core, hc), mates[:, :hc])
    wc = joined(wr1, mates[:, hc : hc + n])
    rc = joined(rd1, mates[:, hc + n :])
    qg = joined(half(q1, core, qc), swap(half(q1, 1 - core, qc), 1))

    mm = 2 * 2 * t * hc * n
    code = ((n + 16, hc), F32)
    st0, coded, wexpc = call(
        state_kernel, [((n, hc), F32), code, ((2 * t, hc), F32)], (xc, wc, lsc, ldc),
        flops=4 * mm,
    )

    def state_stage(coded, bit):
        return swap(coded.astype(F16), 2 << bit).astype(F32)

    stages = [state_stage(coded, 0)] if chips > 1 else []
    qh = qc // HD
    carry = [((qc, 2 * t), F32), ((qh, 2 * t), F32), ((qh, 2 * t), F32)]
    qs, *soft = call(
        own_kernel, [((2 * t, 2 * qc), BF16), *carry], (qg, kv),
        scratch=[pltpu.VMEM((2 * t, 2 * HD), BF16), pltpu.VMEM((HD, 2 * t), BF16), pltpu.VMEM((t, t), F32)]
        + [pltpu.VMEM((t, t), F32), pltpu.VMEM((2 * t, t), F32)] * 2,
        flops=4 * (2 * t) ** 2 * qc,
    )
    ybase, fs, clsx, crow = call(
        local_kernel,
        [((2 * t, hc), F32), ((2 * t, hc), F32), ((2 * t, hc), F32), ((hh, 2 * t), F32)],
        (xc, wc, rc, lsc, ldc, st0),
        scratch=[pltpu.VMEM((t, hc), F32), pltpu.VMEM((hh, t), F32), pltpu.VMEM((t, t), F32)],
        flops=8 * mm,
    )
    for bit in range(1, chips.bit_length() - 1):
        flag = jnp.reshape((chip >> (bit - 1)) % 2, (1,)).astype(jnp.int32)
        (coded,) = call(
            functools.partial(merge_kernel, group=1 << (bit - 1)), [code], (flag, coded, stages[-1]),
            in_specs=[pl.BlockSpec(memory_space=pltpu.SMEM), VM, VM],
        )
        stages.append(state_stage(coded, bit))
    decays = {}
    for bit, got in enumerate(stages):
        for m in range(1 << bit):
            at = n + 1 + 3 * m
            decays[(1 << bit) + m] = jnp.sum(got[at : at + 3], axis=0, keepdims=True)

    def between(low, high, most):
        out = jnp.zeros((1, hc), F32)
        for m in range(1, most):
            at = chip ^ m
            out += jnp.where((at > low) & (at < high), decays[m], 0.0)
        return out

    incoming = jnp.zeros((n, hc), F32)
    for bit, got in enumerate(stages):
        fade = jnp.exp(between(-1, chip, 1 << bit))
        incoming += decode(got, n, jnp.where((chip >> bit) % 2 == 1, fade, 0.0))
    far = relay(keys_near, soft[1])

    def combine(got):
        flat = jnp.concatenate([g.astype(F32) for g in got], axis=0)
        flat = lax.optimization_barrier(flat)
        out = 0.0
        for d in range(1, chips):
            fade = jnp.exp(between(chip, chip ^ d, chips))
            at = (d - 1) * (n + 16)
            out += decode(flat[at : at + n + 16], n, jnp.where((chip ^ d) > chip, fade, 0.0))
        return out

    for d, keys in enumerate(far, 1):
        flag = jnp.reshape((chip ^ d) < chip, (1,)).astype(jnp.int32)
        soft = call(
            far_kernel, carry, (flag, qs, keys, *soft),
            scratch=[pltpu.VMEM((2 * t, 2 * HD), BF16), pltpu.VMEM((HD, 2 * t), BF16)] + [pltpu.VMEM((2 * t, 2 * t), F32)] * 2,
            flops=4 * (2 * t) ** 2 * qc, alias={3: 0, 4: 1, 5: 2},
            in_specs=[pl.BlockSpec(memory_space=pltpu.SMEM)] + [VM] * 5,
        )
    res, d1, dcode = call(
        residual_kernel, [((2 * t, hc), F32), ((n, hc), F32), code],
        (ybase, soft[0], soft[2], rc, fs, incoming), flops=8 * mm,
    )
    sent = dcode.astype(F16)
    coming = []
    for d in range(1, chips):
        coming.append(swap(sent, 2 * d))
    back, shared = call(
        back_kernel, [((2 * t, hc), F32), ((2 * t, 2 * n), F32)],
        (res, xc, wc, rc, clsx, crow, fs, wexpc, incoming, st0, d1),
        scratch=[pltpu.VMEM((t, t), F32), pltpu.VMEM((t, t), F32)],
        flops=16 * mm,
    )
    other_total = jnp.sum(rates[heads:], axis=1)[None, :]
    extra = jnp.where(core == 0, other_total, 0.0)
    wexp, xh, xl = call(
        ready_kernel, [((t, 2 * hc), F32), ((t, 2 * hc), BF16), ((t, 2 * hc), BF16)],
        (x, ls, ld, extra), flops=2 * mm,
    )

    def home(a):
        return half(a, core, t, 0), swap(half(a, 1 - core, t, 0), 1)

    def tp_sum(parts):
        bits = tp.bit_length() - 1
        parts = list(parts)
        for step in range(bits):
            sent = [
                lax.ppermute(a, "tp", [(i, i ^ (1 << ((step + k) % bits))) for i in range(tp)])
                for k, a in enumerate(parts)
            ]
            parts = [a + b for a, b in zip(parts, sent)]
        return parts

    back_all = joined(*home(back), 1)
    own, other = home(shared)
    grads = own + other
    gw0, gr0 = grads[:, :n], grads[:, n:]
    (grad_read,) = tp_sum([gr0])
    arriving = combine(coming)
    met = swap(arriving, 1)
    arrived = joined(arriving, met, 1)
    gwp = call(write_kernel, [((t // 2, n), F32)] * 2, (xh, xl, arrived, gw0), flops=4 * mm)
    grad_write = jnp.concatenate(tp_sum(gwp), axis=0)
    gi, gls = call(
        final_kernel, [((t, 2 * hc), F32), ((heads, t), F32)], (back_all, wexp, x, wr, arrived),
        flops=8 * mm,
    )
    return (gi, grad_write, grad_read, gls)


def solution(mesh):
    in_specs = (
        P("seq", "tp"), P("seq", "tp"), P("seq", "tp"), P("seq", "tp"),
        P("seq", None), P("seq", None), P("tp", "seq"), P("tp", "seq"),
    )
    out_specs = (P("seq", "tp"), P("seq", None), P("seq", None), P("tp", "seq"))
    return jax.shard_map(
        on_device, mesh=mesh, in_specs=in_specs, out_specs=out_specs, check_vma=False
    )
```
